32 devices in a mesh: fsdp: 8 (over z, x), ctx: 2 (over core), tp: 2 (over y).
Axes of the slice: x: 2, y: 2, z: 4, core: 2. Of those that a mesh axis runs over, the one named last changes fastest.
Arguments:
- hidden: bfloat16 [8, 448, 1024], P('fsdp', 'ctx'), may hold values from -6 to 6
- encoder: bfloat16 [8, 1500, 1024], P('fsdp', 'ctx'), may hold values from -6 to 6
- cotangent: bfloat16 [8, 448, 1024], P('fsdp', 'ctx'), may hold values from -6 to 6
- adapter_index: int32 [8], P('fsdp'), may hold values from 0 to 7
- ln_gains: float32 [3, 1024], replicated, may hold values from 0.25 to 1.75
- attn_in_weight: bfloat16 [6, 1024, 1024], P(None, 'fsdp', 'tp'), may hold values from -0.1875 to 0.1875
- attn_out_weight: bfloat16 [2, 1024, 1024], P(None, 'fsdp', 'tp'), may hold values from -0.75 to 0.75
- up_weight: bfloat16 [1024, 4096], P('fsdp', 'tp'), may hold values from -0.1875 to 0.1875
- down_weight: bfloat16 [1024, 4096], P('fsdp', 'tp'), may hold values from -0.09375 to 0.09375
- attn_adapt_in: bfloat16 [8, 8, 16, 1024], replicated, may hold values from -0.1875 to 0.1875
- attn_adapt_out: bfloat16 [8, 8, 16, 1024], replicated, may hold values from -2 to 2
- up_adapt_in: bfloat16 [8, 16, 1024], replicated, may hold values from -0.1875 to 0.1875
- up_adapt_out: bfloat16 [8, 16, 4096], replicated, may hold values from -2 to 2
- down_adapt_in: bfloat16 [8, 16, 4096], replicated, may hold values from -0.09375 to 0.09375
- down_adapt_out: bfloat16 [8, 16, 1024], replicated, may hold values from -2 to 2
Outputs:
- layer_out: bfloat16 [8, 448, 1024], P('fsdp', 'ctx')
- grad_hidden: float32 [8, 448, 1024], P('fsdp', 'ctx')
- grad_encoder: float32 [8, 1500, 1024], P('fsdp', 'ctx')
- grad_attn_adapt_in: float32 [8, 8, 16, 1024], P(None, None, None, ('fsdp', 'ctx', 'tp'))
- grad_attn_adapt_out: float32 [8, 8, 16, 1024], P(None, None, None, ('fsdp', 'ctx', 'tp'))
- grad_up_adapt_in: float32 [8, 16, 1024], P(None, None, ('fsdp', 'ctx', 'tp'))
- grad_up_adapt_out: float32 [8, 16, 4096], P(None, None, ('fsdp', 'ctx', 'tp'))
- grad_down_adapt_in: float32 [8, 16, 4096], P(None, None, ('fsdp', 'ctx', 'tp'))
- grad_down_adapt_out: float32 [8, 16, 1024], P(None, None, ('fsdp', 'ctx', 'tp'))
The draws below stay inside these ranges and needn't reach their ends.
All inputs are finite; a program needn't handle non-finite values.
Results may differ from the reference program's by a relative error of at most 0.029.
Values may be sent and summed in bfloat16 or wider, within the bound.
No kernel may reach another device: no remote copies, remote signals or barrier semaphores. Data moves between devices by JAX's collectives and lax.ppermute only.
A program may use at most 128 MiB of HBM per device.

```python
import jax
import jax.numpy as jnp
from jax import lax

D = 1024
HEAD_DIM = 64
FF = 4096
LEN = 448
FRAMES = 1500
RANK = 16
ADAPTERS = 8
CLIPS = 8


def touch_ends(drawn, stream_key, least, high):
    shape = drawn.shape
    index_at = [jax.random.randint(jax.random.fold_in(stream_key, axis), (), 0, shape[axis]) for axis in range(len(shape))]
    drawn = drawn.at[tuple(index_at)].set(least)
    longest = shape.index(max(shape))
    index_at[longest] = (index_at[longest] + 1) % shape[longest]
    return drawn.at[tuple(index_at)].set(high)


def level_of(rng, extent, cuts, smallest, largest):
    loudness, own = 1.0, jax.random.fold_in(rng, 6)
    for dim, shards_of in cuts:
        steps = jnp.exp(jax.random.uniform(jax.random.fold_in(own, dim), (shards_of,), jnp.float32, smallest / len(cuts), largest / len(cuts)))
        loudness = loudness * jnp.repeat(steps, extent[dim] // shards_of).reshape([-1 if axis == dim else 1 for axis in range(len(extent))])
    return loudness


def scatter_about(own_key, shape, scale, bound, cuts=(), kind=jnp.bfloat16):
    factor_of = level_of(own_key, shape, cuts, -0.22, 0.18) if cuts else 1.0
    array = jax.random.normal(own_key, shape, jnp.float32) * scale * factor_of
    return jnp.minimum(jnp.maximum(array, -bound), bound).astype(kind)


def setup_inputs(seed: int = 0) -> dict:
    splits = jax.random.split(jax.random.key(seed), 16)
    return {
        "hidden": scatter_about(splits[0], (CLIPS, LEN, D), 1.0, 6.0, ((0, 8), (1, 2))),
        "encoder": scatter_about(splits[1], (CLIPS, FRAMES, D), 1.0, 6.0, ((0, 8), (1, 2))),
        "cotangent": scatter_about(splits[2], (CLIPS, LEN, D), 1.0, 6.0, ((0, 8), (1, 2))),
        "adapter_index": touch_ends(jax.random.randint(splits[3], (CLIPS,), 0, ADAPTERS), jax.random.fold_in(splits[3], 1), 0, ADAPTERS - 1).astype(jnp.int32),
        "ln_gains": jnp.clip(1.0 + 0.15 * jax.random.normal(splits[4], (3, D), jnp.float32), 0.25, 1.75),
        "attn_in_weight": scatter_about(splits[5], (6, D, D), D ** -0.5, 0.1875, ((1, 8), (2, 2))),
        "attn_out_weight": scatter_about(splits[6], (2, D, D), (D // 16) ** -0.5, 0.75, ((1, 8), (2, 2))),
        "up_weight": scatter_about(splits[7], (D, FF), D ** -0.5, 0.1875, ((0, 8), (1, 2))),
        "down_weight": scatter_about(splits[8], (D, FF), FF ** -0.5, 0.09375, ((0, 8), (1, 2))),
        "attn_adapt_in": scatter_about(splits[9], (8, ADAPTERS, RANK, D), D ** -0.5, 0.1875),
        "attn_adapt_out": scatter_about(splits[10], (8, ADAPTERS, RANK, D), 0.125, 2.0),
        "up_adapt_in": scatter_about(splits[11], (ADAPTERS, RANK, D), D ** -0.5, 0.1875),
        "up_adapt_out": scatter_about(splits[12], (ADAPTERS, RANK, FF), 0.125, 2.0),
        "down_adapt_in": scatter_about(splits[13], (ADAPTERS, RANK, FF), FF ** -0.5, 0.09375),
        "down_adapt_out": scatter_about(splits[14], (ADAPTERS, RANK, D), 0.125, 2.0),
    }


EPSILON = 1e-05
EXACT_PRECISION = lax.Precision.HIGHEST
MASKED_SCORE = -1000000000.0

@jax.custom_vjp
def low(v):
    return lax.optimization_barrier(v.astype(jnp.bfloat16)).astype(jnp.float32)

@jax.custom_vjp
def low_back(v):
    return v

def low_keep(v):
    return (low(v), None)

def low_pass(kept, grad):
    return (grad,)

def back_keep(v):
    return (v, None)

def back_low(kept, grad):
    return (low(grad),)
low.defvjp(low_keep, low_pass)
low_back.defvjp(back_keep, back_low)

def matmul_exact(left, right):
    return jnp.matmul(left, right, precision=EXACT_PRECISION)

def normalize(inputs, scale_gain):
    centred = inputs - lax.optimization_barrier(jnp.mean(inputs, axis=-1, keepdims=True))
    spread = lax.optimization_barrier(jnp.mean(centred * centred, axis=-1, keepdims=True))
    return centred * lax.rsqrt(spread + EPSILON) * scale_gain

def erf_gelu(inputs):
    return 0.5 * inputs * (1.0 + lax.erf(inputs * 0.7071067811865476))

def adapted(source_rows, weight, adapter_down_matrix, adapter_up_matrix):
    rank_projection = matmul_exact(source_rows, adapter_down_matrix.T)
    return matmul_exact(source_rows, weight) + matmul_exact(rank_projection, adapter_up_matrix)

def attend(queries, key_rows, value_rows, allowed):
    heads = queries.shape[-1] // HEAD_DIM
    query_heads = queries.reshape(queries.shape[0], heads, HEAD_DIM)
    key_heads = key_rows.reshape(key_rows.shape[0], heads, HEAD_DIM)
    value_heads = value_rows.reshape(value_rows.shape[0], heads, HEAD_DIM)
    scores = low_back(jnp.einsum('qhd,khd->hqk', query_heads, key_heads, precision=EXACT_PRECISION) * HEAD_DIM ** (-0.5))
    if allowed is not None:
        scores = jnp.where(allowed[None], scores, MASKED_SCORE)
    row_top = lax.optimization_barrier(jnp.max(scores, axis=-1, keepdims=True))
    row_total = lax.optimization_barrier(jnp.sum(jnp.exp(scores - row_top), axis=-1, keepdims=True))
    weights = low(jnp.exp(scores - (row_top + jnp.log(row_total))))
    mixed = jnp.einsum('hqk,khd->qhd', weights, value_heads, precision=EXACT_PRECISION)
    return low(low_back(mixed.reshape(queries.shape[0], -1)))

def clip_forward(item, norm_gains, frozen, tables):
    rows, frames, index = item
    attn_in, attn_out, up_full, down_full = frozen
    table_in, table_out, up_in, up_out, down_in, down_out = tables
    sel_in = table_in[:, index]
    sel_out = table_out[:, index]
    first_norm = low(normalize(rows, norm_gains[0]))
    queries = low(low_back(adapted(first_norm, attn_in[0], sel_in[0], sel_out[0])))
    key_rows = low(low_back(adapted(first_norm, attn_in[1], sel_in[1], sel_out[1])))
    value_rows = low(low_back(adapted(first_norm, attn_in[2], sel_in[2], sel_out[2])))
    positions = jnp.arange(rows.shape[0], dtype=jnp.int32)
    causal = positions[None, :] <= positions[:, None]
    self_mixed = attend(queries, key_rows, value_rows, causal)
    first_mid = rows + low_back(adapted(self_mixed, attn_out[0].T, sel_in[3], sel_out[3]))
    second_norm = low(normalize(first_mid, norm_gains[1]))
    cross_queries = low(low_back(adapted(second_norm, attn_in[3], sel_in[4], sel_out[4])))
    cross_keys = low(low_back(adapted(frames, attn_in[4], sel_in[5], sel_out[5])))
    cross_values = low(low_back(adapted(frames, attn_in[5], sel_in[6], sel_out[6])))
    cross_mixed = attend(cross_queries, cross_keys, cross_values, None)
    second_mid = first_mid + low_back(adapted(cross_mixed, attn_out[1].T, sel_in[7], sel_out[7]))
    third_norm = low(normalize(second_mid, norm_gains[2]))
    up_value = low_back(adapted(third_norm, up_full, up_in[index], up_out[index]))
    activated = low(erf_gelu(up_value))
    return second_mid + low_back(adapted(activated, down_full.T, down_in[index], down_out[index]))

def reference(hidden, encoder, cotangent, adapter_index, ln_gains, attn_in_weight, attn_out_weight, up_weight, down_weight, attn_adapt_in, attn_adapt_out, up_adapt_in, up_adapt_out, down_adapt_in, down_adapt_out):
    frozen = (attn_in_weight.astype(jnp.float32), attn_out_weight.astype(jnp.float32), up_weight.astype(jnp.float32), down_weight.astype(jnp.float32))
    norm_gains = ln_gains.astype(jnp.float32)

    def whole(rows, frames, table_in, table_out, up_in, up_out, down_in, down_out):
        tables = (table_in, table_out, up_in, up_out, down_in, down_out)

        def one_clip(item):
            return clip_forward(item, norm_gains, frozen, tables)
        return lax.map(jax.checkpoint(one_clip), (rows, frames, adapter_index))
    primals = (hidden.astype(jnp.float32), encoder.astype(jnp.float32), attn_adapt_in.astype(jnp.float32), attn_adapt_out.astype(jnp.float32), up_adapt_in.astype(jnp.float32), up_adapt_out.astype(jnp.float32), down_adapt_in.astype(jnp.float32), down_adapt_out.astype(jnp.float32))
    result, pullback = jax.vjp(whole, *primals)
    grads = pullback(cotangent.astype(jnp.float32))
    return (result.astype(jnp.bfloat16), grads[0], grads[1], grads[2], grads[3], grads[4], grads[5], grads[6], grads[7])
```

```python
import jax
import jax.numpy as jnp
from jax import lax
from jax.sharding import PartitionSpec as P

HEAD_DIM = 64
EPSILON = 1e-05
MASKED_SCORE = -1000000000.0
SCALE = HEAD_DIM ** (-0.5)
BF = jnp.bfloat16
F32 = jnp.float32


def mm(a, b):
    return lax.dot_general(a, b, (((1,), (0,)), ((), ())), preferred_element_type=F32)


def mm_nt(a, b):
    return lax.dot_general(a, b, (((1,), (1,)), ((), ())), preferred_element_type=F32)


def mm_tn(a, b):
    return lax.dot_general(a, b, (((0,), (0,)), ((), ())), preferred_element_type=F32)


def norm_parts(rows):
    centred = rows - jnp.mean(rows, axis=-1, keepdims=True)
    spread = jnp.mean(centred * centred, axis=-1, keepdims=True)
    inverse = lax.rsqrt(spread + EPSILON)
    return centred * inverse, inverse


def normalize(rows, gain):
    return norm_parts(rows)[0] * gain


def normalize_back(rows, gain, gradient):
    unit, inverse = norm_parts(rows)
    scaled = gradient * gain
    first = jnp.mean(scaled, axis=-1, keepdims=True)
    second = jnp.mean(scaled * unit, axis=-1, keepdims=True)
    return (scaled - first - unit * second) * inverse


def erf_gelu(rows):
    return 0.5 * rows * (1.0 + lax.erf(rows * 0.7071067811865476))


def erf_gelu_slope(rows):
    density = 0.3989422804014327 * jnp.exp(-0.5 * rows * rows)
    return 0.5 * (1.0 + lax.erf(rows * 0.7071067811865476)) + rows * density


def swap(value, axis):
    return lax.ppermute(value, axis, [(0, 1), (1, 0)])


def pair_total(partial_value, axis):
    low = partial_value.astype(BF)
    if lax.axis_size(axis) == 2:
        return low.astype(F32) + swap(low, axis).astype(F32)
    return lax.psum(low, axis).astype(F32)


def to_heads(rows):
    return rows.reshape(rows.shape[0], rows.shape[1] // HEAD_DIM, HEAD_DIM)


def scores_of(queries, key_rows, allowed):
    scores = (
        jnp.einsum("qhd,khd->hqk", to_heads(queries), to_heads(key_rows), preferred_element_type=F32)
        * SCALE
    )
    if allowed is not None:
        scores = jnp.where(allowed, scores, MASKED_SCORE)
    return scores


def attend(queries, key_rows, value_rows, allowed):
    scores = scores_of(queries, key_rows, allowed)
    row_top = jnp.max(scores, axis=-1, keepdims=True)
    row_total = jnp.sum(jnp.exp(scores - row_top), axis=-1, keepdims=True)
    logsum = row_top + jnp.log(row_total)
    weights = jnp.exp(scores - logsum).astype(BF)
    mixed = jnp.einsum("hqk,khd->qhd", weights, to_heads(value_rows), preferred_element_type=F32)
    return (mixed.reshape(queries.shape).astype(BF), logsum)


def attend_back(grad_mixed, queries, key_rows, value_rows, logsum, allowed):
    weights = jnp.exp(scores_of(queries, key_rows, allowed) - logsum)
    grad_heads = to_heads(grad_mixed)
    grad_weights = jnp.einsum(
        "qhd,khd->hqk", grad_heads, to_heads(value_rows), preferred_element_type=F32
    )
    row_inner = jnp.sum(grad_weights * weights, axis=-1, keepdims=True)
    grad_scores = (weights * (grad_weights - row_inner)).astype(BF)
    grad_query = (
        jnp.einsum("hqk,khd->qhd", grad_scores, to_heads(key_rows), preferred_element_type=F32)
        * SCALE
    )
    grad_key = (
        jnp.einsum("hqk,qhd->khd", grad_scores, to_heads(queries), preferred_element_type=F32)
        * SCALE
    )
    grad_value = jnp.einsum(
        "hqk,qhd->khd", weights.astype(BF), grad_heads, preferred_element_type=F32
    )
    return (
        grad_query.reshape(queries.shape).astype(BF),
        grad_key.reshape(key_rows.shape).astype(BF),
        grad_value.reshape(value_rows.shape).astype(BF),
    )


def scatter_pair(rows, axis):
    half = rows.shape[0] // 2
    me = lax.axis_index(axis)
    mine = lax.dynamic_slice_in_dim(rows, me * half, half, axis=0)
    other = lax.dynamic_slice_in_dim(rows, (1 - me) * half, half, axis=0)
    return (mine.astype(F32) + swap(other, axis).astype(F32)).astype(BF)


def gather_pair(rows, axis):
    me = lax.axis_index(axis)
    other = swap(rows, axis)
    return jnp.where(
        me == 0, jnp.concatenate([rows, other], 0), jnp.concatenate([other, rows], 0)
    )


def on_device(
    hidden,
    encoder,
    cotangent,
    adapter_index,
    ln_gains,
    attn_in_weight,
    attn_out_weight,
    up_weight,
    down_weight,
    attn_adapt_in,
    attn_adapt_out,
    up_adapt_in,
    up_adapt_out,
    down_adapt_in,
    down_adapt_out,
):
    fsdp_size = lax.axis_size("fsdp")
    ctx_size = lax.axis_size("ctx")
    tp_size = lax.axis_size("tp")
    tensor_index = lax.axis_index("tp")
    context_index = lax.axis_index("ctx")
    hidden, encoder, cotangent = hidden[0], encoder[0], cotangent[0]
    local_len, width = hidden.shape
    wide = up_adapt_out.shape[2]
    cols = attn_in_weight.shape[2]
    units = up_weight.shape[1]
    rank = attn_adapt_in.shape[2]
    adapters = attn_adapt_in.shape[1]
    head_start = tensor_index * cols
    unit_start = tensor_index * units
    mine = adapter_index[0]

    half_rows = attn_in_weight.shape[1] // ctx_size

    def my_half(table, axis):
        return lax.dynamic_slice_in_dim(table, context_index * half_rows, half_rows, axis=axis)

    attn_half = jnp.concatenate(
        [my_half(attn_in_weight[i], 0) for i in range(6)]
        + [my_half(attn_out_weight[i], 0) for i in range(2)],
        axis=1,
    )
    ff_half = jnp.concatenate([my_half(up_weight, 0), my_half(down_weight, 0)], axis=1)
    attn_full = lax.all_gather(attn_half, ("fsdp", "ctx"), axis=0, tiled=True)
    ff_full = lax.all_gather(ff_half, ("fsdp", "ctx"), axis=0, tiled=True)
    weights = [attn_full[:, i * cols : (i + 1) * cols] for i in range(8)]
    up_full, down_full = ff_full[:, :units], ff_full[:, units:]

    sel_in = lax.dynamic_index_in_dim(attn_adapt_in, mine, 1, keepdims=False)
    sel_out = lax.dynamic_index_in_dim(attn_adapt_out, mine, 1, keepdims=False)
    sel_up_in = lax.dynamic_index_in_dim(up_adapt_in, mine, 0, keepdims=False)
    sel_up_out = lax.dynamic_slice(up_adapt_out, (mine, 0, unit_start), (1, rank, units))[0]
    sel_down_in = lax.dynamic_slice(down_adapt_in, (mine, 0, unit_start), (1, rank, units))[0]
    sel_down_out = lax.dynamic_index_in_dim(down_adapt_out, mine, 0, keepdims=False)
    row_slots = (3, 7)
    in_f = [
        lax.dynamic_slice_in_dim(sel_in[i], head_start, cols, 1) if i in row_slots else sel_in[i]
        for i in range(8)
    ]
    out_f = [
        sel_out[i] if i in row_slots else lax.dynamic_slice_in_dim(sel_out[i], head_start, cols, 1)
        for i in range(8)
    ]

    def col_fwd(rows, weight, low_in, low_out):
        low = mm_nt(rows, low_in)
        return mm(rows, weight) + mm(low.astype(BF), low_out), low.astype(BF)

    def col_bwd(grad, rows, low, weight, low_in, low_out):
        grad_low = mm_nt(grad, low_out)
        source = mm_nt(grad, weight) + mm(grad_low.astype(BF), low_in)
        return source, (grad_low.astype(BF), rows), (low, grad)

    def row_fwd(rows, weight, low_in, low_out):
        low = mm_nt(rows, low_in)
        return mm_nt(rows, weight) + mm(low.astype(BF), low_out), low.astype(BF)

    def row_bwd(grad, rows, low, weight, low_in, low_out):
        grad_low = mm_nt(grad, low_out)
        source = mm(grad, weight) + mm(grad_low.astype(BF), low_in)
        return source, (grad_low.astype(BF), rows), (low, grad)

    start = hidden.astype(F32)
    n1 = normalize(start, ln_gains[0]).astype(BF)
    self_vals, self_low = [], []
    for i in range(3):
        value, low = col_fwd(n1, weights[i], in_f[i], out_f[i])
        self_vals.append(value.astype(BF))
        self_low.append(low)
    queries, key_rows, value_rows = self_vals
    keys_all, values_all = gather_pair(key_rows, "ctx"), gather_pair(value_rows, "ctx")
    query_pos = context_index * local_len + jnp.arange(local_len, dtype=jnp.int32)
    key_pos = jnp.arange(keys_all.shape[0], dtype=jnp.int32)
    causal = key_pos[None, :] <= query_pos[:, None]
    cross_k, low_ck = col_fwd(encoder, weights[4], in_f[5], out_f[5])
    cross_v, low_cv = col_fwd(encoder, weights[5], in_f[6], out_f[6])
    cross_keys = gather_pair(cross_k.astype(BF), "ctx")
    cross_values = gather_pair(cross_v.astype(BF), "ctx")
    self_mixed, self_logsum = attend(queries, keys_all, values_all, causal)
    branch, low_so = row_fwd(self_mixed, weights[6], in_f[3], out_f[3])
    first_mid = start + pair_total(branch, "tp")
    n2 = normalize(first_mid, ln_gains[1]).astype(BF)
    cross_q, low_cq = col_fwd(n2, weights[3], in_f[4], out_f[4])
    cross_q = cross_q.astype(BF)
    cross_mixed, cross_logsum = attend(cross_q, cross_keys, cross_values, None)
    branch, low_co = row_fwd(cross_mixed, weights[7], in_f[7], out_f[7])
    second_mid = first_mid + pair_total(branch, "tp")
    n3 = normalize(second_mid, ln_gains[2]).astype(BF)
    up_value, low_up = col_fwd(n3, up_full, sel_up_in, sel_up_out)
    activated = erf_gelu(up_value).astype(BF)
    branch, low_down = row_fwd(activated, down_full, sel_down_in, sel_down_out)
    layer_out = (second_mid + pair_total(branch, "tp")).astype(BF)

    grad_final = cotangent.astype(F32)
    grad_act, down_in_pair, down_out_pair = row_bwd(
        cotangent, activated, low_down, down_full, sel_down_in, sel_down_out
    )
    grad_up = (grad_act * erf_gelu_slope(up_value)).astype(BF)
    grad_n3, up_in_pair, up_out_pair = col_bwd(
        grad_up, n3, low_up, up_full, sel_up_in, sel_up_out
    )
    grad_second = grad_final + normalize_back(
        second_mid, ln_gains[2], pair_total(grad_n3, "tp")
    )
    grad_cm, co_in, co_out = row_bwd(
        grad_second.astype(BF), cross_mixed, low_co, weights[7], in_f[7], out_f[7]
    )
    grad_cq, grad_ck, grad_cv = attend_back(
        grad_cm.astype(BF), cross_q, cross_keys, cross_values, cross_logsum, None
    )
    grad_ck, grad_cv = scatter_pair(grad_ck, "ctx"), scatter_pair(grad_cv, "ctx")
    grad_n2, cq_in, cq_out = col_bwd(grad_cq, n2, low_cq, weights[3], in_f[4], out_f[4])
    enc_k, ck_in, ck_out = col_bwd(grad_ck, encoder, low_ck, weights[4], in_f[5], out_f[5])
    enc_v, cv_in, cv_out = col_bwd(grad_cv, encoder, low_cv, weights[5], in_f[6], out_f[6])
    grad_encoder = pair_total(enc_k + enc_v, "tp")
    grad_first = grad_second + normalize_back(first_mid, ln_gains[1], pair_total(grad_n2, "tp"))
    grad_sm, so_in, so_out = row_bwd(
        grad_first.astype(BF), self_mixed, low_so, weights[6], in_f[3], out_f[3]
    )
    grad_sq, grad_sk, grad_sv = attend_back(
        grad_sm.astype(BF), queries, keys_all, values_all, self_logsum, causal
    )
    grad_sk, grad_sv = scatter_pair(grad_sk, "ctx"), scatter_pair(grad_sv, "ctx")
    grad_n1 = None
    self_pairs = []
    for i, grad in enumerate((grad_sq, grad_sk, grad_sv)):
        part, pair_in, pair_out = col_bwd(grad, n1, self_low[i], weights[i], in_f[i], out_f[i])
        grad_n1 = part if grad_n1 is None else grad_n1 + part
        self_pairs.append((pair_in, pair_out))
    grad_hidden = grad_first + normalize_back(start, ln_gains[0], pair_total(grad_n1, "tp"))

    in_pairs = [p[0] for p in self_pairs] + [so_in, cq_in, ck_in, cv_in, co_in]
    out_pairs = [p[1] for p in self_pairs] + [so_out, cq_out, ck_out, cv_out, co_out]

    def widen(part, offset, full):
        if part.shape[0] == full:
            return part
        return lax.dynamic_update_slice_in_dim(
            jnp.zeros((full, part.shape[1]), F32), part, offset, axis=0
        )

    in_cols = [widen(mm_tn(rows, low), head_start, width) for low, rows in in_pairs]
    out_cols = [widen(mm_tn(grad, low), head_start, width) for low, grad in out_pairs]
    small = [mm_tn(up_in_pair[1], up_in_pair[0]), mm_tn(down_out_pair[1], down_out_pair[0])]
    wide_cols = [
        widen(mm_tn(up_out_pair[1], up_out_pair[0]), unit_start, wide),
        widen(mm_tn(down_in_pair[1], down_in_pair[0]), unit_start, wide),
    ]
    owners = fsdp_size * ctx_size * tp_size
    narrow_block = width // owners
    wide_block = wide // owners
    narrow = jnp.concatenate(in_cols + out_cols + small, axis=1)
    narrow_lanes = narrow.shape[1]
    narrow = narrow.reshape(fsdp_size, ctx_size, tp_size, narrow_block * narrow_lanes)
    broad = jnp.concatenate(wide_cols, axis=1)
    broad_lanes = broad.shape[1]
    broad = broad.reshape(fsdp_size, ctx_size, tp_size, wide_block * broad_lanes)
    packed = jnp.concatenate([narrow, broad], axis=3)
    if ctx_size == 2 and tp_size == 2:
        pick = lambda v, axis, i: lax.dynamic_index_in_dim(v, i, axis, keepdims=False)
        packed = pick(packed, 1, context_index) + swap(
            pick(packed, 1, 1 - context_index), "ctx"
        )
        packed = pick(packed, 1, tensor_index) + swap(
            pick(packed, 1, 1 - tensor_index).astype(BF), "tp"
        ).astype(F32)
    else:
        packed = packed.reshape(fsdp_size, ctx_size * tp_size, -1)
        packed = lax.psum_scatter(packed, ("ctx", "tp"), scatter_dimension=1, tiled=True)
        packed = packed.reshape(fsdp_size, -1)
    packed = lax.all_to_all(packed.astype(BF), "fsdp", 0, 0, tiled=True)
    clip_adapters = lax.all_gather(adapter_index, "fsdp", axis=0, tiled=True)
    chosen = (
        clip_adapters[None, :] == jnp.arange(adapters, dtype=jnp.int32)[:, None]
    ).astype(BF)
    table = mm(chosen, packed)
    narrow = table[:, : narrow_block * narrow_lanes].reshape(adapters, narrow_block, narrow_lanes)
    broad = table[:, narrow_block * narrow_lanes :].reshape(adapters, wide_block, broad_lanes)
    projections = attn_adapt_in.shape[0]

    def attn_table(part):
        part = part.reshape(adapters, narrow_block, projections, rank)
        return part.transpose(2, 0, 3, 1)

    lanes = projections * rank
    return (
        layer_out[None],
        grad_hidden[None],
        grad_encoder[None],
        attn_table(narrow[:, :, :lanes]),
        attn_table(narrow[:, :, lanes : 2 * lanes]),
        narrow[:, :, 2 * lanes : 2 * lanes + rank].transpose(0, 2, 1),
        broad[:, :, :rank].transpose(0, 2, 1),
        broad[:, :, rank:].transpose(0, 2, 1),
        narrow[:, :, 2 * lanes + rank :].transpose(0, 2, 1),
    )


def solution(mesh):
    in_specs = (
        P("fsdp", "ctx", None),
        P("fsdp", "ctx", None),
        P("fsdp", "ctx", None),
        P("fsdp"),
        P(),
        P(None, "fsdp", "tp"),
        P(None, "fsdp", "tp"),
        P("fsdp", "tp"),
        P("fsdp", "tp"),
        P(),
        P(),
        P(),
        P(),
        P(),
        P(),
    )
    out_specs = (
        P("fsdp", "ctx", None),
        P("fsdp", "ctx", None),
        P("fsdp", "ctx", None),
        P(None, None, None, ("fsdp", "ctx", "tp")),
        P(None, None, None, ("fsdp", "ctx", "tp")),
        P(None, None, ("fsdp", "ctx", "tp")),
        P(None, None, ("fsdp", "ctx", "tp")),
        P(None, None, ("fsdp", "ctx", "tp")),
        P(None, None, ("fsdp", "ctx", "tp")),
    )
    return jax.shard_map(
        on_device, mesh=mesh, in_specs=in_specs, out_specs=out_specs, check_vma=False
    )
```

```python
import jax
import jax.numpy as jnp
from jax import lax
from jax.experimental import pallas as pl
from jax.experimental.pallas import tpu as pltpu
from jax.sharding import PartitionSpec as P

HEAD_DIM = 64
PAIR = 2 * HEAD_DIM
EPSILON = 1e-05
MASKED_SCORE = -1000000000.0
SCALE = HEAD_DIM ** (-0.5)
BF = jnp.bfloat16
F32 = jnp.float32


def mm(a, b):
    return lax.dot_general(a, b, (((1,), (0,)), ((), ())), preferred_element_type=F32)


def mm_nt(a, b):
    return lax.dot_general(a, b, (((1,), (1,)), ((), ())), preferred_element_type=F32)


def mm_tn(a, b):
    return lax.dot_general(a, b, (((0,), (0,)), ((), ())), preferred_element_type=F32)


def norm_parts(rows):
    centred = rows - jnp.mean(rows, axis=-1, keepdims=True)
    spread = jnp.mean(centred * centred, axis=-1, keepdims=True)
    inverse = lax.rsqrt(spread + EPSILON)
    return centred * inverse, inverse


def normalize(rows, gain):
    return norm_parts(rows)[0] * gain


def normalize_back(rows, gain, gradient):
    unit, inverse = norm_parts(rows)
    scaled = gradient * gain
    first = jnp.mean(scaled, axis=-1, keepdims=True)
    second = jnp.mean(scaled * unit, axis=-1, keepdims=True)
    return (scaled - first - unit * second) * inverse


def swap(value, axis):
    return lax.ppermute(value, axis, [(0, 1), (1, 0)])


def with_other(partial_value, axis):
    if lax.axis_size(axis) == 2:
        return partial_value, swap(partial_value, axis)
    return lax.psum(partial_value, axis), jnp.zeros_like(partial_value)


def matrix(ref):
    block = ref[...]
    return block.reshape(block.shape[0] * block.shape[2], block.shape[3])


def half_masks(rows):
    lane = lax.broadcasted_iota(jnp.int32, (rows, PAIR), 1)
    return lane < HEAD_DIM, lane >= HEAD_DIM


def pick_half(rows, keep):
    return jnp.where(keep, rows, jnp.zeros_like(rows))


def join_halves(first, second):
    row = lax.broadcasted_iota(jnp.int32, first.shape, 0)
    return jnp.where(row < HEAD_DIM, first, second).T


def pair_forward(queries, keys, values, limit):
    mixed, logsums = [], []
    for keep in half_masks(queries.shape[0]):
        mine = pick_half(queries, keep)
        scores = [limit(i, mm_nt(k, mine) * SCALE) for i, k in enumerate(keys)]
        top = jnp.max(scores[0], axis=0, keepdims=True)
        for s in scores[1:]:
            top = jnp.maximum(top, jnp.max(s, axis=0, keepdims=True))
        powers = [jnp.exp(s - top) for s in scores]
        total = sum(jnp.sum(e, axis=0, keepdims=True) for e in powers)
        share = 1.0 / total
        out = sum(mm_tn(v, (e * share).astype(BF)) for v, e in zip(values, powers))
        mixed.append(out)
        logsums.append(top + jnp.log(total))
    return join_halves(*mixed), logsums


def pair_backward(grad, queries, keys, values, logsums, limit):
    grad_query, grad_keys, grad_values = [], [0.0] * len(keys), [0.0] * len(keys)
    for keep, logsum in zip(half_masks(queries.shape[0]), logsums):
        mine = pick_half(queries, keep)
        grad_mine = pick_half(grad, keep)
        weights = [
            jnp.exp(limit(i, mm_nt(k, mine) * SCALE) - logsum) for i, k in enumerate(keys)
        ]
        grad_weights = [mm_nt(v, grad_mine) for v in values]
        inner = sum(
            jnp.sum(g * w, axis=0, keepdims=True) for g, w in zip(grad_weights, weights)
        )
        part = 0.0
        for i, key in enumerate(keys):
            grad_scores = (weights[i] * (grad_weights[i] - inner)).astype(BF)
            part = part + mm_tn(key, grad_scores)
            grad_keys[i] = grad_keys[i] + mm(grad_scores, mine)
            grad_values[i] = grad_values[i] + mm(weights[i].astype(BF), grad_mine)
        grad_query.append(part)
    return (
        (join_halves(*grad_query) * SCALE).astype(BF),
        [(g * SCALE).astype(BF) for g in grad_keys],
        [g.astype(BF) for g in grad_values],
    )


def no_limit(index, scores):
    return scores


def causal_limit(context):
    def limit(index, scores):
        if index == 0:
            key = lax.broadcasted_iota(jnp.int32, scores.shape, 0)
            query = lax.broadcasted_iota(jnp.int32, scores.shape, 1)
            return jnp.where(key <= query, scores, MASKED_SCORE)
        return jnp.where(context == 1, scores, MASKED_SCORE)

    return limit


def at_first(step=0):
    return pl.when(pl.program_id(0) == step)


def at_last():
    return pl.when(pl.program_id(0) == pl.num_programs(0) - 1)


def qkv_kernel(hidden, gains, weight, low_in, low_out, normed, query, key_value, low):
    @at_first()
    def _():
        normed[...] = normalize(hidden[...].astype(F32), gains[0:1, :]).astype(BF)

    rows = normed[...]
    rank_rows = mm_nt(rows, low_in[0]).astype(BF)
    low[0] = rank_rows
    value = (mm(rows, matrix(weight)) + mm(rank_rows, low_out[0])).astype(BF)

    @at_first()
    def _():
        query[...] = value

    @pl.when(pl.program_id(0) > 0)
    def _():
        key_value[0] = value


def frames_kernel(frames, weight, low_in, low_out, key_value, low):
    rows = frames[...]
    rank_rows = mm_nt(rows, low_in[0]).astype(BF)
    low[0] = rank_rows
    key_value[0] = (mm(rows, matrix(weight)) + mm(rank_rows, low_out[0])).astype(BF)


def self_kernel(
    where, query, mine, other, weight, low_in, low_out, mixed, logsum, branch, low, acc, low_acc
):
    @at_first()
    def _():
        acc[...] = jnp.zeros_like(acc)
        low_acc[...] = jnp.zeros_like(low_acc)

    out, logs = pair_forward(
        query[...], (mine[0], other[0]), (mine[1], other[1]), causal_limit(where[0])
    )
    out = out.astype(BF)
    mixed[...] = out
    logsum[0, 0:1, :] = logs[0]
    logsum[0, 1:2, :] = logs[1]
    acc[...] += mm_nt(out, matrix(weight))
    low_acc[...] += mm_nt(out, low_in[0])

    @at_last()
    def _():
        rank_rows = low_acc[...].astype(BF)
        low[...] = rank_rows
        branch[...] = (acc[...] + mm(rank_rows, low_out[0])).astype(BF)


def cross_kernel(
    hidden, branch_mine, branch_other, gains, query_weight, query_in, query_out, mine, other,
    weight, low_in, low_out,
    middle, normed, query, query_low, mixed, logsum, branch, low, acc, low_acc,
):
    @at_first()
    def _():
        acc[...] = jnp.zeros_like(acc)
        low_acc[...] = jnp.zeros_like(low_acc)
        total = hidden[...].astype(F32) + (
            branch_mine[...].astype(F32) + branch_other[...].astype(F32)
        )
        middle[...] = total
        rows = normalize(total, gains[1:2, :]).astype(BF)
        normed[...] = rows
        query_low[...] = mm_nt(rows, query_in[0]).astype(BF)

    queries = (
        mm(normed[...], matrix(query_weight)) + mm(query_low[...], query_out[0])
    ).astype(BF)
    query[...] = queries
    out, logs = pair_forward(queries, (mine[0], other[0]), (mine[1], other[1]), no_limit)
    out = out.astype(BF)
    mixed[...] = out
    logsum[0, 0:1, :] = logs[0]
    logsum[0, 1:2, :] = logs[1]
    acc[...] += mm_nt(out, matrix(weight))
    low_acc[...] += mm_nt(out, low_in[0])

    @at_last()
    def _():
        rank_rows = low_acc[...].astype(BF)
        low[...] = rank_rows
        branch[...] = (acc[...] + mm(rank_rows, low_out[0])).astype(BF)


def units_kernel(
    middle, branch_mine, branch_other, gains, cotangent, up, down, up_in, up_out, down_in,
    down_out,
    second, branch, grad_normed, table_up_in, table_up_out, table_down_in, table_down_out,
    normed, up_low, down_back, acc, back, low_acc, back_low,
):
    @at_first()
    def _():
        total = middle[...] + (branch_mine[...].astype(F32) + branch_other[...].astype(F32))
        second[...] = total
        rows = normalize(total, gains[2:3, :]).astype(BF)
        normed[...] = rows
        up_low[...] = mm_nt(rows, up_in[...]).astype(BF)
        down_back[...] = mm_nt(cotangent[...], down_out[...]).astype(BF)
        acc[...] = jnp.zeros_like(acc)
        back[...] = jnp.zeros_like(back)
        low_acc[...] = jnp.zeros_like(low_acc)
        back_low[...] = jnp.zeros_like(back_low)

    up_rows, down_rows = matrix(up), matrix(down)
    value = mm(normed[...], up_rows) + mm(up_low[...], up_out[...])
    spread = 1.0 + lax.erf(value * 0.7071067811865476)
    act = (0.5 * value * spread).astype(BF)
    slope = 0.5 * spread + value * (0.3989422804014327 * jnp.exp(-0.5 * value * value))
    acc[...] += mm_nt(act, down_rows)
    low_acc[...] += mm_nt(act, down_in[...])
    grad_act = mm(cotangent[...], down_rows) + mm(down_back[...], down_in[...])
    grad = (grad_act * slope).astype(BF)
    back[...] += mm_nt(grad, up_rows)
    back_low[...] += mm_nt(grad, up_out[...])
    table_up_out[...] = mm_tn(up_low[...], grad)
    table_down_in[...] = mm_tn(down_back[...], act)

    @at_last()
    def _():
        down_low = low_acc[...].astype(BF)
        branch[...] = (acc[...] + mm(down_low, down_out[...])).astype(BF)
        up_back = back_low[...].astype(BF)
        grad_normed[...] = (back[...] + mm(up_back, up_in[...])).astype(BF)
        table_up_in[...] = mm_tn(up_back, normed[...])
        table_down_out[...] = mm_tn(down_low, cotangent[...])


def attention_back(
    limit, slot, carried, rows, gains, grad_mine, grad_other, weight, low_in, low_out,
    query_weight, query_in, query_out, query, mixed, mine, other, logsum, normed, query_low, low,
    carry, grad_normed, grad_kv, grad_kv_other,
    table_in, table_out, table_query_in, table_query_out,
    narrow, back_low, acc, query_back,
):
    @at_first()
    def _():
        total = carried[...].astype(F32) + normalize_back(
            rows[...],
            gains[slot : slot + 1, :],
            grad_mine[...].astype(F32) + grad_other[...].astype(F32),
        )
        carry[...] = total
        narrow[...] = total.astype(BF)
        back_low[...] = mm_nt(narrow[...], low_out[0]).astype(BF)
        acc[...] = jnp.zeros_like(acc)
        query_back[...] = jnp.zeros_like(query_back)
        table_out[...] = mm_tn(low[...], narrow[...])

    grad = (mm(narrow[...], matrix(weight)) + mm(back_low[...], low_in[0])).astype(BF)
    table_in[...] = mm_tn(back_low[...], mixed[...])
    grad_query, grad_keys, grad_values = pair_backward(
        grad,
        query[...],
        (mine[0], other[0]),
        (mine[1], other[1]),
        (logsum[0, 0:1, :], logsum[0, 1:2, :]),
        limit,
    )
    grad_kv[0], grad_kv_other[0] = grad_keys
    grad_kv[1], grad_kv_other[1] = grad_values
    acc[...] += mm_nt(grad_query, matrix(query_weight))
    query_back[...] += mm_nt(grad_query, query_out[0])
    table_query_out[...] = mm_tn(query_low[...], grad_query)

    @at_last()
    def _():
        rank_rows = query_back[...].astype(BF)
        total = acc[...] + mm(rank_rows, query_in[0])
        grad_normed[...] = total.astype(grad_normed.dtype)
        table_query_in[...] = mm_tn(rank_rows, normed[...])


def cross_back_kernel(*refs):
    attention_back(no_limit, 2, *refs)


def self_back_kernel(where, *refs):
    attention_back(causal_limit(where[0]), 1, *refs)


def pair_project_kernel(
    grad_mine, grad_other, weight, low_in, low_out, rows, low, start, total, table_in, table_out,
    acc,
):
    @at_first()
    def _():
        acc[...] = start[...]

    pair_project_step(
        grad_mine, grad_other, weight, low_in, low_out, rows, low, total, table_in, table_out, acc
    )


def frames_back_kernel(
    grad_mine, grad_other, weight, low_in, low_out, rows, low, total, table_in, table_out, acc
):
    @at_first()
    def _():
        acc[...] = jnp.zeros_like(acc)

    pair_project_step(
        grad_mine, grad_other, weight, low_in, low_out, rows, low, total, table_in, table_out, acc
    )


def pair_project_step(
    grad_mine, grad_other, weight, low_in, low_out, rows, low, total, table_in, table_out, acc
):
    grad = (grad_mine[0].astype(F32) + grad_other[0].astype(F32)).astype(BF)
    rank_rows = mm_nt(grad, low_out[0]).astype(BF)
    acc[...] += mm_nt(grad, matrix(weight)) + mm(rank_rows, low_in[0])
    table_in[0] = mm_tn(rank_rows, rows[...])
    table_out[0] = mm_tn(low[0], grad)

    @at_last()
    def _():
        total[...] = acc[...].astype(BF)


LANE = 128
PIECE = 32


def pack_kernel(fulls, shares, wides, order, tagged, *refs):
    where = refs[0]
    tables = refs[1 : 1 + fulls + shares]
    broad = refs[1 + fulls + shares : 1 + fulls + shares + wides]
    keep, send = refs[1 + fulls + shares + wides :]
    context, tensor = where[0], where[1]
    blocks = keep.shape[0]
    per_group = (len(order) + 3) // 4
    rows = per_group * 16
    lane = lax.broadcasted_iota(jnp.int32, (rows, LANE), 1) // PIECE
    for f in range(blocks):
        shard = f * 2 // blocks
        local = f % (blocks // 2)

        def table_of(k):
            if k is None:
                return jnp.zeros((16, LANE), F32)
            if k < fulls:
                return tables[k][:, f * LANE : (f + 1) * LANE]
            part = tables[k][:, local * LANE : (local + 1) * LANE]
            return jnp.where(tensor == shard, part, 0.0)

        padded = list(order) + [None] * (4 * per_group - len(order))
        groups = [
            jnp.concatenate(
                [table_of(k) for k in padded[g * per_group : (g + 1) * per_group]], axis=0
            )
            for g in range(4)
        ]
        for p in range(4):
            value = jnp.zeros((rows, LANE), F32)
            for g in range(4):
                turned = pltpu.roll(groups[g], (PIECE * (g - p)) % LANE, 1)
                value = jnp.where(lane == g, turned, value)
            pieces = [value]
            for w in broad:
                at = local * 4 * LANE + p * LANE
                pieces.append(jnp.where(tensor == shard, w[:, at : at + LANE], 0.0))
            if tagged:
                tag = where[2].astype(F32) * 0.25
                pieces.append(jnp.full((16, LANE), 1.0, F32) * tag)
            whole = jnp.concatenate(pieces, axis=0)

            @pl.when(context == p // 2)
            def _(whole=whole, f=f, p=p):
                keep[f, p % 2] = whole

            @pl.when(context != p // 2)
            def _(whole=whole, f=f, p=p):
                send[f, p % 2] = whole


def unpack_kernel(early, late, attn_in, attn_out, up_in, up_out, down_in, down_out):
    clips = early.shape[0]
    adapters = attn_in.shape[1]
    tag_row = early.shape[1] - 16
    tags = [early[c, tag_row : tag_row + 1, :].astype(F32) for c in range(clips)]
    early_rows = [early[c].astype(F32) for c in range(clips)]
    late_rows = [late[c].astype(F32) for c in range(clips)]
    for a in range(adapters):
        first = jnp.zeros(early_rows[0].shape, F32)
        second = jnp.zeros(late_rows[0].shape, F32)
        for c in range(clips):
            same = (tags[c] > a - 0.5) & (tags[c] < a + 0.5)
            weight = jnp.where(same, 1.0, 0.0)
            first = first + early_rows[c] * weight
            second = second + late_rows[c] * weight

        def piece(block, k, per_group):
            g, at = k // per_group, 16 * (k % per_group)
            return block[at : at + 16, PIECE * g : PIECE * (g + 1)]

        for j in range(4):
            attn_in[j, a] = piece(second, j, 2)
            attn_out[j, a] = piece(second, 4 + j, 2)
            attn_in[4 + j, a] = piece(first, j, 3)
            attn_out[4 + j, a] = piece(first, 4 + j, 3)
        up_in[a] = piece(first, 8, 3)
        down_out[a] = piece(first, 9, 3)
        up_out[a] = first[48:64]
        down_in[a] = first[64:80]


def shape(dims, dtype):
    return jax.ShapeDtypeStruct(tuple(dims), dtype)


def fixed(array):
    zeros = (0,) * array.ndim
    return pl.BlockSpec(array.shape, lambda *_: zeros)


def fixed_out(*dims):
    zeros = (0,) * len(dims)
    return pl.BlockSpec(dims, lambda *_: zeros)


def call(kernel, steps, ins, outs, scratch=(), scalars=None, name=None):
    arrays = [a for a, _ in ins]
    spec = pltpu.PrefetchScalarGridSpec(
        num_scalar_prefetch=0 if scalars is None else 1,
        grid=(steps,),
        in_specs=[s for _, s in ins],
        out_specs=[s for _, s in outs],
        scratch_shapes=list(scratch),
    )
    run = pl.pallas_call(
        kernel,
        grid_spec=spec,
        out_shape=[o for o, _ in outs],
        compiler_params=pltpu.CompilerParams(dimension_semantics=("arbitrary",)),
        name=name,
    )
    return run(*arrays) if scalars is None else run(scalars, *arrays)


def on_device(
    hidden,
    encoder,
    cotangent,
    adapter_index,
    ln_gains,
    attn_in_weight,
    attn_out_weight,
    up_weight,
    down_weight,
    attn_adapt_in,
    attn_adapt_out,
    up_adapt_in,
    up_adapt_out,
    down_adapt_in,
    down_adapt_out,
):
    fsdp_size = lax.axis_size("fsdp")
    ctx_size = lax.axis_size("ctx")
    tp_size = lax.axis_size("tp")
    tensor_index = lax.axis_index("tp")
    context_index = lax.axis_index("ctx")
    hidden, encoder, cotangent = hidden[0], encoder[0], cotangent[0]
    rows, width = hidden.shape
    frames = encoder.shape[0]
    wide = up_adapt_out.shape[2]
    cols = attn_in_weight.shape[2]
    units = up_weight.shape[1]
    rank = attn_adapt_in.shape[2]
    adapters = attn_adapt_in.shape[1]
    pairs = cols // PAIR
    head_start = tensor_index * cols
    unit_start = tensor_index * units
    mine = adapter_index[0]
    scalars = jnp.stack(
        [context_index.astype(jnp.int32), tensor_index.astype(jnp.int32), mine]
    )

    half_rows = attn_in_weight.shape[1] // ctx_size
    shards = fsdp_size * ctx_size

    def my_half(table):
        return lax.dynamic_slice_in_dim(
            table, context_index * half_rows, half_rows, axis=table.ndim - 2
        )

    attn_half = jnp.concatenate([my_half(attn_in_weight), my_half(attn_out_weight)], axis=0)
    ff_half = jnp.stack([my_half(up_weight), my_half(down_weight)])
    attn_full = lax.all_gather(attn_half, ("fsdp", "ctx"), axis=0)
    ff_full = lax.all_gather(ff_half, ("fsdp", "ctx"), axis=0)

    sel_in = lax.dynamic_index_in_dim(attn_adapt_in, mine, 1, keepdims=False)
    sel_out = lax.dynamic_index_in_dim(attn_adapt_out, mine, 1, keepdims=False)
    part_in = lax.dynamic_slice_in_dim(sel_in, head_start, cols, 2)
    part_out = lax.dynamic_slice_in_dim(sel_out, head_start, cols, 2)
    up_in = lax.dynamic_index_in_dim(up_adapt_in, mine, 0, keepdims=False)
    up_out = lax.dynamic_slice(up_adapt_out, (mine, 0, unit_start), (1, rank, units))[0]
    down_in = lax.dynamic_slice(down_adapt_in, (mine, 0, unit_start), (1, rank, units))[0]
    down_out = lax.dynamic_index_in_dim(down_adapt_out, mine, 0, keepdims=False)

    def weight_cols(slot):
        return attn_full, pl.BlockSpec((shards, 1, half_rows, cols), lambda i, *_: (0, slot(i), 0, 0))

    def weight_pair(slot):
        return attn_full, pl.BlockSpec((shards, 1, half_rows, PAIR), lambda p, *_: (0, slot, 0, p))

    def slot_of(table, slot):
        return table, pl.BlockSpec((1,) + table.shape[1:], lambda i, *_: (slot(i), 0, 0))

    def slot_pair(table, slot):
        return table, pl.BlockSpec((1, rank, PAIR), lambda p, *_: (slot, 0, p))

    def whole(array):
        return array, fixed(array)

    def out(dims, dtype):
        return shape(dims, dtype), fixed_out(*dims)

    def by_pair(count, dtype=BF):
        return shape((count, cols), dtype), pl.BlockSpec((count, PAIR), lambda p, *_: (0, p))

    def kv_pair(array):
        return array, pl.BlockSpec((2, array.shape[1], PAIR), lambda p, *_: (0, 0, p))

    def at(array, first=0):
        return array, pl.BlockSpec((1,) + array.shape[1:], lambda i, *_: (first + i, 0, 0))

    logsum_out = (
        shape((pairs, 2, rows), F32),
        pl.BlockSpec((1, 2, rows), lambda p, *_: (p, 0, 0)),
    )

    def logsum_in(array):
        return array, pl.BlockSpec((1, 2, rows), lambda p, *_: (p, 0, 0))

    def pair_in(array):
        return array, pl.BlockSpec((array.shape[0], PAIR), lambda p, *_: (0, p))

    wide_acc = pltpu.VMEM((rows, width), F32)
    rank_acc = pltpu.VMEM((rows, rank), F32)
    rank_keep = pltpu.VMEM((rows, rank), BF)

    n1, query, self_kv, self_low = call(
        qkv_kernel,
        3,
        [
            whole(hidden),
            whole(ln_gains),
            weight_cols(lambda i: i),
            slot_of(sel_in, lambda i: i),
            slot_of(part_out, lambda i: i),
        ],
        [
            out((rows, width), BF),
            out((rows, cols), BF),
            (
                shape((2, rows, cols), BF),
                pl.BlockSpec((1, rows, cols), lambda i: (jnp.maximum(i - 1, 0), 0, 0)),
            ),
            (shape((3, rows, rank), BF), pl.BlockSpec((1, rows, rank), lambda i: (i, 0, 0))),
        ],
        name="qkv",
    )
    self_kv_other = swap(self_kv, "ctx")
    cross_kv, frames_low = call(
        frames_kernel,
        2,
        [
            whole(encoder),
            weight_cols(lambda i: 4 + i),
            slot_of(sel_in, lambda i: 5 + i),
            slot_of(part_out, lambda i: 5 + i),
        ],
        [
            (
                shape((2, frames, cols), BF),
                pl.BlockSpec((1, frames, cols), lambda i: (i, 0, 0)),
            ),
            (
                shape((2, frames, rank), BF),
                pl.BlockSpec((1, frames, rank), lambda i: (i, 0, 0)),
            ),
        ],
        name="frames",
    )
    cross_kv_other = swap(cross_kv, "ctx")
    self_mixed, self_logsum, branch, self_o_low = call(
        self_kernel,
        pairs,
        [
            pair_in(query),
            kv_pair(self_kv),
            kv_pair(self_kv_other),
            weight_pair(6),
            slot_pair(part_in, 3),
            slot_of(sel_out, lambda i: 3),
        ],
        [by_pair(rows), logsum_out, out((rows, width), BF), out((rows, rank), BF)],
        [wide_acc, rank_acc],
        scalars,
        name="self_attention",
    )
    branch, branch_other = with_other(branch, "tp")
    first_mid, n2, cross_q, cross_q_low, cross_mixed, cross_logsum, branch, cross_o_low = call(
        cross_kernel,
        pairs,
        [
            whole(hidden),
            whole(branch),
            whole(branch_other),
            whole(ln_gains),
            weight_pair(3),
            slot_of(sel_in, lambda i: 4),
            slot_pair(part_out, 4),
            kv_pair(cross_kv),
            kv_pair(cross_kv_other),
            weight_pair(7),
            slot_pair(part_in, 7),
            slot_of(sel_out, lambda i: 7),
        ],
        [
            out((rows, width), F32),
            out((rows, width), BF),
            by_pair(rows),
            out((rows, rank), BF),
            by_pair(rows),
            logsum_out,
            out((rows, width), BF),
            out((rows, rank), BF),
        ],
        [wide_acc, rank_acc],
        name="cross_attention",
    )
    branch, branch_other = with_other(branch, "tp")
    chunk = min(units, 512)

    def unit_weight(slot):
        return ff_full, pl.BlockSpec((shards, 1, half_rows, chunk), lambda i: (0, slot, 0, i))

    def unit_cols(array):
        return array, pl.BlockSpec((rank, chunk), lambda i: (0, i))

    second_mid, branch, grad_n3, up_in_t, up_out_t, down_in_t, down_out_t = call(
        units_kernel,
        units // chunk,
        [
            whole(first_mid),
            whole(branch),
            whole(branch_other),
            whole(ln_gains),
            whole(cotangent),
            unit_weight(0),
            unit_weight(1),
            whole(up_in),
            unit_cols(up_out),
            unit_cols(down_in),
            whole(down_out),
        ],
        [
            out((rows, width), F32),
            out((rows, width), BF),
            out((rows, width), BF),
            out((rank, width), F32),
            unit_cols(shape((rank, units), F32)),
            unit_cols(shape((rank, units), F32)),
            out((rank, width), F32),
        ],
        [
            pltpu.VMEM((rows, width), BF),
            rank_keep,
            rank_keep,
            wide_acc,
            wide_acc,
            rank_acc,
            rank_acc,
        ],
        name="units",
    )
    grad_n3, grad_n3_other = with_other(grad_n3, "tp")
    branch, branch_other = with_other(branch, "tp")
    layer_out = (
        second_mid + (branch.astype(F32) + branch_other.astype(F32))
    ).astype(BF)

    def back_call(
        kernel, scalar, carried, middle, grad, grad_other, slots, queries, mixed, kv, kv_other,
        logsum, normed, query_low, low, kind, name,
    ):
        weight_slot, low_slot, query_slot, query_low_slot = slots
        count = kv.shape[1]
        kv_out = (
            shape((2, count, cols), BF),
            pl.BlockSpec((2, count, PAIR), lambda p, *_: (0, 0, p)),
        )
        return call(
            kernel,
            pairs,
            [
                whole(carried),
                whole(middle),
                whole(ln_gains),
                whole(grad),
                whole(grad_other),
                weight_pair(weight_slot),
                slot_pair(part_in, low_slot),
                slot_of(sel_out, lambda i: low_slot),
                weight_pair(query_slot),
                slot_of(sel_in, lambda i: query_low_slot),
                slot_pair(part_out, query_low_slot),
                pair_in(queries),
                pair_in(mixed),
                kv_pair(kv),
                kv_pair(kv_other),
                logsum_in(logsum),
                whole(normed),
                whole(query_low),
                whole(low),
            ],
            [
                out((rows, width), F32),
                out((rows, width), kind),
                kv_out,
                kv_out,
                by_pair(rank, F32),
                out((rank, width), F32),
                out((rank, width), F32),
                by_pair(rank, F32),
            ],
            [pltpu.VMEM((rows, width), BF), rank_keep, wide_acc, rank_acc],
            scalar,
            name=name,
        )

    grad_second, grad_n2, grad_ckv, grad_ckv_send, co_in_t, co_out_t, cq_in_t, cq_out_t = back_call(
        cross_back_kernel, None, cotangent, second_mid, grad_n3, grad_n3_other, (7, 7, 3, 4),
        cross_q, cross_mixed, cross_kv, cross_kv_other, cross_logsum, n2, cross_q_low,
        cross_o_low, BF, "cross_back",
    )
    grad_n2, grad_n2_other = with_other(grad_n2, "tp")
    grad_ckv_other = swap(grad_ckv_send, "ctx")
    grad_frames, ckv_in_t, ckv_out_t = call(
        frames_back_kernel,
        2,
        [
            at(grad_ckv),
            at(grad_ckv_other),
            weight_cols(lambda i: 4 + i),
            slot_of(sel_in, lambda i: 5 + i),
            slot_of(part_out, lambda i: 5 + i),
            whole(encoder),
            at(frames_low),
        ],
        [
            out((frames, width), BF),
            at(shape((2, rank, width), F32)),
            at(shape((2, rank, cols), F32)),
        ],
        [pltpu.VMEM((frames, width), F32)],
        name="frames_back",
    )
    grad_frames, grad_frames_other = with_other(grad_frames, "tp")
    grad_encoder = grad_frames.astype(F32) + grad_frames_other.astype(F32)
    grad_first, grad_n1_start, grad_skv, grad_skv_send, so_in_t, so_out_t, q_in_t, q_out_t = back_call(
        self_back_kernel, scalars, grad_second, first_mid, grad_n2, grad_n2_other, (6, 3, 0, 0),
        query, self_mixed, self_kv, self_kv_other, self_logsum, n1, self_low[0],
        self_o_low, F32, "self_back",
    )
    grad_skv_other = swap(grad_skv_send, "ctx")
    grad_n1, kv_in_t, kv_out_t = call(
        pair_project_kernel,
        2,
        [
            at(grad_skv),
            at(grad_skv_other),
            weight_cols(lambda i: 1 + i),
            slot_of(sel_in, lambda i: 1 + i),
            slot_of(part_out, lambda i: 1 + i),
            whole(n1),
            at(self_low, 1),
            whole(grad_n1_start),
        ],
        [
            out((rows, width), BF),
            at(shape((2, rank, width), F32)),
            at(shape((2, rank, cols), F32)),
        ],
        [wide_acc],
        name="self_project_back",
    )
    grad_n1, grad_n1_other = with_other(grad_n1, "tp")
    grad_hidden = grad_first + normalize_back(
        hidden.astype(F32), ln_gains[0], grad_n1.astype(F32) + grad_n1_other.astype(F32)
    )

    early_full = [cq_in_t, ckv_in_t[0], ckv_in_t[1], co_out_t, up_in_t, down_out_t]
    early_part = [co_in_t, cq_out_t, ckv_out_t[0], ckv_out_t[1]]
    late_full = [q_in_t, kv_in_t[0], kv_in_t[1], so_out_t]
    late_part = [so_in_t, q_out_t, kv_out_t[0], kv_out_t[1]]
    broad = [up_out_t, down_in_t]
    regular = (
        ctx_size == 2 and tp_size == 2 and rank == 16
        and width == LANE * fsdp_size and wide == 4 * LANE * fsdp_size
    )
    if regular:

        def exchange(full, part, wides, order, tagged, name):
            per_group = (len(order) + 3) // 4
            count = 16 * (per_group + len(wides) + tagged)
            dims = (fsdp_size, 2, count, LANE)

            def kernel(*refs):
                pack_kernel(len(full), len(part), len(wides), order, tagged, *refs)

            keep, send = call(
                kernel,
                1,
                [whole(a) for a in full + part + wides],
                [out(dims, F32), out(dims, F32)],
                scalars=scalars,
                name=name,
            )
            recv = swap(send, "ctx")

            def pick(i):
                return lax.dynamic_index_in_dim(keep, i, 1, keepdims=False) + (
                    lax.dynamic_index_in_dim(recv, i, 1, keepdims=False)
                )

            away = swap(pick(1 - tensor_index).astype(BF), "tp")
            total = (pick(tensor_index) + away.astype(F32)).astype(BF)
            return lax.all_to_all(total, "fsdp", 0, 0, tiled=True)

        early = exchange(
            early_full, early_part, broad, (0, 1, 2, 6, 7, 8, 9, 3, 4, 5), 1, "pack_early"
        )
        late = exchange(late_full, late_part, [], (0, 1, 2, 4, 5, 6, 7, 3), 0, "pack_late")
        narrow_out = (attn_adapt_in.shape[0], adapters, rank, PIECE)
        tables = call(
            unpack_kernel,
            1,
            [whole(early), whole(late)],
            [
                out(narrow_out, F32),
                out(narrow_out, F32),
                out((adapters, rank, PIECE), F32),
                out((adapters, rank, LANE), F32),
                out((adapters, rank, LANE), F32),
                out((adapters, rank, PIECE), F32),
            ],
            name="unpack",
        )
    else:
        chosen = (mine == jnp.arange(adapters, dtype=jnp.int32)).astype(F32)

        def summed(parts, start, full):
            def spread_out(part):
                if part.shape[1] == full:
                    return part
                blank = jnp.zeros((part.shape[0], full), F32)
                return lax.dynamic_update_slice_in_dim(blank, part, start, axis=1)

            stacked = jnp.stack([spread_out(p) for p in parts])
            table = chosen[None, :, None, None] * stacked[:, None]
            return lax.psum_scatter(
                table, ("fsdp", "ctx", "tp"), scatter_dimension=3, tiled=True
            )

        attn_in_t = summed(
            late_full[:3] + [so_in_t] + early_full[:3] + [co_in_t], head_start, width
        )
        attn_out_t = summed(
            late_part[1:] + [so_out_t] + early_part[1:] + [co_out_t], head_start, width
        )
        small = summed([up_in_t, down_out_t], head_start, width)
        large = summed(broad, unit_start, wide)
        tables = (attn_in_t, attn_out_t, small[0], large[0], large[1], small[1])
    return (
        layer_out[None],
        grad_hidden[None],
        grad_encoder[None],
        *tables,
    )
def solution(mesh):
    in_specs = (
        P("fsdp", "ctx", None),
        P("fsdp", "ctx", None),
        P("fsdp", "ctx", None),
        P("fsdp"),
        P(),
        P(None, "fsdp", "tp"),
        P(None, "fsdp", "tp"),
        P("fsdp", "tp"),
        P("fsdp", "tp"),
        P(),
        P(),
        P(),
        P(),
        P(),
        P(),
    )
    out_specs = (
        P("fsdp", "ctx", None),
        P("fsdp", "ctx", None),
        P("fsdp", "ctx", None),
        P(None, None, None, ("fsdp", "ctx", "tp")),
        P(None, None, None, ("fsdp", "ctx", "tp")),
        P(None, None, ("fsdp", "ctx", "tp")),
        P(None, None, ("fsdp", "ctx", "tp")),
        P(None, None, ("fsdp", "ctx", "tp")),
        P(None, None, ("fsdp", "ctx", "tp")),
    )
    return jax.shard_map(
        on_device, mesh=mesh, in_specs=in_specs, out_specs=out_specs, check_vma=False
    )
```

```python
from functools import partial

import jax
import jax.numpy as jnp
from jax import lax
from jax.experimental import pallas as pl
from jax.experimental.pallas import tpu as pltpu
from jax.sharding import PartitionSpec as P

HEAD_DIM = 64
PAIR = 2 * HEAD_DIM
EPSILON = 1e-05
MASKED_SCORE = -1000000000.0
SCALE = HEAD_DIM ** (-0.5)
BF = jnp.bfloat16
F32 = jnp.float32


def mm(a, b):
    return lax.dot_general(a, b, (((1,), (0,)), ((), ())), preferred_element_type=F32)


def mm_nt(a, b):
    return lax.dot_general(a, b, (((1,), (1,)), ((), ())), preferred_element_type=F32)


def mm_tn(a, b):
    return lax.dot_general(a, b, (((0,), (0,)), ((), ())), preferred_element_type=F32)


def norm_parts(rows):
    centred = rows - jnp.mean(rows, axis=-1, keepdims=True)
    spread = jnp.mean(centred * centred, axis=-1, keepdims=True)
    inverse = lax.rsqrt(spread + EPSILON)
    return centred * inverse, inverse


def normalize(rows, gain):
    return norm_parts(rows)[0] * gain


def normalize_back(rows, gain, gradient):
    unit, inverse = norm_parts(rows)
    scaled = gradient * gain
    first = jnp.mean(scaled, axis=-1, keepdims=True)
    second = jnp.mean(scaled * unit, axis=-1, keepdims=True)
    return (scaled - first - unit * second) * inverse


def swap(value, axis):
    return lax.ppermute(value, axis, [(0, 1), (1, 0)])


def with_other(partial_value, axis):
    if lax.axis_size(axis) == 2:
        return partial_value, swap(partial_value, axis)
    return lax.psum(partial_value, axis), jnp.zeros_like(partial_value)


def matrix(ref):
    block = ref[...]
    return block.reshape(block.shape[0] * block.shape[2], block.shape[3])


def half_masks(rows):
    lane = lax.broadcasted_iota(jnp.int32, (rows, PAIR), 1)
    return lane < HEAD_DIM, lane >= HEAD_DIM


def pick_half(rows, keep):
    return jnp.where(keep, rows, jnp.zeros_like(rows))


def join_halves(first, second):
    row = lax.broadcasted_iota(jnp.int32, first.shape, 0)
    return jnp.where(row < HEAD_DIM, first, second).T


def pair_forward(queries, keys, values, limit):
    mixed, logsums = [], []
    for keep in half_masks(queries.shape[0]):
        mine = pick_half(queries, keep)
        scores = [limit(i, mm_nt(k, mine) * SCALE) for i, k in enumerate(keys)]
        top = jnp.max(scores[0], axis=0, keepdims=True)
        for s in scores[1:]:
            top = jnp.maximum(top, jnp.max(s, axis=0, keepdims=True))
        powers = [jnp.exp(s - top) for s in scores]
        total = sum(jnp.sum(e, axis=0, keepdims=True) for e in powers)
        share = 1.0 / total
        out = sum(mm_tn(v, (e * share).astype(BF)) for v, e in zip(values, powers))
        mixed.append(out)
        logsums.append(top + jnp.log(total))
    return join_halves(*mixed), logsums


def pair_backward(grad, queries, keys, values, logsums, limit):
    grad_query, grad_keys, grad_values = [], [0.0] * len(keys), [0.0] * len(keys)
    for keep, logsum in zip(half_masks(queries.shape[0]), logsums):
        mine = pick_half(queries, keep)
        grad_mine = pick_half(grad, keep)
        weights = [
            jnp.exp(limit(i, mm_nt(k, mine) * SCALE) - logsum) for i, k in enumerate(keys)
        ]
        grad_weights = [mm_nt(v, grad_mine) for v in values]
        inner = sum(
            jnp.sum(g * w, axis=0, keepdims=True) for g, w in zip(grad_weights, weights)
        )
        part = 0.0
        for i, key in enumerate(keys):
            grad_scores = (weights[i] * (grad_weights[i] - inner)).astype(BF)
            part = part + mm_tn(key, grad_scores)
            grad_keys[i] = grad_keys[i] + mm(grad_scores, mine)
            grad_values[i] = grad_values[i] + mm(weights[i].astype(BF), grad_mine)
        grad_query.append(part)
    return (
        (join_halves(*grad_query) * SCALE).astype(BF),
        [(g * SCALE).astype(BF) for g in grad_keys],
        [g.astype(BF) for g in grad_values],
    )


def no_limit(index, scores):
    return scores


def causal_limit(context):
    def limit(index, scores):
        if index == 0:
            key = lax.broadcasted_iota(jnp.int32, scores.shape, 0)
            query = lax.broadcasted_iota(jnp.int32, scores.shape, 1)
            return jnp.where(key <= query, scores, MASKED_SCORE)
        return jnp.where(context == 1, scores, MASKED_SCORE)

    return limit


def at_first(step=0):
    return pl.when(pl.program_id(0) == step)


def at_last():
    return pl.when(pl.program_id(0) == pl.num_programs(0) - 1)


def qkv_kernel(hidden, gains, weight, low_in, low_out, normed, query, key_value, low):
    @at_first()
    def _():
        normed[...] = normalize(hidden[...].astype(F32), gains[0:1, :]).astype(BF)

    rows = normed[...]
    rank_rows = mm_nt(rows, low_in[0]).astype(BF)
    low[0] = rank_rows
    value = (mm(rows, matrix(weight)) + mm(rank_rows, low_out[0])).astype(BF)

    @at_first()
    def _():
        query[...] = value

    @pl.when(pl.program_id(0) > 0)
    def _():
        key_value[0] = value


def frames_kernel(frames, weight, low_in, low_out, key_value, low):
    rows = frames[...]
    rank_rows = mm_nt(rows, low_in[0]).astype(BF)
    low[0] = rank_rows
    count = rows.shape[0]
    key_value[0, :count] = (mm(rows, matrix(weight)) + mm(rank_rows, low_out[0])).astype(BF)
    spare = key_value.shape[1] - count
    if spare:
        key_value[0, count:] = jnp.zeros((spare, key_value.shape[2]), BF)


def self_kernel(
    where, query, mine, other, weight, low_in, low_out, mixed, logsum, branch, low, acc, low_acc
):
    @at_first()
    def _():
        acc[...] = jnp.zeros_like(acc)
        low_acc[...] = jnp.zeros_like(low_acc)

    out, logs = pair_forward(
        query[...], (mine[0], other[0]), (mine[1], other[1]), causal_limit(where[0])
    )
    out = out.astype(BF)
    mixed[...] = out
    logsum[0, 0:1, :] = logs[0]
    logsum[0, 1:2, :] = logs[1]
    acc[...] += mm_nt(out, matrix(weight))
    low_acc[...] += mm_nt(out, low_in[0])

    @at_last()
    def _():
        rank_rows = low_acc[...].astype(BF)
        low[...] = rank_rows
        branch[...] = (acc[...] + mm(rank_rows, low_out[0])).astype(BF)


def cross_kernel(
    count,
    hidden, branch_mine, branch_other, gains, query_weight, query_in, query_out, mine, other,
    weight, low_in, low_out,
    middle, normed, query, query_low, mixed, logsum, branch, low, acc, low_acc,
):
    @at_first()
    def _():
        acc[...] = jnp.zeros_like(acc)
        low_acc[...] = jnp.zeros_like(low_acc)
        total = hidden[...].astype(F32) + (
            branch_mine[...].astype(F32) + branch_other[...].astype(F32)
        )
        middle[...] = total
        rows = normalize(total, gains[1:2, :]).astype(BF)
        normed[...] = rows
        query_low[...] = mm_nt(rows, query_in[0]).astype(BF)

    queries = (
        mm(normed[...], matrix(query_weight)) + mm(query_low[...], query_out[0])
    ).astype(BF)
    query[...] = queries
    out, logs = pair_forward(
        queries,
        (mine[0, :count], other[0, :count]),
        (mine[1, :count], other[1, :count]),
        no_limit,
    )
    out = out.astype(BF)
    mixed[...] = out
    logsum[0, 0:1, :] = logs[0]
    logsum[0, 1:2, :] = logs[1]
    acc[...] += mm_nt(out, matrix(weight))
    low_acc[...] += mm_nt(out, low_in[0])

    @at_last()
    def _():
        rank_rows = low_acc[...].astype(BF)
        low[...] = rank_rows
        branch[...] = (acc[...] + mm(rank_rows, low_out[0])).astype(BF)


def units_kernel(
    middle, branch_mine, branch_other, gains, cotangent, up, down, up_in, up_out, down_in,
    down_out,
    second, branch, grad_normed, table_up_in, table_up_out, table_down_in, table_down_out,
    normed, up_low, down_back, acc, back, low_acc, back_low,
):
    @at_first()
    def _():
        total = middle[...] + (branch_mine[...].astype(F32) + branch_other[...].astype(F32))
        second[...] = total
        rows = normalize(total, gains[2:3, :]).astype(BF)
        normed[...] = rows
        up_low[...] = mm_nt(rows, up_in[...]).astype(BF)
        down_back[...] = mm_nt(cotangent[...], down_out[...]).astype(BF)
        acc[...] = jnp.zeros_like(acc)
        back[...] = jnp.zeros_like(back)
        low_acc[...] = jnp.zeros_like(low_acc)
        back_low[...] = jnp.zeros_like(back_low)

    up_rows, down_rows = matrix(up), matrix(down)
    value = mm(normed[...], up_rows) + mm(up_low[...], up_out[...])
    spread = 1.0 + lax.erf(value * 0.7071067811865476)
    act = (0.5 * value * spread).astype(BF)
    slope = 0.5 * spread + value * (0.3989422804014327 * jnp.exp(-0.5 * value * value))
    acc[...] += mm_nt(act, down_rows)
    low_acc[...] += mm_nt(act, down_in[...])
    grad_act = mm(cotangent[...], down_rows) + mm(down_back[...], down_in[...])
    grad = (grad_act * slope).astype(BF)
    back[...] += mm_nt(grad, up_rows)
    back_low[...] += mm_nt(grad, up_out[...])
    table_up_out[...] = mm_tn(up_low[...], grad)
    table_down_in[...] = mm_tn(down_back[...], act)

    @at_last()
    def _():
        down_low = low_acc[...].astype(BF)
        branch[...] = (acc[...] + mm(down_low, down_out[...])).astype(BF)
        up_back = back_low[...].astype(BF)
        grad_normed[...] = (back[...] + mm(up_back, up_in[...])).astype(BF)
        table_up_in[...] = mm_tn(up_back, normed[...])
        table_down_out[...] = mm_tn(down_low, cotangent[...])


def attention_back(
    limit, slot, count, carried, rows, gains, grad_mine, grad_other, weight, low_in, low_out,
    query_weight, query_in, query_out, query, mixed, mine, other, logsum, normed, query_low, low,
    carry, grad_normed, grad_kv, grad_kv_other,
    table_in, table_out, table_query_in, table_query_out,
    narrow, back_low, acc, query_back,
):
    @at_first()
    def _():
        total = carried[...].astype(F32) + normalize_back(
            rows[...],
            gains[slot : slot + 1, :],
            grad_mine[...].astype(F32) + grad_other[...].astype(F32),
        )
        carry[...] = total
        narrow[...] = total.astype(BF)
        back_low[...] = mm_nt(narrow[...], low_out[0]).astype(BF)
        acc[...] = jnp.zeros_like(acc)
        query_back[...] = jnp.zeros_like(query_back)
        table_out[...] = mm_tn(low[...], narrow[...])

    grad = (mm(narrow[...], matrix(weight)) + mm(back_low[...], low_in[0])).astype(BF)
    table_in[...] = mm_tn(back_low[...], mixed[...])
    grad_query, grad_keys, grad_values = pair_backward(
        grad,
        query[...],
        (mine[0, :count], other[0, :count]),
        (mine[1, :count], other[1, :count]),
        (logsum[0, 0:1, :], logsum[0, 1:2, :]),
        limit,
    )
    for which, (first, second) in enumerate((grad_keys, grad_values)):
        grad_kv[which, :count] = first
        grad_kv_other[which, :count] = second
        spare = grad_kv.shape[1] - count
        if spare:
            grad_kv[which, count:] = jnp.zeros((spare, PAIR), BF)
            grad_kv_other[which, count:] = jnp.zeros((spare, PAIR), BF)
    acc[...] += mm_nt(grad_query, matrix(query_weight))
    query_back[...] += mm_nt(grad_query, query_out[0])
    table_query_out[...] = mm_tn(query_low[0], grad_query)

    @at_last()
    def _():
        rank_rows = query_back[...].astype(BF)
        total = acc[...] + mm(rank_rows, query_in[0])
        grad_normed[...] = total.astype(grad_normed.dtype)
        table_query_in[...] = mm_tn(rank_rows, normed[...])


def self_back_kernel(count, where, *refs):
    attention_back(causal_limit(where[0]), 1, count, *refs)


def pair_project_kernel(
    grad_mine, grad_other, weight, low_in, low_out, rows, low, start, total, table_in, table_out,
    acc,
):
    @at_first()
    def _():
        acc[...] = start[...]

    pair_project_step(
        grad_mine, grad_other, weight, low_in, low_out, rows, low, table_in, table_out, acc
    )

    @at_last()
    def _():
        total[...] = acc[...].astype(BF)


def add_rows_kernel(top, top_other, low, low_other, total):
    count = top.shape[0]
    first = top[...].astype(F32) + top_other[...].astype(F32)
    second = low[...].astype(F32) + low_other[...].astype(F32)
    total[:count] = first[:, None, :]
    total[count:] = second[:, None, :]


def frames_back_kernel(
    grad_mine, grad_other, weight, low_in, low_out, rows, low, top, rest, table_in, table_out, acc
):
    @at_first()
    def _():
        acc[...] = jnp.zeros_like(acc)

    pair_project_step(
        grad_mine, grad_other, weight, low_in, low_out, rows, low, table_in, table_out, acc
    )

    @at_last()
    def _():
        count = top.shape[0]
        top[...] = acc[:count].astype(BF)
        rest[...] = acc[count:].astype(BF)


def pair_project_step(
    grad_mine, grad_other, weight, low_in, low_out, rows, low, table_in, table_out, acc
):
    count = rows.shape[0]
    grad = (grad_mine[0, :count].astype(F32) + grad_other[0, :count].astype(F32)).astype(BF)
    rank_rows = mm_nt(grad, low_out[0]).astype(BF)
    acc[...] += mm_nt(grad, matrix(weight)) + mm(rank_rows, low_in[0])
    table_in[0] = mm_tn(rank_rows, rows[...])
    table_out[0] = mm_tn(low[0], grad)


LANE = 128
PIECE = 32


def pack_kernel(fulls, shares, wides, order, tagged, *refs):
    where = refs[0]
    keep, send = refs[-2:]
    flat = []
    for ref in refs[1:-2]:
        flat += [ref] if len(ref.shape) == 2 else [ref.at[i] for i in range(ref.shape[0])]
    tables, broad = flat[: fulls + shares], flat[fulls + shares :]
    context, tensor = where[0], where[1]
    blocks = keep.shape[1]
    per_group = (len(order) + 3) // 4
    rows = per_group * 16
    lane = lax.broadcasted_iota(jnp.int32, (rows, LANE), 1) // PIECE
    for f in range(blocks):
        shard = f * 2 // blocks
        local = f % (blocks // 2)

        def table_of(k):
            if k is None:
                return jnp.zeros((16, LANE), F32)
            if k < fulls:
                return tables[k][:, f * LANE : (f + 1) * LANE]
            part = tables[k][:, local * LANE : (local + 1) * LANE]
            return jnp.where(tensor == shard, part, 0.0)

        padded = list(order) + [None] * (4 * per_group - len(order))
        groups = [
            jnp.concatenate(
                [table_of(k) for k in padded[g * per_group : (g + 1) * per_group]], axis=0
            )
            for g in range(4)
        ]
        for p in range(4):
            value = jnp.zeros((rows, LANE), F32)
            for g in range(4):
                turned = pltpu.roll(groups[g], (PIECE * (g - p)) % LANE, 1)
                value = jnp.where(lane == g, turned, value)
            pieces = [value]
            for w in broad:
                at = local * 4 * LANE + p * LANE
                pieces.append(jnp.where(tensor == shard, w[:, at : at + LANE], 0.0))
            if tagged:
                tag = where[2].astype(F32) * 0.25
                pieces.append(jnp.full((16, LANE), 1.0, F32) * tag)
            whole = jnp.concatenate(pieces, axis=0)

            @pl.when(context == p // 2)
            def _(whole=whole, f=f, p=p):
                keep[p % 2, f] = whole

            @pl.when(context != p // 2)
            def _(whole=whole, f=f, p=p):
                send[p % 2, f] = whole


def unpack_kernel(early, late, attn_in, attn_out, up_in, up_out, down_in, down_out):
    clips = early.shape[0]
    adapters = attn_in.shape[1]
    tag_row = early.shape[1] - 16
    tags = [early[c, tag_row : tag_row + 1, :].astype(F32) for c in range(clips)]
    early_rows = [early[c].astype(F32) for c in range(clips)]
    late_rows = [late[c].astype(F32) for c in range(clips)]
    for a in range(adapters):
        first = jnp.zeros(early_rows[0].shape, F32)
        second = jnp.zeros(late_rows[0].shape, F32)
        for c in range(clips):
            same = (tags[c] > a - 0.5) & (tags[c] < a + 0.5)
            weight = jnp.where(same, 1.0, 0.0)
            first = first + early_rows[c] * weight
            second = second + late_rows[c] * weight

        def piece(block, k, per_group):
            g, at = k // per_group, 16 * (k % per_group)
            return block[at : at + 16, PIECE * g : PIECE * (g + 1)]

        for j in range(4):
            attn_in[j, a] = piece(second, j, 2)
            attn_out[j, a] = piece(second, 4 + j, 2)
            attn_in[4 + j, a] = piece(first, j, 3)
            attn_out[4 + j, a] = piece(first, 4 + j, 3)
        up_in[a] = piece(first, 8, 3)
        down_out[a] = piece(first, 9, 3)
        up_out[a] = first[48:64]
        down_in[a] = first[64:80]


def shape(dims, dtype):
    return jax.ShapeDtypeStruct(tuple(dims), dtype)


def fixed(array):
    zeros = (0,) * array.ndim
    return pl.BlockSpec(array.shape, lambda *_: zeros)


def fixed_out(*dims):
    zeros = (0,) * len(dims)
    return pl.BlockSpec(dims, lambda *_: zeros)


def call(kernel, steps, ins, outs, scratch=(), scalars=None, name=None, cost=5):
    arrays = [a for a, _ in ins]
    spec = pltpu.PrefetchScalarGridSpec(
        num_scalar_prefetch=0 if scalars is None else 1,
        grid=(steps,),
        in_specs=[s for _, s in ins],
        out_specs=[s for _, s in outs],
        scratch_shapes=list(scratch),
    )
    run = pl.pallas_call(
        kernel,
        grid_spec=spec,
        out_shape=[o for o, _ in outs],
        compiler_params=pltpu.CompilerParams(dimension_semantics=("arbitrary",)),
        cost_estimate=pl.CostEstimate(
            flops=cost * 1_000_000_000, transcendentals=0, bytes_accessed=cost * 3_690_000
        ),
        name=name,
    )
    return run(*arrays) if scalars is None else run(scalars, *arrays)


def on_device(
    hidden,
    encoder,
    cotangent,
    adapter_index,
    ln_gains,
    attn_in_weight,
    attn_out_weight,
    up_weight,
    down_weight,
    attn_adapt_in,
    attn_adapt_out,
    up_adapt_in,
    up_adapt_out,
    down_adapt_in,
    down_adapt_out,
):
    fsdp_size = lax.axis_size("fsdp")
    ctx_size = lax.axis_size("ctx")
    tp_size = lax.axis_size("tp")
    tensor_index = lax.axis_index("tp")
    context_index = lax.axis_index("ctx")
    hidden, encoder, cotangent = hidden[0], encoder[0], cotangent[0]
    rows, width = hidden.shape
    frames = encoder.shape[0]
    padded = -(-frames // 16) * 16
    wide = up_adapt_out.shape[2]
    cols = attn_in_weight.shape[2]
    units = up_weight.shape[1]
    rank = attn_adapt_in.shape[2]
    adapters = attn_adapt_in.shape[1]
    pairs = cols // PAIR
    head_start = tensor_index * cols
    unit_start = tensor_index * units
    mine = adapter_index[0]
    scalars = jnp.stack(
        [context_index.astype(jnp.int32), tensor_index.astype(jnp.int32), mine]
    )

    half_rows = attn_in_weight.shape[1] // ctx_size
    shards = fsdp_size * ctx_size

    def my_half(table):
        return lax.dynamic_slice_in_dim(
            table, context_index * half_rows, half_rows, axis=table.ndim - 2
        )

    attn_half = jnp.concatenate([my_half(attn_in_weight), my_half(attn_out_weight)], axis=0)
    ff_half = jnp.stack([my_half(up_weight), my_half(down_weight)])
    attn_full = lax.all_gather(attn_half, ("fsdp", "ctx"), axis=0)
    ff_full = lax.all_gather(ff_half, ("fsdp", "ctx"), axis=0)

    sel_in = lax.dynamic_index_in_dim(attn_adapt_in, mine, 1, keepdims=False)
    sel_out = lax.dynamic_index_in_dim(attn_adapt_out, mine, 1, keepdims=False)
    part_in = lax.dynamic_slice_in_dim(sel_in, head_start, cols, 2)
    part_out = lax.dynamic_slice_in_dim(sel_out, head_start, cols, 2)
    up_in = lax.dynamic_index_in_dim(up_adapt_in, mine, 0, keepdims=False)
    up_out = lax.dynamic_slice(up_adapt_out, (mine, 0, unit_start), (1, rank, units))[0]
    down_in = lax.dynamic_slice(down_adapt_in, (mine, 0, unit_start), (1, rank, units))[0]
    down_out = lax.dynamic_index_in_dim(down_adapt_out, mine, 0, keepdims=False)

    def weight_cols(slot):
        return attn_full, pl.BlockSpec((shards, 1, half_rows, cols), lambda i, *_: (0, slot(i), 0, 0))

    def weight_pair(slot):
        return attn_full, pl.BlockSpec((shards, 1, half_rows, PAIR), lambda p, *_: (0, slot, 0, p))

    def slot_of(table, slot):
        return table, pl.BlockSpec((1,) + table.shape[1:], lambda i, *_: (slot(i), 0, 0))

    def slot_pair(table, slot):
        return table, pl.BlockSpec((1, rank, PAIR), lambda p, *_: (slot, 0, p))

    def whole(array):
        return array, fixed(array)

    def out(dims, dtype):
        return shape(dims, dtype), fixed_out(*dims)

    def by_pair(count, dtype=BF):
        return shape((count, cols), dtype), pl.BlockSpec((count, PAIR), lambda p, *_: (0, p))

    def kv_pair(array):
        return array, pl.BlockSpec((2, array.shape[1], PAIR), lambda p, *_: (0, 0, p))

    def at(array, first=0):
        return array, pl.BlockSpec((1,) + array.shape[1:], lambda i, *_: (first + i, 0, 0))

    def at_slot(array):
        return array, pl.BlockSpec((1,) + array.shape[1:], lambda i, *_: (0, 0, 0))

    logsum_out = (
        shape((pairs, 2, rows), F32),
        pl.BlockSpec((1, 2, rows), lambda p, *_: (p, 0, 0)),
    )

    def logsum_in(array):
        return array, pl.BlockSpec((1, 2, rows), lambda p, *_: (p, 0, 0))

    def pair_in(array):
        return array, pl.BlockSpec((array.shape[0], PAIR), lambda p, *_: (0, p))

    wide_acc = pltpu.VMEM((rows, width), F32)
    rank_acc = pltpu.VMEM((rows, rank), F32)
    rank_keep = pltpu.VMEM((rows, rank), BF)

    n1, query, self_kv, self_low = call(
        qkv_kernel,
        3,
        [
            whole(hidden),
            whole(ln_gains),
            weight_cols(lambda i: i),
            slot_of(sel_in, lambda i: i),
            slot_of(part_out, lambda i: i),
        ],
        [
            out((rows, width), BF),
            out((rows, cols), BF),
            (
                shape((2, rows, cols), BF),
                pl.BlockSpec((1, rows, cols), lambda i: (jnp.maximum(i - 1, 0), 0, 0)),
            ),
            (shape((3, rows, rank), BF), pl.BlockSpec((1, rows, rank), lambda i: (i, 0, 0))),
        ],
        name="qkv",
    )
    self_kv_other = swap(self_kv, "ctx")
    cross_kv, frames_low = call(
        frames_kernel,
        2,
        [
            whole(encoder),
            weight_cols(lambda i: 4 + i),
            slot_of(sel_in, lambda i: 5 + i),
            slot_of(part_out, lambda i: 5 + i),
        ],
        [
            (
                shape((2, padded, cols), BF),
                pl.BlockSpec((1, padded, cols), lambda i: (i, 0, 0)),
            ),
            (
                shape((2, frames, rank), BF),
                pl.BlockSpec((1, frames, rank), lambda i: (i, 0, 0)),
            ),
        ],
        name="frames",
        cost=7,
    )
    cross_kv_other = swap(cross_kv, "ctx")
    self_mixed, self_logsum, branch, self_o_low = call(
        self_kernel,
        pairs,
        [
            pair_in(query),
            kv_pair(self_kv),
            kv_pair(self_kv_other),
            weight_pair(6),
            slot_pair(part_in, 3),
            slot_of(sel_out, lambda i: 3),
        ],
        [by_pair(rows), logsum_out, out((rows, width), BF), out((rows, rank), BF)],
        [wide_acc, rank_acc],
        scalars,
        name="self_attention",
        cost=7,
    )
    branch, branch_other = with_other(branch, "tp")
    first_mid, n2, cross_q, cross_q_low, cross_mixed, cross_logsum, branch, cross_o_low = call(
        partial(cross_kernel, frames),
        pairs,
        [
            whole(hidden),
            whole(branch),
            whole(branch_other),
            whole(ln_gains),
            weight_pair(3),
            slot_of(sel_in, lambda i: 4),
            slot_pair(part_out, 4),
            kv_pair(cross_kv),
            kv_pair(cross_kv_other),
            weight_pair(7),
            slot_pair(part_in, 7),
            slot_of(sel_out, lambda i: 7),
        ],
        [
            out((rows, width), F32),
            out((rows, width), BF),
            by_pair(rows),
            out((rows, rank), BF),
            by_pair(rows),
            logsum_out,
            out((rows, width), BF),
            out((rows, rank), BF),
        ],
        [wide_acc, rank_acc],
        name="cross_attention",
        cost=13,
    )
    branch, branch_other = with_other(branch, "tp")
    chunk = min(units, 512)

    def unit_weight(slot):
        return ff_full, pl.BlockSpec((shards, 1, half_rows, chunk), lambda i: (0, slot, 0, i))

    def unit_cols(array):
        return array, pl.BlockSpec((rank, chunk), lambda i: (0, i))

    second_mid, branch, grad_n3, up_in_t, up_out_t, down_in_t, down_out_t = call(
        units_kernel,
        units // chunk,
        [
            whole(first_mid),
            whole(branch),
            whole(branch_other),
            whole(ln_gains),
            whole(cotangent),
            unit_weight(0),
            unit_weight(1),
            whole(up_in),
            unit_cols(up_out),
            unit_cols(down_in),
            whole(down_out),
        ],
        [
            out((rows, width), F32),
            out((rows, width), BF),
            out((rows, width), BF),
            out((rank, width), F32),
            unit_cols(shape((rank, units), F32)),
            unit_cols(shape((rank, units), F32)),
            out((rank, width), F32),
        ],
        [
            pltpu.VMEM((rows, width), BF),
            rank_keep,
            rank_keep,
            wide_acc,
            wide_acc,
            rank_acc,
            rank_acc,
        ],
        name="units",
        cost=11,
    )
    grad_n3, grad_n3_other = with_other(grad_n3, "tp")
    branch, branch_other = with_other(branch, "tp")

    def back_call(
        kernel, scalar, carried, middle, grad, grad_other, slots, queries, mixed, kv, kv_other,
        logsum, normed, query_low, low, kind, name, cost,
    ):
        weight_slot, low_slot, query_slot, query_low_slot = slots
        count = kv.shape[1]
        kv_out = (
            shape((2, count, cols), BF),
            pl.BlockSpec((2, count, PAIR), lambda p, *_: (0, 0, p)),
        )
        return call(
            kernel,
            pairs,
            [
                whole(carried),
                whole(middle),
                whole(ln_gains),
                whole(grad),
                whole(grad_other),
                weight_pair(weight_slot),
                slot_pair(part_in, low_slot),
                slot_of(sel_out, lambda i: low_slot),
                weight_pair(query_slot),
                slot_of(sel_in, lambda i: query_low_slot),
                slot_pair(part_out, query_low_slot),
                pair_in(queries),
                pair_in(mixed),
                kv_pair(kv),
                kv_pair(kv_other),
                logsum_in(logsum),
                whole(normed),
                at_slot(query_low),
                whole(low),
            ],
            [
                out((rows, width), F32),
                out((rows, width), kind),
                kv_out,
                kv_out,
                by_pair(rank, F32),
                out((rank, width), F32),
                out((rank, width), F32),
                by_pair(rank, F32),
            ],
            [pltpu.VMEM((rows, width), BF), rank_keep, wide_acc, rank_acc],
            scalar,
            name=name,
            cost=cost,
        )

    grad_second, grad_n2, grad_ckv, grad_ckv_send, co_in_t, co_out_t, cq_in_t, cq_out_t = back_call(
        partial(attention_back, no_limit, 2, frames), None, cotangent, second_mid, grad_n3, grad_n3_other, (7, 7, 3, 4),
        cross_q, cross_mixed, cross_kv, cross_kv_other, cross_logsum, n2, cross_q_low[None],
        cross_o_low, BF, "cross_back", 18,
    )
    grad_n2, grad_n2_other = with_other(grad_n2, "tp")
    grad_ckv_other = swap(grad_ckv_send, "ctx")
    grad_ckv_other, branch_other = lax.optimization_barrier((grad_ckv_other, branch_other))
    layer_out = (
        second_mid + (branch.astype(F32) + branch_other.astype(F32))
    ).astype(BF)
    first_half = padded // 2
    grad_top, grad_low, ckv_in_t, ckv_out_t = call(
        frames_back_kernel,
        2,
        [
            at(grad_ckv),
            at(grad_ckv_other),
            weight_cols(lambda i: 4 + i),
            slot_of(sel_in, lambda i: 5 + i),
            slot_of(part_out, lambda i: 5 + i),
            whole(encoder),
            at(frames_low),
        ],
        [
            out((first_half, width), BF),
            out((frames - first_half, width), BF),
            at(shape((2, rank, width), F32)),
            at(shape((2, rank, cols), F32)),
        ],
        [pltpu.VMEM((frames, width), F32)],
        name="frames_back",
        cost=9,
    )
    grad_top, grad_low, grad_n2_other = lax.optimization_barrier(
        (grad_top, grad_low, grad_n2_other)
    )
    grad_top, grad_top_other = with_other(grad_top, "tp")
    grad_low, grad_low_other = with_other(grad_low, "tp")
    grad_first, grad_n1_start, grad_skv, grad_skv_send, so_in_t, so_out_t, q_in_t, q_out_t = back_call(
        partial(self_back_kernel, rows), scalars, grad_second, first_mid, grad_n2, grad_n2_other, (6, 3, 0, 0),
        query, self_mixed, self_kv, self_kv_other, self_logsum, n1, self_low,
        self_o_low, F32, "self_back", 12,
    )
    grad_skv_other = swap(grad_skv_send, "ctx")
    grad_skv_other, grad_top_other = lax.optimization_barrier((grad_skv_other, grad_top_other))
    grad_n1, kv_in_t, kv_out_t = call(
        pair_project_kernel,
        2,
        [
            at(grad_skv),
            at(grad_skv_other),
            weight_cols(lambda i: 1 + i),
            slot_of(sel_in, lambda i: 1 + i),
            slot_of(part_out, lambda i: 1 + i),
            whole(n1),
            at(self_low, 1),
            whole(grad_n1_start),
        ],
        [
            out((rows, width), BF),
            at(shape((2, rank, width), F32)),
            at(shape((2, rank, cols), F32)),
        ],
        [wide_acc],
        name="self_project_back",
    )
    grad_n1, grad_n1_other = with_other(grad_n1, "tp")
    grad_encoder = call(
        add_rows_kernel,
        1,
        [whole(grad_top), whole(grad_top_other), whole(grad_low), whole(grad_low_other)],
        [out((frames, 1, width), F32)],
        name="encoder_total",
    )[0].reshape(frames, width)
    grad_hidden = grad_first + normalize_back(
        hidden.astype(F32), ln_gains[0], grad_n1.astype(F32) + grad_n1_other.astype(F32)
    )

    early_full = [cq_in_t, ckv_in_t, co_out_t, up_in_t, down_out_t]
    early_part = [co_in_t, cq_out_t, ckv_out_t]
    late_full = [q_in_t, kv_in_t, so_out_t]
    late_part = [so_in_t, q_out_t, kv_out_t]
    broad = [up_out_t, down_in_t]
    regular = (
        ctx_size == 2 and tp_size == 2 and rank == 16
        and width == LANE * fsdp_size and wide == 4 * LANE * fsdp_size
    )
    if regular:

        def exchange(full, part, wides, order, tagged, name):
            per_group = (len(order) + 3) // 4
            count = 16 * (per_group + len(wides) + tagged)
            dims = (2, fsdp_size, count, LANE)

            def number(arrays):
                return sum(1 if a.ndim == 2 else a.shape[0] for a in arrays)

            def kernel(*refs):
                pack_kernel(number(full), number(part), len(wides), order, tagged, *refs)

            keep, send = call(
                kernel,
                1,
                [whole(a) for a in full + part + wides],
                [out(dims, F32), out(dims, F32)],
                scalars=scalars,
                name=name,
            )
            recv = swap(send, "ctx")

            def pick(i):
                return lax.dynamic_index_in_dim(keep, i, 0, keepdims=False) + (
                    lax.dynamic_index_in_dim(recv, i, 0, keepdims=False)
                )

            away = swap(pick(1 - tensor_index).astype(BF), "tp")
            total = (pick(tensor_index) + away.astype(F32)).astype(BF)
            return lax.all_to_all(total, "fsdp", 0, 0, tiled=True)

        early = exchange(
            early_full, early_part, broad, (0, 1, 2, 6, 7, 8, 9, 3, 4, 5), 1, "pack_early"
        )
        late = exchange(late_full, late_part, [], (0, 1, 2, 4, 5, 6, 7, 3), 0, "pack_late")
        narrow_out = (attn_adapt_in.shape[0], adapters, rank, PIECE)
        tables = call(
            unpack_kernel,
            1,
            [whole(early), whole(late)],
            [
                out(narrow_out, F32),
                out(narrow_out, F32),
                out((adapters, rank, PIECE), F32),
                out((adapters, rank, LANE), F32),
                out((adapters, rank, LANE), F32),
                out((adapters, rank, PIECE), F32),
            ],
            name="unpack",
        )
    else:
        chosen = (mine == jnp.arange(adapters, dtype=jnp.int32)).astype(F32)

        def summed(parts, start, full):
            parts = [t for p in parts for t in ([p] if p.ndim == 2 else [p[0], p[1]])]

            def spread_out(part):
                if part.shape[1] == full:
                    return part
                blank = jnp.zeros((part.shape[0], full), F32)
                return lax.dynamic_update_slice_in_dim(blank, part, start, axis=1)

            stacked = jnp.stack([spread_out(p) for p in parts])
            table = chosen[None, :, None, None] * stacked[:, None]
            return lax.psum_scatter(
                table, ("fsdp", "ctx", "tp"), scatter_dimension=3, tiled=True
            )

        attn_in_t = summed(
            late_full[:2] + [so_in_t] + early_full[:2] + [co_in_t], head_start, width
        )
        attn_out_t = summed(
            late_part[1:] + [so_out_t] + early_part[1:] + [co_out_t], head_start, width
        )
        small = summed([up_in_t, down_out_t], head_start, width)
        large = summed(broad, unit_start, wide)
        tables = (attn_in_t, attn_out_t, small[0], large[0], large[1], small[1])
    return (
        layer_out[None],
        grad_hidden[None],
        grad_encoder[None],
        *tables,
    )
def solution(mesh):
    in_specs = (
        P("fsdp", "ctx", None),
        P("fsdp", "ctx", None),
        P("fsdp", "ctx", None),
        P("fsdp"),
        P(),
        P(None, "fsdp", "tp"),
        P(None, "fsdp", "tp"),
        P("fsdp", "tp"),
        P("fsdp", "tp"),
        P(),
        P(),
        P(),
        P(),
        P(),
        P(),
    )
    out_specs = (
        P("fsdp", "ctx", None),
        P("fsdp", "ctx", None),
        P("fsdp", "ctx", None),
        P(None, None, None, ("fsdp", "ctx", "tp")),
        P(None, None, None, ("fsdp", "ctx", "tp")),
        P(None, None, ("fsdp", "ctx", "tp")),
        P(None, None, ("fsdp", "ctx", "tp")),
        P(None, None, ("fsdp", "ctx", "tp")),
        P(None, None, ("fsdp", "ctx", "tp")),
    )
    return jax.shard_map(
        on_device, mesh=mesh, in_specs=in_specs, out_specs=out_specs, check_vma=False
    )
```

```python
from functools import partial

import jax
import jax.numpy as jnp
from jax import lax
from jax.experimental import pallas as pl
from jax.experimental.pallas import tpu as pltpu
from jax.sharding import PartitionSpec as P

HEAD_DIM = 64
PAIR = 2 * HEAD_DIM
EPSILON = 1e-05
MASKED_SCORE = -1000000000.0
SCALE = HEAD_DIM ** (-0.5)
BF = jnp.bfloat16
F32 = jnp.float32


def mm(a, b):
    return lax.dot_general(a, b, (((1,), (0,)), ((), ())), preferred_element_type=F32)


def mm_nt(a, b):
    return lax.dot_general(a, b, (((1,), (1,)), ((), ())), preferred_element_type=F32)


def mm_tn(a, b):
    return lax.dot_general(a, b, (((0,), (0,)), ((), ())), preferred_element_type=F32)


def norm_parts(rows):
    centred = rows - jnp.mean(rows, axis=-1, keepdims=True)
    spread = jnp.mean(centred * centred, axis=-1, keepdims=True)
    inverse = lax.rsqrt(spread + EPSILON)
    return centred * inverse, inverse


def normalize(rows, gain):
    return norm_parts(rows)[0] * gain


def normalize_back(rows, gain, gradient):
    unit, inverse = norm_parts(rows)
    scaled = gradient * gain
    first = jnp.mean(scaled, axis=-1, keepdims=True)
    second = jnp.mean(scaled * unit, axis=-1, keepdims=True)
    return (scaled - first - unit * second) * inverse


def swap(value, axis):
    return lax.ppermute(value, axis, [(0, 1), (1, 0)])


def with_other(partial_value, axis):
    if lax.axis_size(axis) == 2:
        return partial_value, swap(partial_value, axis)
    return lax.psum(partial_value, axis), jnp.zeros_like(partial_value)


def matrix(ref):
    block = ref[...]
    return block.reshape(block.shape[0] * block.shape[2], block.shape[3])


def half_masks(rows):
    lane = lax.broadcasted_iota(jnp.int32, (rows, PAIR), 1)
    return lane < HEAD_DIM, lane >= HEAD_DIM


def pick_half(rows, keep):
    return jnp.where(keep, rows, jnp.zeros_like(rows))


def join_halves(first, second):
    row = lax.broadcasted_iota(jnp.int32, first.shape, 0)
    return jnp.where(row < HEAD_DIM, first, second).T


def pair_forward(queries, keys, values, limit, saved=None):
    mixed, logsums = [], []
    turned = [v.T for v in values]
    for half, keep in enumerate(half_masks(queries.shape[0])):
        mine = pick_half(queries, keep) * BF(SCALE)
        scores = [limit(i, mm_nt(k, mine)) for i, k in enumerate(keys)]
        top = jnp.max(scores[0], axis=0, keepdims=True)
        for s in scores[1:]:
            top = jnp.maximum(top, jnp.max(s, axis=0, keepdims=True))
        powers = [jnp.exp(s - top) for s in scores]
        total = sum(jnp.sum(e, axis=0, keepdims=True) for e in powers)
        share = 1.0 / total
        weights = [(e * share).astype(BF) for e in powers]
        if saved is not None:
            for i, w in enumerate(weights):
                saved[0, half, i, : w.shape[0]] = w
        mixed.append(sum(mm(v, w) for v, w in zip(turned, weights)))
        logsums.append(top + jnp.log(total))
    return join_halves(*mixed), logsums


def pair_backward(grad, mixed, queries, keys, values, logsums, limit, saved=None):
    grad_query, grad_keys, grad_values = [], [0.0] * len(keys), [0.0] * len(keys)
    inners = (grad.astype(F32) * mixed.astype(F32)).T
    turned = [k.T for k in keys]
    for half, (keep, logsum) in enumerate(zip(half_masks(queries.shape[0]), logsums)):
        mine = pick_half(queries, keep) * BF(SCALE)
        grad_mine = pick_half(grad, keep)
        at = HEAD_DIM * half
        inner = jnp.sum(inners[at : at + HEAD_DIM], axis=0, keepdims=True)
        part = 0.0
        for i, (key, value) in enumerate(zip(keys, values)):
            if saved is None:
                weights = jnp.exp(limit(i, mm_nt(key, mine)) - logsum)
                rounded = weights.astype(BF)
            else:
                rounded = saved[0, half, i, : key.shape[0]]
                weights = rounded.astype(F32)
            grad_scores = (weights * (mm_nt(value, grad_mine) - inner)).astype(BF)
            part = part + mm(turned[i], grad_scores)
            grad_keys[i] = grad_keys[i] + mm(grad_scores, mine)
            grad_values[i] = grad_values[i] + mm(rounded, grad_mine)
        grad_query.append(part)
    return (
        (join_halves(*grad_query) * SCALE).astype(BF),
        [g.astype(BF) for g in grad_keys],
        [g.astype(BF) for g in grad_values],
    )


def no_limit(index, scores):
    return scores


def causal_limit(context):
    def limit(index, scores):
        if index == 0:
            key = lax.broadcasted_iota(jnp.int32, scores.shape, 0)
            query = lax.broadcasted_iota(jnp.int32, scores.shape, 1)
            return jnp.where(key <= query, scores, MASKED_SCORE)
        return jnp.where(context == 1, scores, MASKED_SCORE)

    return limit


def at_first(step=0):
    return pl.when(pl.program_id(0) == step)


def at_last():
    return pl.when(pl.program_id(0) == pl.num_programs(0) - 1)


def qkv_kernel(hidden, gains, weight, low_in, low_out, normed, query, key_value, low):
    @at_first()
    def _():
        normed[...] = normalize(hidden[...].astype(F32), gains[0:1, :]).astype(BF)

    rows = normed[...]
    rank_rows = mm_nt(rows, low_in[0]).astype(BF)
    low[0] = rank_rows
    value = (mm(rows, matrix(weight)) + mm(rank_rows, low_out[0])).astype(BF)

    @at_first()
    def _():
        query[...] = value

    @pl.when(pl.program_id(0) > 0)
    def _():
        key_value[0] = value


def frames_kernel(frames, weight, low_in, low_out, key_value, low):
    rows = frames[...]
    rank_rows = mm_nt(rows, low_in[0]).astype(BF)
    low[0] = rank_rows
    count = rows.shape[0]
    key_value[0, :count] = (mm(rows, matrix(weight)) + mm(rank_rows, low_out[0])).astype(BF)
    spare = key_value.shape[1] - count
    if spare:
        key_value[0, count:] = jnp.zeros((spare, key_value.shape[2]), BF)


def self_kernel(
    where, query, mine, other, weight, low_in, low_out, mixed, logsum, branch, low, acc, low_acc
):
    @at_first()
    def _():
        acc[...] = jnp.zeros_like(acc)
        low_acc[...] = jnp.zeros_like(low_acc)

    out, logs = pair_forward(
        query[...], (mine[0], other[0]), (mine[1], other[1]), causal_limit(where[0])
    )
    out = out.astype(BF)
    mixed[...] = out
    logsum[0, 0:1, :] = logs[0]
    logsum[0, 1:2, :] = logs[1]
    acc[...] += mm_nt(out, matrix(weight))
    low_acc[...] += mm_nt(out, low_in[0])

    @at_last()
    def _():
        rank_rows = low_acc[...].astype(BF)
        low[...] = rank_rows
        branch[...] = (acc[...] + mm(rank_rows, low_out[0])).astype(BF)


def cross_kernel(
    count,
    hidden, branch_mine, branch_other, gains, query_weight, query_in, query_out, mine, other,
    weight, low_in, low_out,
    middle, normed, query, query_low, mixed, saved, branch, low, acc, low_acc,
):
    @at_first()
    def _():
        acc[...] = jnp.zeros_like(acc)
        low_acc[...] = jnp.zeros_like(low_acc)
        total = hidden[...].astype(F32) + (
            branch_mine[...].astype(F32) + branch_other[...].astype(F32)
        )
        middle[...] = total
        rows = normalize(total, gains[1:2, :]).astype(BF)
        normed[...] = rows
        query_low[...] = mm_nt(rows, query_in[0]).astype(BF)

    queries = (
        mm(normed[...], matrix(query_weight)) + mm(query_low[...], query_out[0])
    ).astype(BF)
    query[...] = queries
    out, _ = pair_forward(
        queries,
        (mine[0, :count], other[0, :count]),
        (mine[1, :count], other[1, :count]),
        no_limit,
        saved,
    )
    out = out.astype(BF)
    mixed[...] = out
    acc[...] += mm_nt(out, matrix(weight))
    low_acc[...] += mm_nt(out, low_in[0])

    @at_last()
    def _():
        rank_rows = low_acc[...].astype(BF)
        low[...] = rank_rows
        branch[...] = (acc[...] + mm(rank_rows, low_out[0])).astype(BF)


def units_kernel(
    middle, branch_mine, branch_other, gains, cotangent, up, down, up_in, up_out, down_in,
    down_out,
    second, branch, grad_normed, table_up_in, table_up_out, table_down_in, table_down_out,
    normed, up_low, down_back, acc, back, low_acc, back_low,
):
    @at_first()
    def _():
        total = middle[...] + (branch_mine[...].astype(F32) + branch_other[...].astype(F32))
        second[...] = total
        rows = normalize(total, gains[2:3, :]).astype(BF)
        normed[...] = rows
        up_low[...] = mm_nt(rows, up_in[...]).astype(BF)
        down_back[...] = mm_nt(cotangent[...], down_out[...]).astype(BF)
        acc[...] = jnp.zeros_like(acc)
        back[...] = jnp.zeros_like(back)
        low_acc[...] = jnp.zeros_like(low_acc)
        back_low[...] = jnp.zeros_like(back_low)

    up_rows, down_rows = matrix(up), matrix(down)
    value = mm(normed[...], up_rows) + mm(up_low[...], up_out[...])
    spread = 1.0 + lax.erf(value * 0.7071067811865476)
    act = (0.5 * value * spread).astype(BF)
    slope = 0.5 * spread + value * (0.3989422804014327 * jnp.exp(-0.5 * value * value))
    acc[...] += mm_nt(act, down_rows)
    low_acc[...] += mm_nt(act, down_in[...])
    grad_act = mm(cotangent[...], down_rows) + mm(down_back[...], down_in[...])
    grad = (grad_act * slope).astype(BF)
    back[...] += mm_nt(grad, up_rows)
    back_low[...] += mm_nt(grad, up_out[...])
    table_up_out[...] = mm_tn(up_low[...], grad)
    table_down_in[...] = mm_tn(down_back[...], act)

    @at_last()
    def _():
        down_low = low_acc[...].astype(BF)
        branch[...] = (acc[...] + mm(down_low, down_out[...])).astype(BF)
        up_back = back_low[...].astype(BF)
        grad_normed[...] = (back[...] + mm(up_back, up_in[...])).astype(BF)
        table_up_in[...] = mm_tn(up_back, normed[...])
        table_down_out[...] = mm_tn(down_low, cotangent[...])


def attention_back(
    limit, slot, count, stored, carried, rows, gains, grad_mine, grad_other, weight, low_in, low_out,
    query_weight, query_in, query_out, query, mixed, mine, other, logsum, normed, query_low, low,
    carry, grad_normed, grad_kv, grad_kv_other,
    table_in, table_out, table_query_in, table_query_out,
    narrow, back_low, acc, query_back,
):
    @at_first()
    def _():
        total = carried[...].astype(F32) + normalize_back(
            rows[...],
            gains[slot : slot + 1, :],
            grad_mine[...].astype(F32) + grad_other[...].astype(F32),
        )
        carry[...] = total
        narrow[...] = total.astype(BF)
        back_low[...] = mm_nt(narrow[...], low_out[0]).astype(BF)
        acc[...] = jnp.zeros_like(acc)
        query_back[...] = jnp.zeros_like(query_back)
        table_out[...] = mm_tn(low[...], narrow[...])

    grad = (mm(narrow[...], matrix(weight)) + mm(back_low[...], low_in[0])).astype(BF)
    table_in[...] = mm_tn(back_low[...], mixed[...])
    grad_query, grad_keys, grad_values = pair_backward(
        grad,
        mixed[...],
        query[...],
        (mine[0, :count], other[0, :count]),
        (mine[1, :count], other[1, :count]),
        (None, None) if stored else (logsum[0, 0:1, :], logsum[0, 1:2, :]),
        limit,
        logsum if stored else None,
    )
    for which, (first, second) in enumerate((grad_keys, grad_values)):
        grad_kv[which, :count] = first
        grad_kv_other[which, :count] = second
        spare = grad_kv.shape[1] - count
        if spare:
            grad_kv[which, count:] = jnp.zeros((spare, PAIR), BF)
            grad_kv_other[which, count:] = jnp.zeros((spare, PAIR), BF)
    acc[...] += mm_nt(grad_query, matrix(query_weight))
    query_back[...] += mm_nt(grad_query, query_out[0])
    table_query_out[...] = mm_tn(query_low[0], grad_query)

    @at_last()
    def _():
        rank_rows = query_back[...].astype(BF)
        total = acc[...] + mm(rank_rows, query_in[0])
        grad_normed[...] = total.astype(grad_normed.dtype)
        table_query_in[...] = mm_tn(rank_rows, normed[...])


def self_back_kernel(count, where, *refs):
    attention_back(causal_limit(where[0]), 1, count, False, *refs)


def pair_project_kernel(
    grad_mine, grad_other, weight, low_in, low_out, rows, low, start, total, table_in, table_out,
    acc,
):
    @at_first()
    def _():
        acc[...] = start[...]

    pair_project_step(
        grad_mine, grad_other, weight, low_in, low_out, rows, low, table_in, table_out, acc
    )

    @at_last()
    def _():
        total[...] = acc[...].astype(BF)


def close_kernel(hidden, gains, carried, grad_mine, grad_other, total):
    total[...] = carried[...] + normalize_back(
        hidden[...].astype(F32),
        gains[0:1, :],
        grad_mine[...].astype(F32) + grad_other[...].astype(F32),
    )


def add_rows_kernel(mine, other, *refs):
    total = refs[-1]
    value = mine[...].astype(F32) + other[...].astype(F32)
    total[...] = value[:, None, :]


def frames_back_kernel(
    grad_mine, grad_other, weight, low_in, low_out, rows, low, top, rest, table_in, table_out, acc
):
    @at_first()
    def _():
        acc[...] = jnp.zeros_like(acc)

    pair_project_step(
        grad_mine, grad_other, weight, low_in, low_out, rows, low, table_in, table_out, acc
    )

    @at_last()
    def _():
        count = top.shape[0]
        top[...] = acc[:count].astype(BF)
        rest[...] = acc[count:].astype(BF)


def pair_project_step(
    grad_mine, grad_other, weight, low_in, low_out, rows, low, table_in, table_out, acc
):
    count = rows.shape[0]
    grad = (grad_mine[0, :count].astype(F32) + grad_other[0, :count].astype(F32)).astype(BF)
    rank_rows = mm_nt(grad, low_out[0]).astype(BF)
    acc[...] += mm_nt(grad, matrix(weight)) + mm(rank_rows, low_in[0])
    table_in[0] = mm_tn(rank_rows, rows[...])
    table_out[0] = mm_tn(low[0], grad)


LANE = 128
PIECE = 32


def pack_kernel(fulls, shares, order, tagged, *refs):
    where = refs[0]
    keep, send = refs[-2:]
    flat = []
    for ref in refs[1:-2]:
        flat += [ref] if len(ref.shape) == 2 else [ref.at[i] for i in range(ref.shape[0])]
    tables, broad = flat[: fulls + shares], flat[fulls + shares :]
    context, tensor = where[0], where[1]
    blocks = keep.shape[1]
    per_group = (len(order) + 3) // 4
    rows = per_group * 16
    lane = lax.broadcasted_iota(jnp.int32, (rows, LANE), 1) // PIECE
    padded = list(order) + [None] * (4 * per_group - len(order))

    def one_block(f, carry):
        shard = f // (blocks // 2)
        local = f - shard * (blocks // 2)
        owned = tensor == shard

        def table_of(k):
            if k is None:
                return jnp.zeros((16, LANE), F32)
            if k < fulls:
                return tables[k][:, pl.ds(pl.multiple_of(f * LANE, LANE), LANE)]
            part = tables[k][:, pl.ds(pl.multiple_of(local * LANE, LANE), LANE)]
            return jnp.where(owned, part, 0.0)

        groups = [
            jnp.concatenate(
                [table_of(k) for k in padded[g * per_group : (g + 1) * per_group]], axis=0
            )
            for g in range(4)
        ]
        for target, side in ((keep, context), (send, 1 - context)):
            for t in range(2):
                p = 2 * side + t
                value = jnp.zeros((rows, LANE), F32)
                for g in range(4):
                    turned = pltpu.roll(groups[g], (PIECE * (g + 4 - p)) % LANE, 1)
                    value = jnp.where(lane == g, turned, value)
                target[t, f, :rows] = value
                row = rows
                for w in broad:
                    at = pl.multiple_of(local * 4 * LANE + p * LANE, LANE)
                    target[t, f, row : row + 16] = jnp.where(owned, w[:, pl.ds(at, LANE)], 0.0)
                    row += 16
                if tagged:
                    tag = where[2].astype(F32) * 0.25
                    target[t, f, row : row + 16] = jnp.full((16, LANE), 1.0, F32) * tag
        return carry

    lax.fori_loop(0, blocks, one_block, 0)


def unpack_kernel(parts, attn_in, attn_out, up_in, up_out, down_in, down_out):
    projections, adapters = attn_in.shape[:2]
    clips, rows = parts.shape[:2]
    per_group = (2 * projections + 2 + 3) // 4
    narrow = 16 * per_group

    def one(a, carry):
        adapter = a.astype(F32)
        block = jnp.zeros((rows - 16, LANE), F32)
        for c in range(clips):
            tag = parts[c, rows - 16 : rows - 15, :].astype(F32)
            same = (tag > adapter - 0.5) & (tag < adapter + 0.5)
            block = block + jnp.where(same, parts[c, : rows - 16].astype(F32), 0.0)

        def piece(k):
            g, at = k // per_group, 16 * (k % per_group)
            return block[at : at + 16, PIECE * g : PIECE * (g + 1)]

        for j in range(projections):
            attn_in[j, a] = piece(j)
            attn_out[j, a] = piece(projections + j)
        up_in[a] = piece(2 * projections)
        down_out[a] = piece(2 * projections + 1)
        up_out[a] = block[narrow : narrow + 16]
        down_in[a] = block[narrow + 16 : narrow + 32]
        return carry

    lax.fori_loop(0, adapters, one, 0)


def shape(dims, dtype):
    return jax.ShapeDtypeStruct(tuple(dims), dtype)


def fixed(array):
    zeros = (0,) * array.ndim
    return pl.BlockSpec(array.shape, lambda *_: zeros)


def fixed_out(*dims):
    zeros = (0,) * len(dims)
    return pl.BlockSpec(dims, lambda *_: zeros)


def call(kernel, steps, ins, outs, scratch=(), scalars=None, name=None, cost=5, aliases=None):
    arrays = [a for a, _ in ins]
    spec = pltpu.PrefetchScalarGridSpec(
        num_scalar_prefetch=0 if scalars is None else 1,
        grid=(steps,),
        in_specs=[s for _, s in ins],
        out_specs=[s for _, s in outs],
        scratch_shapes=list(scratch),
    )
    run = pl.pallas_call(
        kernel,
        grid_spec=spec,
        out_shape=[o for o, _ in outs],
        compiler_params=pltpu.CompilerParams(dimension_semantics=("arbitrary",)),
        cost_estimate=pl.CostEstimate(
            flops=cost * 10_000_000, transcendentals=0, bytes_accessed=cost * 36_900
        ),
        input_output_aliases=aliases or {},
        name=name,
    )
    return run(*arrays) if scalars is None else run(scalars, *arrays)


def on_device(
    hidden,
    encoder,
    cotangent,
    adapter_index,
    ln_gains,
    attn_in_weight,
    attn_out_weight,
    up_weight,
    down_weight,
    attn_adapt_in,
    attn_adapt_out,
    up_adapt_in,
    up_adapt_out,
    down_adapt_in,
    down_adapt_out,
):
    fsdp_size = lax.axis_size("fsdp")
    ctx_size = lax.axis_size("ctx")
    tp_size = lax.axis_size("tp")
    tensor_index = lax.axis_index("tp")
    context_index = lax.axis_index("ctx")
    hidden, encoder, cotangent = hidden[0], encoder[0], cotangent[0]
    rows, width = hidden.shape
    frames = encoder.shape[0]
    padded = -(-frames // 16) * 16
    wide = up_adapt_out.shape[2]
    cols = attn_in_weight.shape[2]
    units = up_weight.shape[1]
    rank = attn_adapt_in.shape[2]
    adapters = attn_adapt_in.shape[1]
    pairs = cols // PAIR
    head_start = tensor_index * cols
    unit_start = tensor_index * units
    mine = adapter_index[0]
    scalars = jnp.stack(
        [context_index.astype(jnp.int32), tensor_index.astype(jnp.int32), mine]
    )

    half_rows = attn_in_weight.shape[1] // ctx_size
    shards = fsdp_size * ctx_size

    def my_half(table):
        return lax.dynamic_slice_in_dim(
            table, context_index * half_rows, half_rows, axis=table.ndim - 2
        )

    attn_half = jnp.concatenate([my_half(attn_in_weight), my_half(attn_out_weight)], axis=0)
    ff_half = jnp.stack([my_half(up_weight), my_half(down_weight)])
    attn_full = lax.all_gather(attn_half, ("fsdp", "ctx"), axis=0)
    ff_full = lax.all_gather(ff_half, ("fsdp", "ctx"), axis=0)

    sel_in = lax.dynamic_index_in_dim(attn_adapt_in, mine, 1, keepdims=False)
    sel_out = lax.dynamic_index_in_dim(attn_adapt_out, mine, 1, keepdims=False)
    part_in = lax.dynamic_slice_in_dim(sel_in, head_start, cols, 2)
    part_out = lax.dynamic_slice_in_dim(sel_out, head_start, cols, 2)
    up_in = lax.dynamic_index_in_dim(up_adapt_in, mine, 0, keepdims=False)
    up_out = lax.dynamic_slice(up_adapt_out, (mine, 0, unit_start), (1, rank, units))[0]
    down_in = lax.dynamic_slice(down_adapt_in, (mine, 0, unit_start), (1, rank, units))[0]
    down_out = lax.dynamic_index_in_dim(down_adapt_out, mine, 0, keepdims=False)

    def weight_cols(slot):
        return attn_full, pl.BlockSpec((shards, 1, half_rows, cols), lambda i, *_: (0, slot(i), 0, 0))

    def weight_pair(slot):
        return attn_full, pl.BlockSpec((shards, 1, half_rows, PAIR), lambda p, *_: (0, slot, 0, p))

    def slot_of(table, slot):
        return table, pl.BlockSpec((1,) + table.shape[1:], lambda i, *_: (slot(i), 0, 0))

    def slot_pair(table, slot):
        return table, pl.BlockSpec((1, rank, PAIR), lambda p, *_: (slot, 0, p))

    def whole(array):
        return array, fixed(array)

    def out(dims, dtype):
        return shape(dims, dtype), fixed_out(*dims)

    def by_pair(count, dtype=BF):
        return shape((count, cols), dtype), pl.BlockSpec((count, PAIR), lambda p, *_: (0, p))

    def kv_pair(array):
        return array, pl.BlockSpec((2, array.shape[1], PAIR), lambda p, *_: (0, 0, p))

    def at(array, first=0):
        return array, pl.BlockSpec((1,) + array.shape[1:], lambda i, *_: (first + i, 0, 0))

    def at_slot(array):
        return array, pl.BlockSpec((1,) + array.shape[1:], lambda i, *_: (0, 0, 0))

    logsum_out = (
        shape((pairs, 2, rows), F32),
        pl.BlockSpec((1, 2, rows), lambda p, *_: (p, 0, 0)),
    )

    def logsum_in(array):
        rest = (0,) * (array.ndim - 1)
        return array, pl.BlockSpec((1,) + array.shape[1:], lambda p, *_: (p, *rest))

    saved_shape = shape((pairs, 2, 2, padded, rows), BF)

    def pair_in(array):
        return array, pl.BlockSpec((array.shape[0], PAIR), lambda p, *_: (0, p))

    regular = (
        ctx_size == 2 and tp_size == 2 and rank == 16
        and width == LANE * fsdp_size and wide == 4 * LANE * fsdp_size
    )

    def ordered(first, *others):
        return lax.optimization_barrier((first, *others))

    def pack(full, part, wides, order, tagged, name):
        count = 16 * ((len(order) + 3) // 4 + len(wides) + tagged)
        dims = (2, fsdp_size, count, LANE)

        def number(arrays):
            return sum(1 if a.ndim == 2 else a.shape[0] for a in arrays)

        keep, send = call(
            partial(pack_kernel, number(full), number(part), order, tagged),
            1,
            [whole(a) for a in full + part + wides],
            [out(dims, F32), out(dims, F32)],
            scalars=scalars,
            name=name,
        )
        recv = swap(send, "ctx")

        def pick(i):
            return lax.dynamic_index_in_dim(keep, i, 0, keepdims=False) + (
                lax.dynamic_index_in_dim(recv, i, 0, keepdims=False)
            )

        return pick(tensor_index), pick(1 - tensor_index).astype(BF)

    def finish(kept, away):
        return lax.all_to_all((kept + away.astype(F32)).astype(BF), "fsdp", 0, 0, tiled=True)

    wide_acc = pltpu.VMEM((rows, width), F32)
    rank_acc = pltpu.VMEM((rows, rank), F32)
    rank_keep = pltpu.VMEM((rows, rank), BF)

    n1, query, self_kv, self_low = call(
        qkv_kernel,
        3,
        [
            whole(hidden),
            whole(ln_gains),
            weight_cols(lambda i: i),
            slot_of(sel_in, lambda i: i),
            slot_of(part_out, lambda i: i),
        ],
        [
            out((rows, width), BF),
            out((rows, cols), BF),
            (
                shape((2, rows, cols), BF),
                pl.BlockSpec((1, rows, cols), lambda i: (jnp.maximum(i - 1, 0), 0, 0)),
            ),
            (shape((3, rows, rank), BF), pl.BlockSpec((1, rows, rank), lambda i: (i, 0, 0))),
        ],
        name="qkv",
    )
    self_kv_other = swap(self_kv, "ctx")
    cross_kv, frames_low = call(
        frames_kernel,
        2,
        [
            whole(encoder),
            weight_cols(lambda i: 4 + i),
            slot_of(sel_in, lambda i: 5 + i),
            slot_of(part_out, lambda i: 5 + i),
        ],
        [
            (
                shape((2, padded, cols), BF),
                pl.BlockSpec((1, padded, cols), lambda i: (i, 0, 0)),
            ),
            (
                shape((2, frames, rank), BF),
                pl.BlockSpec((1, frames, rank), lambda i: (i, 0, 0)),
            ),
        ],
        name="frames",
        cost=7,
    )
    cross_kv_other = swap(cross_kv, "ctx")
    self_mixed, self_logsum, branch, self_o_low = call(
        self_kernel,
        pairs,
        [
            pair_in(query),
            kv_pair(self_kv),
            kv_pair(self_kv_other),
            weight_pair(6),
            slot_pair(part_in, 3),
            slot_of(sel_out, lambda i: 3),
        ],
        [by_pair(rows), logsum_out, out((rows, width), BF), out((rows, rank), BF)],
        [wide_acc, rank_acc],
        scalars,
        name="self_attention",
        cost=7,
    )
    branch, branch_other = with_other(branch, "tp")
    first_mid, n2, cross_q, cross_q_low, cross_mixed, cross_logsum, branch, cross_o_low = call(
        partial(cross_kernel, frames),
        pairs,
        [
            whole(hidden),
            whole(branch),
            whole(branch_other),
            whole(ln_gains),
            weight_pair(3),
            slot_of(sel_in, lambda i: 4),
            slot_pair(part_out, 4),
            kv_pair(cross_kv),
            kv_pair(cross_kv_other),
            weight_pair(7),
            slot_pair(part_in, 7),
            slot_of(sel_out, lambda i: 7),
        ],
        [
            out((rows, width), F32),
            out((rows, width), BF),
            by_pair(rows),
            out((rows, rank), BF),
            by_pair(rows),
            logsum_in(saved_shape),
            out((rows, width), BF),
            out((rows, rank), BF),
        ],
        [wide_acc, rank_acc],
        name="cross_attention",
        cost=13,
    )
    branch, branch_other = with_other(branch, "tp")
    chunk = min(units, 512)

    def unit_weight(slot):
        return ff_full, pl.BlockSpec((shards, 1, half_rows, chunk), lambda i: (0, slot, 0, i))

    def unit_cols(array):
        return array, pl.BlockSpec((rank, chunk), lambda i: (0, i))

    second_mid, branch, grad_n3, up_in_t, up_out_t, down_in_t, down_out_t = call(
        units_kernel,
        units // chunk,
        [
            whole(first_mid),
            whole(branch),
            whole(branch_other),
            whole(ln_gains),
            whole(cotangent),
            unit_weight(0),
            unit_weight(1),
            whole(up_in),
            unit_cols(up_out),
            unit_cols(down_in),
            whole(down_out),
        ],
        [
            out((rows, width), F32),
            out((rows, width), BF),
            out((rows, width), BF),
            out((rank, width), F32),
            unit_cols(shape((rank, units), F32)),
            unit_cols(shape((rank, units), F32)),
            out((rank, width), F32),
        ],
        [
            pltpu.VMEM((rows, width), BF),
            rank_keep,
            rank_keep,
            wide_acc,
            wide_acc,
            rank_acc,
            rank_acc,
        ],
        name="units",
        cost=11,
    )
    grad_n3, grad_n3_other = with_other(grad_n3, "tp")
    branch, grad_n3_other = ordered(branch, grad_n3_other)
    branch, branch_other = with_other(branch, "tp")

    def back_call(
        kernel, scalar, carried, middle, grad, grad_other, slots, queries, mixed, kv, kv_other,
        logsum, normed, query_low, low, kind, name, cost,
    ):
        weight_slot, low_slot, query_slot, query_low_slot = slots
        count = kv.shape[1]
        kv_out = (
            shape((2, count, cols), BF),
            pl.BlockSpec((2, count, PAIR), lambda p, *_: (0, 0, p)),
        )
        return call(
            kernel,
            pairs,
            [
                whole(carried),
                whole(middle),
                whole(ln_gains),
                whole(grad),
                whole(grad_other),
                weight_pair(weight_slot),
                slot_pair(part_in, low_slot),
                slot_of(sel_out, lambda i: low_slot),
                weight_pair(query_slot),
                slot_of(sel_in, lambda i: query_low_slot),
                slot_pair(part_out, query_low_slot),
                pair_in(queries),
                pair_in(mixed),
                kv_pair(kv),
                kv_pair(kv_other),
                logsum_in(logsum),
                whole(normed),
                at_slot(query_low),
                whole(low),
            ],
            [
                out((rows, width), F32),
                out((rows, width), kind),
                kv_out,
                kv_out,
                by_pair(rank, F32),
                out((rank, width), F32),
                out((rank, width), F32),
                by_pair(rank, F32),
            ],
            [pltpu.VMEM((rows, width), BF), rank_keep, wide_acc, rank_acc],
            scalar,
            name=name,
            cost=cost,
        )

    grad_second, grad_n2, grad_ckv, grad_ckv_send, co_in_t, co_out_t, cq_in_t, cq_out_t = back_call(
        partial(attention_back, no_limit, 2, frames, True), None, cotangent, second_mid, grad_n3, grad_n3_other, (7, 7, 3, 4),
        cross_q, cross_mixed, cross_kv, cross_kv_other, cross_logsum, n2, cross_q_low[None],
        cross_o_low, BF, "cross_back", 18,
    )
    grad_n2, grad_ckv_send, branch_other = ordered(grad_n2, grad_ckv_send, branch_other)
    grad_n2, grad_n2_other = with_other(grad_n2, "tp")
    grad_ckv_other = swap(grad_ckv_send, "ctx")
    layer_out = (
        second_mid + (branch.astype(F32) + branch_other.astype(F32))
    ).astype(BF)
    block_rows = 128
    first_rows = (frames * 3 // 4) // block_rows * block_rows
    grad_top, grad_low, ckv_in_t, ckv_out_t = call(
        frames_back_kernel,
        2,
        [
            at(grad_ckv),
            at(grad_ckv_other),
            weight_cols(lambda i: 4 + i),
            slot_of(sel_in, lambda i: 5 + i),
            slot_of(part_out, lambda i: 5 + i),
            whole(encoder),
            at(frames_low),
        ],
        [
            out((first_rows, width), BF),
            out((frames - first_rows, width), BF),
            at(shape((2, rank, width), F32)),
            at(shape((2, rank, cols), F32)),
        ],
        [pltpu.VMEM((frames, width), F32)],
        name="frames_back",
        cost=9,
    )
    grad_top, grad_low, grad_n2_other = lax.optimization_barrier(
        (grad_top, grad_low, grad_n2_other)
    )
    grad_top, grad_top_other = with_other(grad_top, "tp")
    grad_first, grad_n1_start, grad_skv, grad_skv_send, so_in_t, so_out_t, q_in_t, q_out_t = back_call(
        partial(self_back_kernel, rows), scalars, grad_second, first_mid, grad_n2, grad_n2_other, (6, 3, 0, 0),
        query, self_mixed, self_kv, self_kv_other, self_logsum, n1, self_low,
        self_o_low, F32, "self_back", 12,
    )
    grad_skv_other = swap(grad_skv_send, "ctx")
    grad_n1, kv_in_t, kv_out_t = call(
        pair_project_kernel,
        2,
        [
            at(grad_skv),
            at(grad_skv_other),
            weight_cols(lambda i: 1 + i),
            slot_of(sel_in, lambda i: 1 + i),
            slot_of(part_out, lambda i: 1 + i),
            whole(n1),
            at(self_low, 1),
            whole(grad_n1_start),
        ],
        [
            out((rows, width), BF),
            at(shape((2, rank, width), F32)),
            at(shape((2, rank, cols), F32)),
        ],
        [wide_acc],
        name="self_project_back",
    )
    grad_n1, grad_n1_other = with_other(grad_n1, "tp")
    full = [q_in_t, kv_in_t, cq_in_t, ckv_in_t, so_out_t, co_out_t, up_in_t, down_out_t]
    part = [so_in_t, co_in_t, q_out_t, kv_out_t, cq_out_t, ckv_out_t]
    if regular:
        order = (0, 1, 2, 10, 3, 4, 5, 11, 12, 13, 14, 6, 15, 16, 17, 7, 8, 9)
        full[0], layer_out, grad_top_other = ordered(q_in_t, layer_out, grad_top_other)
        kept, away = pack(full, part, [up_out_t, down_in_t], order, 1, "pack")
        away, grad_low = ordered(swap(away, "tp"), grad_low)
        parts = finish(kept, away)
        narrow_out = (attn_adapt_in.shape[0], adapters, rank, PIECE)
        tables = call(
            unpack_kernel,
            1,
            [whole(parts)],
            [
                out(narrow_out, F32),
                out(narrow_out, F32),
                out((adapters, rank, PIECE), F32),
                out((adapters, rank, LANE), F32),
                out((adapters, rank, LANE), F32),
                out((adapters, rank, PIECE), F32),
            ],
            name="unpack",
        )
    else:
        chosen = (mine == jnp.arange(adapters, dtype=jnp.int32)).astype(F32)

        def summed(parts, start, full):
            parts = [t for p in parts for t in ([p] if p.ndim == 2 else [p[0], p[1]])]

            def spread_out(part):
                if part.shape[1] == full:
                    return part
                blank = jnp.zeros((part.shape[0], full), F32)
                return lax.dynamic_update_slice_in_dim(blank, part, start, axis=1)

            stacked = jnp.stack([spread_out(p) for p in parts])
            table = chosen[None, :, None, None] * stacked[:, None]
            return lax.psum_scatter(
                table, ("fsdp", "ctx", "tp"), scatter_dimension=3, tiled=True
            )

        attn_in_t = summed(
            [q_in_t, kv_in_t, so_in_t, cq_in_t, ckv_in_t, co_in_t], head_start, width
        )
        attn_out_t = summed(
            [q_out_t, kv_out_t, so_out_t, cq_out_t, ckv_out_t, co_out_t], head_start, width
        )
        small = summed([up_in_t, down_out_t], head_start, width)
        large = summed([up_out_t, down_in_t], unit_start, wide)
        tables = (attn_in_t, attn_out_t, small[0], large[0], large[1], small[1])
    grad_low, grad_low_other = with_other(grad_low, "tp")
    def row_blocks(array, first=0):
        block = (block_rows,) + array.shape[1:]
        rest = (0,) * (array.ndim - 1)
        return array, pl.BlockSpec(block, lambda i: (first + i, *rest))

    total_shape = shape((frames, 1, width), F32)
    steps = first_rows // block_rows
    (grad_encoder,) = call(
        add_rows_kernel,
        steps,
        [row_blocks(grad_top), row_blocks(grad_top_other)],
        [row_blocks(total_shape)],
        name="encoder_top",
    )
    (grad_encoder,) = call(
        add_rows_kernel,
        -(-(frames - first_rows) // block_rows),
        [
            row_blocks(grad_low),
            row_blocks(grad_low_other),
            (grad_encoder, pl.BlockSpec(memory_space=pl.ANY)),
        ],
        [row_blocks(total_shape, steps)],
        aliases={2: 0},
        name="encoder_low",
    )
    grad_encoder = grad_encoder.reshape(frames, width)
    (grad_hidden,) = call(
        close_kernel,
        1,
        [whole(a) for a in (hidden, ln_gains, grad_first, grad_n1, grad_n1_other)],
        [out((rows, width), F32)],
        name="hidden_total",
    )
    return (
        layer_out[None],
        grad_hidden[None],
        grad_encoder[None],
        *tables,
    )
def solution(mesh):
    in_specs = (
        P("fsdp", "ctx", None),
        P("fsdp", "ctx", None),
        P("fsdp", "ctx", None),
        P("fsdp"),
        P(),
        P(None, "fsdp", "tp"),
        P(None, "fsdp", "tp"),
        P("fsdp", "tp"),
        P("fsdp", "tp"),
        P(),
        P(),
        P(),
        P(),
        P(),
        P(),
    )
    out_specs = (
        P("fsdp", "ctx", None),
        P("fsdp", "ctx", None),
        P("fsdp", "ctx", None),
        P(None, None, None, ("fsdp", "ctx", "tp")),
        P(None, None, None, ("fsdp", "ctx", "tp")),
        P(None, None, ("fsdp", "ctx", "tp")),
        P(None, None, ("fsdp", "ctx", "tp")),
        P(None, None, ("fsdp", "ctx", "tp")),
        P(None, None, ("fsdp", "ctx", "tp")),
    )
    return jax.shard_map(
        on_device, mesh=mesh, in_specs=in_specs, out_specs=out_specs, check_vma=False
    )
```

```python
from functools import partial

import jax
import jax.numpy as jnp
from jax import lax
from jax.experimental import pallas as pl
from jax.experimental.pallas import tpu as pltpu
from jax.sharding import PartitionSpec as P

HEAD_DIM = 64
PAIR = 2 * HEAD_DIM
EPSILON = 1e-05
MASKED_SCORE = -1000000000.0
SCALE = HEAD_DIM ** (-0.5)
BF = jnp.bfloat16
F32 = jnp.float32


def mm(a, b):
    return lax.dot_general(a, b, (((1,), (0,)), ((), ())), preferred_element_type=F32)


def mm_nt(a, b):
    return lax.dot_general(a, b, (((1,), (1,)), ((), ())), preferred_element_type=F32)


def mm_tn(a, b):
    return lax.dot_general(a, b, (((0,), (0,)), ((), ())), preferred_element_type=F32)


def norm_parts(rows):
    centred = rows - jnp.mean(rows, axis=-1, keepdims=True)
    spread = jnp.mean(centred * centred, axis=-1, keepdims=True)
    inverse = lax.rsqrt(spread + EPSILON)
    return centred * inverse, inverse


def normalize(rows, gain):
    return norm_parts(rows)[0] * gain


def normalize_back(rows, gain, gradient):
    unit, inverse = norm_parts(rows)
    scaled = gradient * gain
    first = jnp.mean(scaled, axis=-1, keepdims=True)
    second = jnp.mean(scaled * unit, axis=-1, keepdims=True)
    return (scaled - first - unit * second) * inverse


def swap(value, axis):
    return lax.ppermute(value, axis, [(0, 1), (1, 0)])


def with_other(partial_value, axis):
    if lax.axis_size(axis) == 2:
        return partial_value, swap(partial_value, axis)
    return lax.psum(partial_value, axis), jnp.zeros_like(partial_value)


def matrix(ref):
    block = ref[...]
    return block.reshape(block.shape[0] * block.shape[2], block.shape[3])


def half_masks(rows):
    lane = lax.broadcasted_iota(jnp.int32, (rows, PAIR), 1)
    return lane < HEAD_DIM, lane >= HEAD_DIM


def pick_half(rows, keep):
    return jnp.where(keep, rows, jnp.zeros_like(rows))


def join_halves(first, second):
    row = lax.broadcasted_iota(jnp.int32, first.shape, 0)
    return jnp.where(row < HEAD_DIM, first, second).T


def pair_forward(queries, keys, values, limit, saved=None):
    mixed, logsums = [], []
    turned = [v.T for v in values]
    for half, keep in enumerate(half_masks(queries.shape[0])):
        mine = pick_half(queries, keep) * BF(SCALE)
        scores = [limit(i, mm_nt(k, mine)) for i, k in enumerate(keys)]
        top = jnp.max(scores[0], axis=0, keepdims=True)
        for s in scores[1:]:
            top = jnp.maximum(top, jnp.max(s, axis=0, keepdims=True))
        powers = [jnp.exp(s - top) for s in scores]
        total = sum(jnp.sum(e, axis=0, keepdims=True) for e in powers)
        share = 1.0 / total
        weights = [(e * share).astype(BF) for e in powers]
        if saved is not None:
            for i, w in enumerate(weights):
                saved[0, half, i, : w.shape[0]] = w
        mixed.append(sum(mm(v, w) for v, w in zip(turned, weights)))
        logsums.append(top + jnp.log(total))
    return join_halves(*mixed), logsums


def pair_backward(grad, mixed, queries, keys, values, logsums, limit, saved=None):
    grad_query, grad_keys, grad_values = [], [0.0] * len(keys), [0.0] * len(keys)
    inners = (grad.astype(F32) * mixed.astype(F32)).T
    turned = [k.T for k in keys]
    for half, (keep, logsum) in enumerate(zip(half_masks(queries.shape[0]), logsums)):
        mine = pick_half(queries, keep) * BF(SCALE)
        grad_mine = pick_half(grad, keep)
        at = HEAD_DIM * half
        inner = jnp.sum(inners[at : at + HEAD_DIM], axis=0, keepdims=True)
        part = 0.0
        for i, (key, value) in enumerate(zip(keys, values)):
            if saved is None:
                weights = jnp.exp(limit(i, mm_nt(key, mine)) - logsum)
                rounded = weights.astype(BF)
            else:
                rounded = saved[0, half, i, : key.shape[0]]
                weights = rounded.astype(F32)
            grad_scores = (weights * (mm_nt(value, grad_mine) - inner)).astype(BF)
            part = part + mm(turned[i], grad_scores)
            grad_keys[i] = grad_keys[i] + mm(grad_scores, mine)
            grad_values[i] = grad_values[i] + mm(rounded, grad_mine)
        grad_query.append(part)
    return (
        (join_halves(*grad_query) * SCALE).astype(BF),
        [g.astype(BF) for g in grad_keys],
        [g.astype(BF) for g in grad_values],
    )


def no_limit(index, scores):
    return scores


def causal_limit(context):
    def limit(index, scores):
        if index == 0:
            key = lax.broadcasted_iota(jnp.int32, scores.shape, 0)
            query = lax.broadcasted_iota(jnp.int32, scores.shape, 1)
            return jnp.where(key <= query, scores, MASKED_SCORE)
        return jnp.where(context == 1, scores, MASKED_SCORE)

    return limit


def at_first(step=0):
    return pl.when(pl.program_id(0) == step)


def at_last():
    return pl.when(pl.program_id(0) == pl.num_programs(0) - 1)


def qkv_kernel(hidden, gains, weight, low_in, low_out, normed, query, key_value, low):
    @at_first()
    def _():
        normed[...] = normalize(hidden[...].astype(F32), gains[0:1, :]).astype(BF)

    rows = normed[...]
    rank_rows = mm_nt(rows, low_in[0]).astype(BF)
    low[0] = rank_rows
    value = (mm(rows, matrix(weight)) + mm(rank_rows, low_out[0])).astype(BF)

    @at_first()
    def _():
        query[...] = value

    @pl.when(pl.program_id(0) > 0)
    def _():
        key_value[0] = value


def frames_kernel(frames, weight, low_in, low_out, key_value, low):
    rows = frames[...]
    rank_rows = mm_nt(rows, low_in[0]).astype(BF)
    low[0] = rank_rows
    count = rows.shape[0]
    key_value[0, :count] = (mm(rows, matrix(weight)) + mm(rank_rows, low_out[0])).astype(BF)
    spare = key_value.shape[1] - count
    if spare:
        key_value[0, count:] = jnp.zeros((spare, key_value.shape[2]), BF)


def self_kernel(
    where, query, mine, other, weight, low_in, low_out, mixed, logsum, branch, low, acc, low_acc
):
    @at_first()
    def _():
        acc[...] = jnp.zeros_like(acc)
        low_acc[...] = jnp.zeros_like(low_acc)

    out, logs = pair_forward(
        query[...], (mine[0], other[0]), (mine[1], other[1]), causal_limit(where[0])
    )
    out = out.astype(BF)
    mixed[...] = out
    logsum[0, 0:1, :] = logs[0]
    logsum[0, 1:2, :] = logs[1]
    acc[...] += mm_nt(out, matrix(weight))
    low_acc[...] += mm_nt(out, low_in[0])

    @at_last()
    def _():
        rank_rows = low_acc[...].astype(BF)
        low[...] = rank_rows
        branch[...] = (acc[...] + mm(rank_rows, low_out[0])).astype(BF)


def cross_kernel(
    count,
    hidden, branch_mine, branch_other, gains, query_weight, query_in, query_out, mine, other,
    weight, low_in, low_out,
    middle, normed, query, query_low, mixed, saved, branch, low, acc, low_acc,
):
    @at_first()
    def _():
        acc[...] = jnp.zeros_like(acc)
        low_acc[...] = jnp.zeros_like(low_acc)
        total = hidden[...].astype(F32) + (
            branch_mine[...].astype(F32) + branch_other[...].astype(F32)
        )
        middle[...] = total
        rows = normalize(total, gains[1:2, :]).astype(BF)
        normed[...] = rows
        query_low[...] = mm_nt(rows, query_in[0]).astype(BF)

    queries = (
        mm(normed[...], matrix(query_weight)) + mm(query_low[...], query_out[0])
    ).astype(BF)
    query[...] = queries
    out, _ = pair_forward(
        queries,
        (mine[0, :count], other[0, :count]),
        (mine[1, :count], other[1, :count]),
        no_limit,
        saved,
    )
    out = out.astype(BF)
    mixed[...] = out
    acc[...] += mm_nt(out, matrix(weight))
    low_acc[...] += mm_nt(out, low_in[0])

    @at_last()
    def _():
        rank_rows = low_acc[...].astype(BF)
        low[...] = rank_rows
        branch[...] = (acc[...] + mm(rank_rows, low_out[0])).astype(BF)


def third_norm_kernel(
    middle, branch_mine, branch_other, gains, cotangent, up_in, down_out,
    second, normed, up_low, down_back,
):
    total = middle[...] + (branch_mine[...].astype(F32) + branch_other[...].astype(F32))
    second[...] = total
    rows = normalize(total, gains[2:3, :]).astype(BF)
    normed[...] = rows
    up_low[...] = mm_nt(rows, up_in[...]).astype(BF)
    down_back[...] = mm_nt(cotangent[...], down_out[...]).astype(BF)


def units_kernel(
    normed, up_low, down_back, cotangent, up, down, up_in, up_out, down_in, down_out,
    branch, grad_normed, table_up_in, table_up_out, table_down_in, table_down_out,
    acc, back, low_acc, back_low,
):
    @at_first()
    def _():
        acc[...] = jnp.zeros_like(acc)
        back[...] = jnp.zeros_like(back)
        low_acc[...] = jnp.zeros_like(low_acc)
        back_low[...] = jnp.zeros_like(back_low)

    up_rows, down_rows = matrix(up), matrix(down)
    value = mm(normed[...], up_rows) + mm(up_low[...], up_out[...])
    spread = 1.0 + lax.erf(value * 0.7071067811865476)
    act = (0.5 * value * spread).astype(BF)
    slope = 0.5 * spread + value * (0.3989422804014327 * jnp.exp(-0.5 * value * value))
    acc[...] += mm_nt(act, down_rows)
    low_acc[...] += mm_nt(act, down_in[...])
    grad_act = mm(cotangent[...], down_rows) + mm(down_back[...], down_in[...])
    grad = (grad_act * slope).astype(BF)
    back[...] += mm_nt(grad, up_rows)
    back_low[...] += mm_nt(grad, up_out[...])
    table_up_out[...] = mm_tn(up_low[...], grad)
    table_down_in[...] = mm_tn(down_back[...], act)

    @at_last()
    def _():
        down_low = low_acc[...].astype(BF)
        branch[...] = (acc[...] + mm(down_low, down_out[...])).astype(BF)
        up_back = back_low[...].astype(BF)
        grad_normed[...] = (back[...] + mm(up_back, up_in[...])).astype(BF)
        table_up_in[...] = mm_tn(up_back, normed[...])
        table_down_out[...] = mm_tn(down_low, cotangent[...])


def attention_back(
    limit, slot, count, stored, carried, rows, gains, grad_mine, grad_other, weight, low_in, low_out,
    query_weight, query_in, query_out, query, mixed, mine, other, logsum, normed, query_low, low,
    carry, grad_normed, grad_kv, grad_kv_other,
    table_in, table_out, table_query_in, table_query_out,
    narrow, back_low, acc, query_back,
):
    @at_first()
    def _():
        total = carried[...].astype(F32) + normalize_back(
            rows[...],
            gains[slot : slot + 1, :],
            grad_mine[...].astype(F32) + grad_other[...].astype(F32),
        )
        carry[...] = total
        narrow[...] = total.astype(BF)
        back_low[...] = mm_nt(narrow[...], low_out[0]).astype(BF)
        acc[...] = jnp.zeros_like(acc)
        query_back[...] = jnp.zeros_like(query_back)
        table_out[...] = mm_tn(low[...], narrow[...])

    grad = (mm(narrow[...], matrix(weight)) + mm(back_low[...], low_in[0])).astype(BF)
    table_in[...] = mm_tn(back_low[...], mixed[...])
    grad_query, grad_keys, grad_values = pair_backward(
        grad,
        mixed[...],
        query[...],
        (mine[0, :count], other[0, :count]),
        (mine[1, :count], other[1, :count]),
        (None, None) if stored else (logsum[0, 0:1, :], logsum[0, 1:2, :]),
        limit,
        logsum if stored else None,
    )
    for which, (first, second) in enumerate((grad_keys, grad_values)):
        grad_kv[which, :count] = first
        grad_kv_other[which, :count] = second
        spare = grad_kv.shape[1] - count
        if spare:
            grad_kv[which, count:] = jnp.zeros((spare, PAIR), BF)
            grad_kv_other[which, count:] = jnp.zeros((spare, PAIR), BF)
    acc[...] += mm_nt(grad_query, matrix(query_weight))
    query_back[...] += mm_nt(grad_query, query_out[0])
    table_query_out[...] = mm_tn(query_low[0], grad_query)

    @at_last()
    def _():
        rank_rows = query_back[...].astype(BF)
        total = acc[...] + mm(rank_rows, query_in[0])
        grad_normed[...] = total.astype(grad_normed.dtype)
        table_query_in[...] = mm_tn(rank_rows, normed[...])


def self_back_kernel(count, where, *refs):
    attention_back(causal_limit(where[0]), 1, count, False, *refs)


def pair_project_kernel(
    grad_mine, grad_other, weight, low_in, low_out, rows, low, start, total, table_in, table_out,
    acc,
):
    @at_first()
    def _():
        acc[...] = start[...]

    pair_project_step(
        grad_mine, grad_other, weight, low_in, low_out, rows, low, table_in, table_out, acc
    )

    @at_last()
    def _():
        total[...] = acc[...].astype(BF)


def close_kernel(hidden, gains, carried, grad_mine, grad_other, total):
    total[...] = carried[...] + normalize_back(
        hidden[...].astype(F32),
        gains[0:1, :],
        grad_mine[...].astype(F32) + grad_other[...].astype(F32),
    )


def add_rows_kernel(mine, other, *refs):
    total = refs[-1]
    value = mine[...].astype(F32) + other[...].astype(F32)
    total[...] = value[:, None, :]


def frames_back_kernel(
    grad_mine, grad_other, weight, low_in, low_out, rows, low, total, table_in, table_out, acc
):
    @at_first()
    def _():
        acc[...] = jnp.zeros_like(acc)

    pair_project_step(
        grad_mine, grad_other, weight, low_in, low_out, rows, low, table_in, table_out, acc
    )

    @at_last()
    def _():
        total[...] = acc[...].astype(BF)


def pair_project_step(
    grad_mine, grad_other, weight, low_in, low_out, rows, low, table_in, table_out, acc
):
    count = rows.shape[0]
    grad = (grad_mine[0, :count].astype(F32) + grad_other[0, :count].astype(F32)).astype(BF)
    rank_rows = mm_nt(grad, low_out[0]).astype(BF)
    acc[...] += mm_nt(grad, matrix(weight)) + mm(rank_rows, low_in[0])
    table_in[0] = mm_tn(rank_rows, rows[...])
    table_out[0] = mm_tn(low[0], grad)


LANE = 128
PIECE = 32


def pack_kernel(fulls, shares, order, tagged, *refs):
    where = refs[0]
    keep, send = refs[-2:]
    flat = []
    for ref in refs[1:-2]:
        flat += [ref] if len(ref.shape) == 2 else [ref.at[i] for i in range(ref.shape[0])]
    tables, broad = flat[: fulls + shares], flat[fulls + shares :]
    context, tensor = where[0], where[1]
    blocks = keep.shape[1]
    per_group = (len(order) + 3) // 4
    rows = per_group * 16
    lane = lax.broadcasted_iota(jnp.int32, (rows, LANE), 1) // PIECE
    padded = list(order) + [None] * (4 * per_group - len(order))

    def one_block(f, carry):
        shard = f // (blocks // 2)
        local = f - shard * (blocks // 2)
        owned = tensor == shard

        def table_of(k):
            if k is None:
                return jnp.zeros((16, LANE), F32)
            if k < fulls:
                return tables[k][:, pl.ds(pl.multiple_of(f * LANE, LANE), LANE)]
            part = tables[k][:, pl.ds(pl.multiple_of(local * LANE, LANE), LANE)]
            return jnp.where(owned, part, 0.0)

        groups = [
            jnp.concatenate(
                [table_of(k) for k in padded[g * per_group : (g + 1) * per_group]], axis=0
            )
            for g in range(4)
        ]
        for target, side in ((keep, context), (send, 1 - context)):
            for t in range(2):
                p = 2 * side + t
                value = jnp.zeros((rows, LANE), F32)
                for g in range(4):
                    turned = pltpu.roll(groups[g], (PIECE * (g + 4 - p)) % LANE, 1)
                    value = jnp.where(lane == g, turned, value)
                target[t, f, :rows] = value
                row = rows
                for w in broad:
                    at = pl.multiple_of(local * 4 * LANE + p * LANE, LANE)
                    target[t, f, row : row + 16] = jnp.where(owned, w[:, pl.ds(at, LANE)], 0.0)
                    row += 16
                if tagged:
                    tag = where[2].astype(F32) * 0.25
                    target[t, f, row : row + 16] = jnp.full((16, LANE), 1.0, F32) * tag
        return carry

    lax.fori_loop(0, blocks, one_block, 0)


def unpack_kernel(parts, attn_in, attn_out, up_in, up_out, down_in, down_out):
    projections, adapters = attn_in.shape[:2]
    clips, rows = parts.shape[:2]
    per_group = (2 * projections + 2 + 3) // 4
    narrow = 16 * per_group

    def one(a, carry):
        adapter = a.astype(F32)
        block = jnp.zeros((rows - 16, LANE), F32)
        for c in range(clips):
            tag = parts[c, rows - 16 : rows - 15, :].astype(F32)
            same = (tag > adapter - 0.5) & (tag < adapter + 0.5)
            block = block + jnp.where(same, parts[c, : rows - 16].astype(F32), 0.0)

        def piece(k):
            g, at = k // per_group, 16 * (k % per_group)
            return block[at : at + 16, PIECE * g : PIECE * (g + 1)]

        for j in range(projections):
            attn_in[j, a] = piece(j)
            attn_out[j, a] = piece(projections + j)
        up_in[a] = piece(2 * projections)
        down_out[a] = piece(2 * projections + 1)
        up_out[a] = block[narrow : narrow + 16]
        down_in[a] = block[narrow + 16 : narrow + 32]
        return carry

    lax.fori_loop(0, adapters, one, 0)


def shape(dims, dtype):
    return jax.ShapeDtypeStruct(tuple(dims), dtype)


def fixed(array):
    zeros = (0,) * array.ndim
    return pl.BlockSpec(array.shape, lambda *_: zeros)


def fixed_out(*dims):
    zeros = (0,) * len(dims)
    return pl.BlockSpec(dims, lambda *_: zeros)


def call(kernel, steps, ins, outs, scratch=(), scalars=None, name=None, cost=5, aliases=None):
    arrays = [a for a, _ in ins]
    spec = pltpu.PrefetchScalarGridSpec(
        num_scalar_prefetch=0 if scalars is None else 1,
        grid=(steps,),
        in_specs=[s for _, s in ins],
        out_specs=[s for _, s in outs],
        scratch_shapes=list(scratch),
    )
    run = pl.pallas_call(
        kernel,
        grid_spec=spec,
        out_shape=[o for o, _ in outs],
        compiler_params=pltpu.CompilerParams(dimension_semantics=("arbitrary",)),
        cost_estimate=pl.CostEstimate(
            flops=cost * 10_000_000, transcendentals=0, bytes_accessed=cost * 36_900
        ),
        input_output_aliases=aliases or {},
        name=name,
    )
    return run(*arrays) if scalars is None else run(scalars, *arrays)


def on_device(
    hidden,
    encoder,
    cotangent,
    adapter_index,
    ln_gains,
    attn_in_weight,
    attn_out_weight,
    up_weight,
    down_weight,
    attn_adapt_in,
    attn_adapt_out,
    up_adapt_in,
    up_adapt_out,
    down_adapt_in,
    down_adapt_out,
):
    fsdp_size = lax.axis_size("fsdp")
    ctx_size = lax.axis_size("ctx")
    tp_size = lax.axis_size("tp")
    tensor_index = lax.axis_index("tp")
    context_index = lax.axis_index("ctx")
    hidden, encoder, cotangent = hidden[0], encoder[0], cotangent[0]
    rows, width = hidden.shape
    frames = encoder.shape[0]
    padded = -(-frames // 16) * 16
    wide = up_adapt_out.shape[2]
    cols = attn_in_weight.shape[2]
    units = up_weight.shape[1]
    rank = attn_adapt_in.shape[2]
    adapters = attn_adapt_in.shape[1]
    pairs = cols // PAIR
    head_start = tensor_index * cols
    unit_start = tensor_index * units
    mine = adapter_index[0]
    scalars = jnp.stack(
        [context_index.astype(jnp.int32), tensor_index.astype(jnp.int32), mine]
    )

    half_rows = attn_in_weight.shape[1] // ctx_size
    shards = fsdp_size * ctx_size

    def my_half(table):
        return lax.dynamic_slice_in_dim(
            table, context_index * half_rows, half_rows, axis=table.ndim - 2
        )

    attn_half = jnp.concatenate([my_half(attn_in_weight), my_half(attn_out_weight)], axis=0)
    ff_half = jnp.stack([my_half(up_weight), my_half(down_weight)])
    attn_full = lax.all_gather(attn_half, ("fsdp", "ctx"), axis=0)
    ff_full = lax.all_gather(ff_half, ("fsdp", "ctx"), axis=0)

    sel_in = lax.dynamic_index_in_dim(attn_adapt_in, mine, 1, keepdims=False)
    sel_out = lax.dynamic_index_in_dim(attn_adapt_out, mine, 1, keepdims=False)
    part_in = lax.dynamic_slice_in_dim(sel_in, head_start, cols, 2)
    part_out = lax.dynamic_slice_in_dim(sel_out, head_start, cols, 2)
    up_in = lax.dynamic_index_in_dim(up_adapt_in, mine, 0, keepdims=False)
    up_out = lax.dynamic_slice(up_adapt_out, (mine, 0, unit_start), (1, rank, units))[0]
    down_in = lax.dynamic_slice(down_adapt_in, (mine, 0, unit_start), (1, rank, units))[0]
    down_out = lax.dynamic_index_in_dim(down_adapt_out, mine, 0, keepdims=False)

    def weight_cols(slot):
        return attn_full, pl.BlockSpec((shards, 1, half_rows, cols), lambda i, *_: (0, slot(i), 0, 0))

    def weight_pair(slot):
        return attn_full, pl.BlockSpec((shards, 1, half_rows, PAIR), lambda p, *_: (0, slot, 0, p))

    def slot_of(table, slot):
        return table, pl.BlockSpec((1,) + table.shape[1:], lambda i, *_: (slot(i), 0, 0))

    def slot_pair(table, slot):
        return table, pl.BlockSpec((1, rank, PAIR), lambda p, *_: (slot, 0, p))

    def whole(array):
        return array, fixed(array)

    def out(dims, dtype):
        return shape(dims, dtype), fixed_out(*dims)

    def by_pair(count, dtype=BF):
        return shape((count, cols), dtype), pl.BlockSpec((count, PAIR), lambda p, *_: (0, p))

    def kv_pair(array):
        return array, pl.BlockSpec((2, array.shape[1], PAIR), lambda p, *_: (0, 0, p))

    def at(array, first=0):
        return array, pl.BlockSpec((1,) + array.shape[1:], lambda i, *_: (first + i, 0, 0))

    def at_slot(array):
        return array, pl.BlockSpec((1,) + array.shape[1:], lambda i, *_: (0, 0, 0))

    logsum_out = (
        shape((pairs, 2, rows), F32),
        pl.BlockSpec((1, 2, rows), lambda p, *_: (p, 0, 0)),
    )

    def logsum_in(array):
        rest = (0,) * (array.ndim - 1)
        return array, pl.BlockSpec((1,) + array.shape[1:], lambda p, *_: (p, *rest))

    saved_shape = shape((pairs, 2, 2, padded, rows), BF)

    def pair_in(array):
        return array, pl.BlockSpec((array.shape[0], PAIR), lambda p, *_: (0, p))

    regular = (
        ctx_size == 2 and tp_size == 2 and rank == 16
        and width == LANE * fsdp_size and wide == 4 * LANE * fsdp_size
    )

    def ordered(first, *others):
        return lax.optimization_barrier((first, *others))

    def pack(full, part, wides, order, tagged, name, after):
        count = 16 * ((len(order) + 3) // 4 + len(wides) + tagged)
        dims = (2, fsdp_size, count, LANE)

        def number(arrays):
            return sum(1 if a.ndim == 2 else a.shape[0] for a in arrays)

        keep, send = call(
            partial(pack_kernel, number(full), number(part), order, tagged),
            1,
            [whole(a) for a in full + part + wides],
            [out(dims, F32), out(dims, F32)],
            scalars=scalars,
            name=name,
        )
        recv, after = ordered(swap(send, "ctx"), after)

        def pick(i):
            return lax.dynamic_index_in_dim(keep, i, 0, keepdims=False) + (
                lax.dynamic_index_in_dim(recv, i, 0, keepdims=False)
            )

        return pick(tensor_index), pick(1 - tensor_index).astype(BF), after

    def finish(kept, away):
        return lax.all_to_all((kept + away.astype(F32)).astype(BF), "fsdp", 0, 0, tiled=True)

    wide_acc = pltpu.VMEM((rows, width), F32)
    rank_acc = pltpu.VMEM((rows, rank), F32)
    rank_keep = pltpu.VMEM((rows, rank), BF)

    n1, query, self_kv, self_low = call(
        qkv_kernel,
        3,
        [
            whole(hidden),
            whole(ln_gains),
            weight_cols(lambda i: i),
            slot_of(sel_in, lambda i: i),
            slot_of(part_out, lambda i: i),
        ],
        [
            out((rows, width), BF),
            out((rows, cols), BF),
            (
                shape((2, rows, cols), BF),
                pl.BlockSpec((1, rows, cols), lambda i: (jnp.maximum(i - 1, 0), 0, 0)),
            ),
            (shape((3, rows, rank), BF), pl.BlockSpec((1, rows, rank), lambda i: (i, 0, 0))),
        ],
        name="qkv",
    )
    self_kv_other = swap(self_kv, "ctx")
    cross_kv, frames_low = call(
        frames_kernel,
        2,
        [
            whole(encoder),
            weight_cols(lambda i: 4 + i),
            slot_of(sel_in, lambda i: 5 + i),
            slot_of(part_out, lambda i: 5 + i),
        ],
        [
            (
                shape((2, padded, cols), BF),
                pl.BlockSpec((1, padded, cols), lambda i: (i, 0, 0)),
            ),
            (
                shape((2, frames, rank), BF),
                pl.BlockSpec((1, frames, rank), lambda i: (i, 0, 0)),
            ),
        ],
        name="frames",
        cost=7,
    )
    cross_kv_other = swap(cross_kv, "ctx")
    self_mixed, self_logsum, branch, self_o_low = call(
        self_kernel,
        pairs,
        [
            pair_in(query),
            kv_pair(self_kv),
            kv_pair(self_kv_other),
            weight_pair(6),
            slot_pair(part_in, 3),
            slot_of(sel_out, lambda i: 3),
        ],
        [by_pair(rows), logsum_out, out((rows, width), BF), out((rows, rank), BF)],
        [wide_acc, rank_acc],
        scalars,
        name="self_attention",
        cost=7,
    )
    branch, branch_other = with_other(branch, "tp")
    first_mid, n2, cross_q, cross_q_low, cross_mixed, cross_logsum, branch, cross_o_low = call(
        partial(cross_kernel, frames),
        pairs,
        [
            whole(hidden),
            whole(branch),
            whole(branch_other),
            whole(ln_gains),
            weight_pair(3),
            slot_of(sel_in, lambda i: 4),
            slot_pair(part_out, 4),
            kv_pair(cross_kv),
            kv_pair(cross_kv_other),
            weight_pair(7),
            slot_pair(part_in, 7),
            slot_of(sel_out, lambda i: 7),
        ],
        [
            out((rows, width), F32),
            out((rows, width), BF),
            by_pair(rows),
            out((rows, rank), BF),
            by_pair(rows),
            logsum_in(saved_shape),
            out((rows, width), BF),
            out((rows, rank), BF),
        ],
        [wide_acc, rank_acc],
        name="cross_attention",
        cost=13,
    )
    branch, branch_other = with_other(branch, "tp")
    chunk = min(units, 512)

    def unit_weight(slot):
        return ff_full, pl.BlockSpec((shards, 1, half_rows, chunk), lambda i: (0, slot, 0, i))

    def unit_cols(array):
        return array, pl.BlockSpec((rank, chunk), lambda i: (0, i))

    second_mid, n3, up_low, down_back = call(
        third_norm_kernel,
        1,
        [
            whole(a)
            for a in (
                first_mid, branch, branch_other, ln_gains, cotangent, up_in, down_out
            )
        ],
        [
            out((rows, width), F32),
            out((rows, width), BF),
            out((rows, rank), BF),
            out((rows, rank), BF),
        ],
        name="third_norm",
    )
    branch, grad_n3, up_in_t, up_out_t, down_in_t, down_out_t = call(
        units_kernel,
        units // chunk,
        [
            whole(n3),
            whole(up_low),
            whole(down_back),
            whole(cotangent),
            unit_weight(0),
            unit_weight(1),
            whole(up_in),
            unit_cols(up_out),
            unit_cols(down_in),
            whole(down_out),
        ],
        [
            out((rows, width), BF),
            out((rows, width), BF),
            out((rank, width), F32),
            unit_cols(shape((rank, units), F32)),
            unit_cols(shape((rank, units), F32)),
            out((rank, width), F32),
        ],
        [wide_acc, wide_acc, rank_acc, rank_acc],
        name="units",
        cost=11,
    )
    grad_n3, grad_n3_other = with_other(grad_n3, "tp")
    branch, grad_n3_other = ordered(branch, grad_n3_other)
    branch, branch_other = with_other(branch, "tp")

    def back_call(
        kernel, scalar, carried, middle, grad, grad_other, slots, queries, mixed, kv, kv_other,
        logsum, normed, query_low, low, kind, name, cost,
    ):
        weight_slot, low_slot, query_slot, query_low_slot = slots
        count = kv.shape[1]
        kv_out = (
            shape((2, count, cols), BF),
            pl.BlockSpec((2, count, PAIR), lambda p, *_: (0, 0, p)),
        )
        return call(
            kernel,
            pairs,
            [
                whole(carried),
                whole(middle),
                whole(ln_gains),
                whole(grad),
                whole(grad_other),
                weight_pair(weight_slot),
                slot_pair(part_in, low_slot),
                slot_of(sel_out, lambda i: low_slot),
                weight_pair(query_slot),
                slot_of(sel_in, lambda i: query_low_slot),
                slot_pair(part_out, query_low_slot),
                pair_in(queries),
                pair_in(mixed),
                kv_pair(kv),
                kv_pair(kv_other),
                logsum_in(logsum),
                whole(normed),
                at_slot(query_low),
                whole(low),
            ],
            [
                out((rows, width), F32),
                out((rows, width), kind),
                kv_out,
                kv_out,
                by_pair(rank, F32),
                out((rank, width), F32),
                out((rank, width), F32),
                by_pair(rank, F32),
            ],
            [pltpu.VMEM((rows, width), BF), rank_keep, wide_acc, rank_acc],
            scalar,
            name=name,
            cost=cost,
        )

    grad_second, grad_n2, grad_ckv, grad_ckv_send, co_in_t, co_out_t, cq_in_t, cq_out_t = back_call(
        partial(attention_back, no_limit, 2, frames, True), None, cotangent, second_mid, grad_n3, grad_n3_other, (7, 7, 3, 4),
        cross_q, cross_mixed, cross_kv, cross_kv_other, cross_logsum, n2, cross_q_low[None],
        cross_o_low, BF, "cross_back", 18,
    )
    grad_n2, grad_ckv_send, branch_other = ordered(grad_n2, grad_ckv_send, branch_other)
    grad_n2, grad_n2_other = with_other(grad_n2, "tp")
    grad_ckv_other = swap(grad_ckv_send, "ctx")
    layer_out = (
        second_mid + (branch.astype(F32) + branch_other.astype(F32))
    ).astype(BF)
    block_rows = 128
    grad_frames, ckv_in_t, ckv_out_t = call(
        frames_back_kernel,
        2,
        [
            at(grad_ckv),
            at(grad_ckv_other),
            weight_cols(lambda i: 4 + i),
            slot_of(sel_in, lambda i: 5 + i),
            slot_of(part_out, lambda i: 5 + i),
            whole(encoder),
            at(frames_low),
        ],
        [
            out((frames, width), BF),
            at(shape((2, rank, width), F32)),
            at(shape((2, rank, cols), F32)),
        ],
        [pltpu.VMEM((frames, width), F32)],
        name="frames_back",
        cost=9,
    )
    grad_frames, grad_n2_other = ordered(grad_frames, grad_n2_other)
    grad_frames, grad_frames_other = with_other(grad_frames, "tp")
    grad_first, grad_n1_start, grad_skv, grad_skv_send, so_in_t, so_out_t, q_in_t, q_out_t = back_call(
        partial(self_back_kernel, rows), scalars, grad_second, first_mid, grad_n2, grad_n2_other, (6, 3, 0, 0),
        query, self_mixed, self_kv, self_kv_other, self_logsum, n1, self_low,
        self_o_low, F32, "self_back", 12,
    )
    grad_skv_other = swap(grad_skv_send, "ctx")
    grad_n1, kv_in_t, kv_out_t = call(
        pair_project_kernel,
        2,
        [
            at(grad_skv),
            at(grad_skv_other),
            weight_cols(lambda i: 1 + i),
            slot_of(sel_in, lambda i: 1 + i),
            slot_of(part_out, lambda i: 1 + i),
            whole(n1),
            at(self_low, 1),
            whole(grad_n1_start),
        ],
        [
            out((rows, width), BF),
            at(shape((2, rank, width), F32)),
            at(shape((2, rank, cols), F32)),
        ],
        [wide_acc],
        name="self_project_back",
    )
    grad_n1, grad_n1_other = with_other(grad_n1, "tp")
    def row_blocks(array):
        rest = (0,) * (array.ndim - 1)
        return array, pl.BlockSpec((block_rows,) + array.shape[1:], lambda i: (i, *rest))

    block_rows = 256
    encoder_args = (
        add_rows_kernel,
        -(-frames // block_rows),
        [row_blocks(grad_frames)],
        [row_blocks(shape((frames, 1, width), F32))],
    )

    def encoder_total(other):
        kernel, steps, ins, outs = encoder_args
        (total,) = call(kernel, steps, ins + [row_blocks(other)], outs, name="encoder_total")
        return total

    full = [q_in_t, kv_in_t, cq_in_t, ckv_in_t, so_out_t, co_out_t, up_in_t, down_out_t]
    part = [so_in_t, co_in_t, q_out_t, kv_out_t, cq_out_t, ckv_out_t]
    if regular:
        order = (0, 1, 2, 10, 3, 4, 5, 11, 12, 13, 14, 6, 15, 16, 17, 7, 8, 9)
        full[0], layer_out = ordered(q_in_t, layer_out)
        kept, away, grad_frames_other = pack(
            full, part, [up_out_t, down_in_t], order, 1, "pack", grad_frames_other
        )
        grad_encoder = encoder_total(grad_frames_other)
        away, grad_encoder = ordered(swap(away, "tp"), grad_encoder)
        parts = finish(kept, away)
        narrow_out = (attn_adapt_in.shape[0], adapters, rank, PIECE)
        tables = call(
            unpack_kernel,
            1,
            [whole(parts)],
            [
                out(narrow_out, F32),
                out(narrow_out, F32),
                out((adapters, rank, PIECE), F32),
                out((adapters, rank, LANE), F32),
                out((adapters, rank, LANE), F32),
                out((adapters, rank, PIECE), F32),
            ],
            name="unpack",
        )
    else:
        grad_encoder = encoder_total(grad_frames_other)
        chosen = (mine == jnp.arange(adapters, dtype=jnp.int32)).astype(F32)

        def summed(parts, start, full):
            parts = [t for p in parts for t in ([p] if p.ndim == 2 else [p[0], p[1]])]

            def spread_out(part):
                if part.shape[1] == full:
                    return part
                blank = jnp.zeros((part.shape[0], full), F32)
                return lax.dynamic_update_slice_in_dim(blank, part, start, axis=1)

            stacked = jnp.stack([spread_out(p) for p in parts])
            table = chosen[None, :, None, None] * stacked[:, None]
            return lax.psum_scatter(
                table, ("fsdp", "ctx", "tp"), scatter_dimension=3, tiled=True
            )

        attn_in_t = summed(
            [q_in_t, kv_in_t, so_in_t, cq_in_t, ckv_in_t, co_in_t], head_start, width
        )
        attn_out_t = summed(
            [q_out_t, kv_out_t, so_out_t, cq_out_t, ckv_out_t, co_out_t], head_start, width
        )
        small = summed([up_in_t, down_out_t], head_start, width)
        large = summed([up_out_t, down_in_t], unit_start, wide)
        tables = (attn_in_t, attn_out_t, small[0], large[0], large[1], small[1])
    grad_encoder = grad_encoder.reshape(frames, width)
    (grad_hidden,) = call(
        close_kernel,
        1,
        [whole(a) for a in (hidden, ln_gains, grad_first, grad_n1, grad_n1_other)],
        [out((rows, width), F32)],
        name="hidden_total",
    )
    return (
        layer_out[None],
        grad_hidden[None],
        grad_encoder[None],
        *tables,
    )
def solution(mesh):
    in_specs = (
        P("fsdp", "ctx", None),
        P("fsdp", "ctx", None),
        P("fsdp", "ctx", None),
        P("fsdp"),
        P(),
        P(None, "fsdp", "tp"),
        P(None, "fsdp", "tp"),
        P("fsdp", "tp"),
        P("fsdp", "tp"),
        P(),
        P(),
        P(),
        P(),
        P(),
        P(),
    )
    out_specs = (
        P("fsdp", "ctx", None),
        P("fsdp", "ctx", None),
        P("fsdp", "ctx", None),
        P(None, None, None, ("fsdp", "ctx", "tp")),
        P(None, None, None, ("fsdp", "ctx", "tp")),
        P(None, None, ("fsdp", "ctx", "tp")),
        P(None, None, ("fsdp", "ctx", "tp")),
        P(None, None, ("fsdp", "ctx", "tp")),
        P(None, None, ("fsdp", "ctx", "tp")),
    )
    return jax.shard_map(
        on_device, mesh=mesh, in_specs=in_specs, out_specs=out_specs, check_vma=False
    )
```

```python
from functools import partial

import jax
import jax.numpy as jnp
from jax import lax
from jax.experimental import pallas as pl
from jax.experimental.pallas import tpu as pltpu
from jax.sharding import PartitionSpec as P

HEAD_DIM = 64
PAIR = 2 * HEAD_DIM
EPSILON = 1e-05
MASKED_SCORE = -1000000000.0
SCALE = HEAD_DIM ** (-0.5)
BF = jnp.bfloat16
F32 = jnp.float32


def mm(a, b):
    return lax.dot_general(a, b, (((1,), (0,)), ((), ())), preferred_element_type=F32)


def mm_nt(a, b):
    return lax.dot_general(a, b, (((1,), (1,)), ((), ())), preferred_element_type=F32)


def mm_tn(a, b):
    return lax.dot_general(a, b, (((0,), (0,)), ((), ())), preferred_element_type=F32)


def norm_parts(rows):
    centred = rows - jnp.mean(rows, axis=-1, keepdims=True)
    spread = jnp.mean(centred * centred, axis=-1, keepdims=True)
    inverse = lax.rsqrt(spread + EPSILON)
    return centred * inverse, inverse


def normalize(rows, gain):
    return norm_parts(rows)[0] * gain


def normalize_back(rows, gain, gradient):
    unit, inverse = norm_parts(rows)
    scaled = gradient * gain
    first = jnp.mean(scaled, axis=-1, keepdims=True)
    second = jnp.mean(scaled * unit, axis=-1, keepdims=True)
    return (scaled - first - unit * second) * inverse


def swap(value, axis):
    return lax.ppermute(value, axis, [(0, 1), (1, 0)])


def with_other(partial_value, axis):
    if lax.axis_size(axis) == 2:
        return partial_value, swap(partial_value, axis)
    return lax.psum(partial_value, axis), jnp.zeros_like(partial_value)


def matrix(ref):
    block = ref[...]
    return block.reshape(block.shape[0] * block.shape[2], block.shape[3])


def half_masks(rows):
    lane = lax.broadcasted_iota(jnp.int32, (rows, PAIR), 1)
    return lane < HEAD_DIM, lane >= HEAD_DIM


def pick_half(rows, keep):
    return jnp.where(keep, rows, jnp.zeros_like(rows))


def join_halves(first, second):
    row = lax.broadcasted_iota(jnp.int32, first.shape, 0)
    return jnp.where(row < HEAD_DIM, first, second).T


def pair_forward(queries, keys, values, limit, saved=None):
    mixed, logsums = [], []
    turned = [v.T for v in values]
    for half, keep in enumerate(half_masks(queries.shape[0])):
        mine = pick_half(queries, keep) * BF(SCALE)
        scores = [limit(i, mm_nt(k, mine)) for i, k in enumerate(keys)]
        top = jnp.max(scores[0], axis=0, keepdims=True)
        for s in scores[1:]:
            top = jnp.maximum(top, jnp.max(s, axis=0, keepdims=True))
        powers = [jnp.exp(s - top) for s in scores]
        total = sum(jnp.sum(e, axis=0, keepdims=True) for e in powers)
        share = 1.0 / total
        weights = [(e * share).astype(BF) for e in powers]
        if saved is not None:
            for i, w in enumerate(weights):
                saved[0, half, i, : w.shape[0]] = w
        mixed.append(sum(mm(v, w) for v, w in zip(turned, weights)))
        logsums.append(top + jnp.log(total))
    return join_halves(*mixed), logsums


def pair_backward(grad, mixed, queries, keys, values, logsums, limit, saved=None):
    grad_query, grad_keys, grad_values = [], [0.0] * len(keys), [0.0] * len(keys)
    inners = (grad.astype(F32) * mixed.astype(F32)).T
    turned = [k.T for k in keys]
    for half, (keep, logsum) in enumerate(zip(half_masks(queries.shape[0]), logsums)):
        mine = pick_half(queries, keep) * BF(SCALE)
        grad_mine = pick_half(grad, keep)
        at = HEAD_DIM * half
        inner = jnp.sum(inners[at : at + HEAD_DIM], axis=0, keepdims=True)
        part = 0.0
        for i, (key, value) in enumerate(zip(keys, values)):
            if saved is None:
                weights = jnp.exp(limit(i, mm_nt(key, mine)) - logsum)
                rounded = weights.astype(BF)
            else:
                rounded = saved[0, half, i, : key.shape[0]]
                weights = rounded.astype(F32)
            grad_scores = (weights * (mm_nt(value, grad_mine) - inner)).astype(BF)
            part = part + mm(turned[i], grad_scores)
            grad_keys[i] = grad_keys[i] + mm(grad_scores, mine)
            grad_values[i] = grad_values[i] + mm(rounded, grad_mine)
        grad_query.append(part)
    return (
        (join_halves(*grad_query) * SCALE).astype(BF),
        [g.astype(BF) for g in grad_keys],
        [g.astype(BF) for g in grad_values],
    )


def no_limit(index, scores):
    return scores


def causal_limit(context):
    def limit(index, scores):
        if index == 0:
            key = lax.broadcasted_iota(jnp.int32, scores.shape, 0)
            query = lax.broadcasted_iota(jnp.int32, scores.shape, 1)
            return jnp.where(key <= query, scores, MASKED_SCORE)
        return jnp.where(context == 1, scores, MASKED_SCORE)

    return limit


def at_first(step=0):
    return pl.when(pl.program_id(0) == step)


def at_last():
    return pl.when(pl.program_id(0) == pl.num_programs(0) - 1)


def halves_kernel(where, inputs, outputs, joined):
    count = inputs.shape[0]
    joined[:count] = inputs[...]
    joined[count:] = outputs[...]


def qkv_kernel(hidden, gains, weight, low_in, low_out, normed, query, key_value, low):
    @at_first()
    def _():
        normed[...] = normalize(hidden[...].astype(F32), gains[0:1, :]).astype(BF)

    rows = normed[...]
    rank_rows = mm_nt(rows, low_in[0]).astype(BF)
    low[0] = rank_rows
    value = (mm(rows, matrix(weight)) + mm(rank_rows, low_out[0])).astype(BF)

    @at_first()
    def _():
        query[...] = value

    @pl.when(pl.program_id(0) > 0)
    def _():
        key_value[0] = value


def frames_kernel(frames, weight, low_in, low_out, key_value, low):
    rows = frames[...]
    rank_rows = mm_nt(rows, low_in[0]).astype(BF)
    low[0] = rank_rows
    count = rows.shape[0]
    key_value[0, :count] = (mm(rows, matrix(weight)) + mm(rank_rows, low_out[0])).astype(BF)
    spare = key_value.shape[1] - count
    if spare:
        key_value[0, count:] = jnp.zeros((spare, key_value.shape[2]), BF)


def self_kernel(
    where, query, mine, other, weight, low_in, low_out, mixed, logsum, branch, low, acc, low_acc
):
    @at_first()
    def _():
        acc[...] = jnp.zeros_like(acc)
        low_acc[...] = jnp.zeros_like(low_acc)

    out, logs = pair_forward(
        query[...], (mine[0], other[0]), (mine[1], other[1]), causal_limit(where[0])
    )
    out = out.astype(BF)
    mixed[...] = out
    logsum[0, 0:1, :] = logs[0]
    logsum[0, 1:2, :] = logs[1]
    acc[...] += mm_nt(out, matrix(weight))
    low_acc[...] += mm_nt(out, low_in[0])

    @at_last()
    def _():
        rank_rows = low_acc[...].astype(BF)
        low[...] = rank_rows
        branch[...] = (acc[...] + mm(rank_rows, low_out[0])).astype(BF)


def cross_kernel(
    count,
    hidden, branch_mine, branch_other, gains, query_weight, query_in, query_out, mine, other,
    weight, low_in, low_out,
    middle, normed, query, query_low, mixed, saved, branch, low, acc, low_acc,
):
    @at_first()
    def _():
        acc[...] = jnp.zeros_like(acc)
        low_acc[...] = jnp.zeros_like(low_acc)
        total = hidden[...].astype(F32) + (
            branch_mine[...].astype(F32) + branch_other[...].astype(F32)
        )
        middle[...] = total
        rows = normalize(total, gains[1:2, :]).astype(BF)
        normed[...] = rows
        query_low[...] = mm_nt(rows, query_in[0]).astype(BF)

    queries = (
        mm(normed[...], matrix(query_weight)) + mm(query_low[...], query_out[0])
    ).astype(BF)
    query[...] = queries
    out, _ = pair_forward(
        queries,
        (mine[0, :count], other[0, :count]),
        (mine[1, :count], other[1, :count]),
        no_limit,
        saved,
    )
    out = out.astype(BF)
    mixed[...] = out
    acc[...] += mm_nt(out, matrix(weight))
    low_acc[...] += mm_nt(out, low_in[0])

    @at_last()
    def _():
        rank_rows = low_acc[...].astype(BF)
        low[...] = rank_rows
        branch[...] = (acc[...] + mm(rank_rows, low_out[0])).astype(BF)


def third_norm_kernel(
    middle, branch_mine, branch_other, gains, cotangent, up_in, down_out,
    second, normed, up_low, down_back,
):
    total = middle[...] + (branch_mine[...].astype(F32) + branch_other[...].astype(F32))
    second[...] = total
    rows = normalize(total, gains[2:3, :]).astype(BF)
    normed[...] = rows
    up_low[...] = mm_nt(rows, up_in[...]).astype(BF)
    down_back[...] = mm_nt(cotangent[...], down_out[...]).astype(BF)


def units_kernel(
    normed, up_low, down_back, cotangent, up, down, up_in, up_out, down_in, down_out,
    branch, grad_normed, table_up_in, table_up_out, table_down_in, table_down_out,
    acc, back, low_acc, back_low,
):
    @at_first()
    def _():
        acc[...] = jnp.zeros_like(acc)
        back[...] = jnp.zeros_like(back)
        low_acc[...] = jnp.zeros_like(low_acc)
        back_low[...] = jnp.zeros_like(back_low)

    up_rows, down_rows = matrix(up), matrix(down)
    value = mm(normed[...], up_rows) + mm(up_low[...], up_out[...])
    spread = 1.0 + lax.erf(value * 0.7071067811865476)
    act = (0.5 * value * spread).astype(BF)
    slope = 0.5 * spread + value * (0.3989422804014327 * jnp.exp(-0.5 * value * value))
    acc[...] += mm_nt(act, down_rows)
    low_acc[...] += mm_nt(act, down_in[...])
    grad_act = mm(cotangent[...], down_rows) + mm(down_back[...], down_in[...])
    grad = (grad_act * slope).astype(BF)
    back[...] += mm_nt(grad, up_rows)
    back_low[...] += mm_nt(grad, up_out[...])
    table_up_out[...] = mm_tn(up_low[...], grad)
    table_down_in[...] = mm_tn(down_back[...], act)

    @at_last()
    def _():
        down_low = low_acc[...].astype(BF)
        branch[...] = (acc[...] + mm(down_low, down_out[...])).astype(BF)
        up_back = back_low[...].astype(BF)
        grad_normed[...] = (back[...] + mm(up_back, up_in[...])).astype(BF)
        table_up_in[...] = mm_tn(up_back, normed[...])
        table_down_out[...] = mm_tn(down_low, cotangent[...])


def attention_back(
    limit, slot, count, stored, carried, rows, gains, grad_mine, grad_other, weight, low_in, low_out,
    query_weight, query_in, query_out, query, mixed, mine, other, logsum, normed, query_low, low,
    carry, grad_normed, grad_kv, grad_kv_other,
    table_in, table_out, table_query_in, table_query_out,
    narrow, back_low, acc, query_back,
):
    @at_first()
    def _():
        total = carried[...].astype(F32) + normalize_back(
            rows[...],
            gains[slot : slot + 1, :],
            grad_mine[...].astype(F32) + grad_other[...].astype(F32),
        )
        carry[...] = total
        narrow[...] = total.astype(BF)
        back_low[...] = mm_nt(narrow[...], low_out[0]).astype(BF)
        acc[...] = jnp.zeros_like(acc)
        query_back[...] = jnp.zeros_like(query_back)
        table_out[...] = mm_tn(low[...], narrow[...])

    grad = (mm(narrow[...], matrix(weight)) + mm(back_low[...], low_in[0])).astype(BF)
    table_in[...] = mm_tn(back_low[...], mixed[...])
    grad_query, grad_keys, grad_values = pair_backward(
        grad,
        mixed[...],
        query[...],
        (mine[0, :count], other[0, :count]),
        (mine[1, :count], other[1, :count]),
        (None, None) if stored else (logsum[0, 0:1, :], logsum[0, 1:2, :]),
        limit,
        logsum if stored else None,
    )
    for which, (first, second) in enumerate((grad_keys, grad_values)):
        grad_kv[which, :count] = first
        grad_kv_other[which, :count] = second
        spare = grad_kv.shape[1] - count
        if spare:
            grad_kv[which, count:] = jnp.zeros((spare, PAIR), BF)
            grad_kv_other[which, count:] = jnp.zeros((spare, PAIR), BF)
    acc[...] += mm_nt(grad_query, matrix(query_weight))
    query_back[...] += mm_nt(grad_query, query_out[0])
    table_query_out[...] = mm_tn(query_low[0], grad_query)

    @at_last()
    def _():
        rank_rows = query_back[...].astype(BF)
        total = acc[...] + mm(rank_rows, query_in[0])
        grad_normed[...] = total.astype(grad_normed.dtype)
        table_query_in[...] = mm_tn(rank_rows, normed[...])


def self_back_kernel(count, where, *refs):
    attention_back(causal_limit(where[0]), 1, count, False, *refs)


def pair_project_kernel(
    grad_mine, grad_other, weight, low_in, low_out, rows, low, start, total, table_in, table_out,
    acc,
):
    @at_first()
    def _():
        acc[...] = start[...]

    pair_project_step(
        grad_mine, grad_other, weight, low_in, low_out, rows, low, table_in, table_out, acc
    )

    @at_last()
    def _():
        total[...] = acc[...].astype(BF)


def close_kernel(hidden, gains, carried, grad_mine, grad_other, total):
    total[...] = carried[...] + normalize_back(
        hidden[...].astype(F32),
        gains[0:1, :],
        grad_mine[...].astype(F32) + grad_other[...].astype(F32),
    )


def add_rows_kernel(mine, other, *refs):
    total = refs[-1]
    value = mine[...].astype(F32) + other[...].astype(F32)
    total[...] = value[:, None, :]


def frames_back_kernel(
    grad_mine, grad_other, weight, low_in, low_out, rows, low, total, table_in, table_out, acc
):
    @at_first()
    def _():
        acc[...] = jnp.zeros_like(acc)

    pair_project_step(
        grad_mine, grad_other, weight, low_in, low_out, rows, low, table_in, table_out, acc
    )

    @at_last()
    def _():
        total[...] = acc[...].astype(BF)


def pair_project_step(
    grad_mine, grad_other, weight, low_in, low_out, rows, low, table_in, table_out, acc
):
    count = rows.shape[0]
    grad = (grad_mine[0, :count].astype(F32) + grad_other[0, :count].astype(F32)).astype(BF)
    rank_rows = mm_nt(grad, low_out[0]).astype(BF)
    acc[...] += mm_nt(grad, matrix(weight)) + mm(rank_rows, low_in[0])
    table_in[0] = mm_tn(rank_rows, rows[...])
    table_out[0] = mm_tn(low[0], grad)


LANE = 128
PIECE = 32


def pack_kernel(fulls, shares, order, tagged, *refs):
    where = refs[0]
    keep, send = refs[-2:]
    flat = []
    for ref in refs[1:-2]:
        flat += [ref] if len(ref.shape) == 2 else [ref.at[i] for i in range(ref.shape[0])]
    tables, broad = flat[: fulls + shares], flat[fulls + shares :]
    context, tensor = where[0], where[1]
    blocks = keep.shape[1]
    per_group = (len(order) + 3) // 4
    rows = per_group * 16
    lane = lax.broadcasted_iota(jnp.int32, (rows, LANE), 1) // PIECE
    padded = list(order) + [None] * (4 * per_group - len(order))

    def one_block(f, carry):
        shard = f // (blocks // 2)
        local = f - shard * (blocks // 2)
        owned = tensor == shard

        def table_of(k):
            if k is None:
                return jnp.zeros((16, LANE), F32)
            if k < fulls:
                return tables[k][:, pl.ds(pl.multiple_of(f * LANE, LANE), LANE)]
            part = tables[k][:, pl.ds(pl.multiple_of(local * LANE, LANE), LANE)]
            return jnp.where(owned, part, 0.0)

        groups = [
            jnp.concatenate(
                [table_of(k) for k in padded[g * per_group : (g + 1) * per_group]], axis=0
            )
            for g in range(4)
        ]
        for target, side in ((keep, context), (send, 1 - context)):
            for t in range(2):
                p = 2 * side + t
                value = jnp.zeros((rows, LANE), F32)
                for g in range(4):
                    turned = pltpu.roll(groups[g], (PIECE * (g + 4 - p)) % LANE, 1)
                    value = jnp.where(lane == g, turned, value)
                if tagged:
                    spare = 4 * per_group - len(order)
                    tag = where[2].astype(F32) * 0.25
                    low = rows - 16 * spare
                    at_row = lax.broadcasted_iota(jnp.int32, (rows, LANE), 0)
                    value = jnp.where((lane == 3) & (at_row >= low), tag, value)
                target[t, f, :rows] = value
                row = rows
                for w in broad:
                    at = pl.multiple_of(local * 4 * LANE + p * LANE, LANE)
                    target[t, f, row : row + 16] = jnp.where(owned, w[:, pl.ds(at, LANE)], 0.0)
                    row += 16
        return carry

    lax.fori_loop(0, blocks, one_block, 0)


def unpack_kernel(parts, attn_in, attn_out, up_in, up_out, down_in, down_out):
    projections, adapters = attn_in.shape[:2]
    clips, rows = parts.shape[:2]
    per_group = (2 * projections + 2 + 3) // 4
    narrow = 16 * per_group

    tags = []
    for c in range(clips):
        tag = parts[c, narrow - 16 : narrow, 3 * PIECE :].astype(F32)[0:1, 0:1]
        tags.append(jnp.broadcast_to(tag, (1, LANE)))

    def one(a, carry):
        adapter = a.astype(F32)
        block = jnp.zeros((rows, LANE), F32)
        for c in range(clips):
            same = (tags[c] > adapter - 0.5) & (tags[c] < adapter + 0.5)
            weight = jnp.where(same, 1.0, 0.0)
            block = block + parts[c].astype(F32) * weight

        def piece(k):
            g, at = k // per_group, 16 * (k % per_group)
            return block[at : at + 16, PIECE * g : PIECE * (g + 1)]

        for j in range(projections):
            attn_in[j, a] = piece(j)
            attn_out[j, a] = piece(projections + j)
        up_in[a] = piece(2 * projections)
        down_out[a] = piece(2 * projections + 1)
        up_out[a] = block[narrow : narrow + 16]
        down_in[a] = block[narrow + 16 : narrow + 32]
        return carry

    lax.fori_loop(0, adapters, one, 0)


def shape(dims, dtype):
    return jax.ShapeDtypeStruct(tuple(dims), dtype)


def fixed(array):
    zeros = (0,) * array.ndim
    return pl.BlockSpec(array.shape, lambda *_: zeros)


def fixed_out(*dims):
    zeros = (0,) * len(dims)
    return pl.BlockSpec(dims, lambda *_: zeros)


def call(kernel, steps, ins, outs, scratch=(), scalars=None, name=None, cost=5, aliases=None):
    arrays = [a for a, _ in ins]
    spec = pltpu.PrefetchScalarGridSpec(
        num_scalar_prefetch=0 if scalars is None else 1,
        grid=(steps,),
        in_specs=[s for _, s in ins],
        out_specs=[s for _, s in outs],
        scratch_shapes=list(scratch),
    )
    run = pl.pallas_call(
        kernel,
        grid_spec=spec,
        out_shape=[o for o, _ in outs],
        compiler_params=pltpu.CompilerParams(dimension_semantics=("arbitrary",)),
        cost_estimate=pl.CostEstimate(
            flops=cost * 10_000_000, transcendentals=0, bytes_accessed=cost * 36_900
        ),
        input_output_aliases=aliases or {},
        name=name,
    )
    return run(*arrays) if scalars is None else run(scalars, *arrays)


def on_device(
    hidden,
    encoder,
    cotangent,
    adapter_index,
    ln_gains,
    attn_in_weight,
    attn_out_weight,
    up_weight,
    down_weight,
    attn_adapt_in,
    attn_adapt_out,
    up_adapt_in,
    up_adapt_out,
    down_adapt_in,
    down_adapt_out,
):
    fsdp_size = lax.axis_size("fsdp")
    ctx_size = lax.axis_size("ctx")
    tp_size = lax.axis_size("tp")
    tensor_index = lax.axis_index("tp")
    context_index = lax.axis_index("ctx")
    hidden, encoder, cotangent = hidden[0], encoder[0], cotangent[0]
    rows, width = hidden.shape
    frames = encoder.shape[0]
    padded = -(-frames // 16) * 16
    wide = up_adapt_out.shape[2]
    cols = attn_in_weight.shape[2]
    units = up_weight.shape[1]
    rank = attn_adapt_in.shape[2]
    adapters = attn_adapt_in.shape[1]
    pairs = cols // PAIR
    head_start = tensor_index * cols
    unit_start = tensor_index * units
    mine = adapter_index[0]
    scalars = jnp.stack(
        [context_index.astype(jnp.int32), tensor_index.astype(jnp.int32), mine]
    )

    def out(dims, dtype):
        return shape(dims, dtype), fixed_out(*dims)

    half_rows = attn_in_weight.shape[1] // ctx_size
    shards = fsdp_size * ctx_size

    def my_half(table):
        return lax.dynamic_slice_in_dim(
            table, context_index * half_rows, half_rows, axis=table.ndim - 2
        )

    heads_tables = (attn_in_weight, attn_out_weight)
    (attn_half,) = call(
        halves_kernel,
        1,
        [
            (t, pl.BlockSpec((t.shape[0], half_rows, cols), lambda i, where: (0, where[0], 0)))
            for t in heads_tables
        ],
        [out((sum(t.shape[0] for t in heads_tables), half_rows, cols), BF)],
        scalars=context_index.astype(jnp.int32).reshape(1),
        name="halves",
    )
    ff_half = jnp.stack([my_half(up_weight), my_half(down_weight)])
    attn_full = lax.all_gather(attn_half, ("fsdp", "ctx"), axis=0)
    ff_full = lax.all_gather(ff_half, ("fsdp", "ctx"), axis=0)

    sel_in = lax.dynamic_index_in_dim(attn_adapt_in, mine, 1, keepdims=False)
    sel_out = lax.dynamic_index_in_dim(attn_adapt_out, mine, 1, keepdims=False)
    part_in = lax.dynamic_slice_in_dim(sel_in, head_start, cols, 2)
    part_out = lax.dynamic_slice_in_dim(sel_out, head_start, cols, 2)
    up_in = lax.dynamic_index_in_dim(up_adapt_in, mine, 0, keepdims=False)
    up_out = lax.dynamic_slice(up_adapt_out, (mine, 0, unit_start), (1, rank, units))[0]
    down_in = lax.dynamic_slice(down_adapt_in, (mine, 0, unit_start), (1, rank, units))[0]
    down_out = lax.dynamic_index_in_dim(down_adapt_out, mine, 0, keepdims=False)

    def weight_cols(slot):
        return attn_full, pl.BlockSpec((shards, 1, half_rows, cols), lambda i, *_: (0, slot(i), 0, 0))

    def weight_pair(slot):
        return attn_full, pl.BlockSpec((shards, 1, half_rows, PAIR), lambda p, *_: (0, slot, 0, p))

    def slot_of(table, slot):
        return table, pl.BlockSpec((1,) + table.shape[1:], lambda i, *_: (slot(i), 0, 0))

    def slot_pair(table, slot):
        return table, pl.BlockSpec((1, rank, PAIR), lambda p, *_: (slot, 0, p))

    def whole(array):
        return array, fixed(array)

    def by_pair(count, dtype=BF):
        return shape((count, cols), dtype), pl.BlockSpec((count, PAIR), lambda p, *_: (0, p))

    def kv_pair(array):
        return array, pl.BlockSpec((2, array.shape[1], PAIR), lambda p, *_: (0, 0, p))

    def at(array, first=0):
        return array, pl.BlockSpec((1,) + array.shape[1:], lambda i, *_: (first + i, 0, 0))

    def at_slot(array):
        return array, pl.BlockSpec((1,) + array.shape[1:], lambda i, *_: (0, 0, 0))

    logsum_out = (
        shape((pairs, 2, rows), F32),
        pl.BlockSpec((1, 2, rows), lambda p, *_: (p, 0, 0)),
    )

    def logsum_in(array):
        rest = (0,) * (array.ndim - 1)
        return array, pl.BlockSpec((1,) + array.shape[1:], lambda p, *_: (p, *rest))

    saved_shape = shape((pairs, 2, 2, padded, rows), BF)

    def pair_in(array):
        return array, pl.BlockSpec((array.shape[0], PAIR), lambda p, *_: (0, p))

    regular = (
        ctx_size == 2 and tp_size == 2 and rank == 16
        and width == LANE * fsdp_size and wide == 4 * LANE * fsdp_size
    )

    def ordered(first, *others):
        return lax.optimization_barrier((first, *others))

    def pack(full, part, wides, order, tagged, name, after):
        count = 16 * ((len(order) + 3) // 4 + len(wides))
        dims = (2, fsdp_size, count, LANE)

        def number(arrays):
            return sum(1 if a.ndim == 2 else a.shape[0] for a in arrays)

        keep, send = call(
            partial(pack_kernel, number(full), number(part), order, tagged),
            1,
            [whole(a) for a in full + part + wides],
            [out(dims, F32), out(dims, F32)],
            scalars=scalars,
            name=name,
        )
        recv = swap(send, "ctx")

        def pick(i):
            return lax.dynamic_index_in_dim(keep, i, 0, keepdims=False) + (
                lax.dynamic_index_in_dim(recv, i, 0, keepdims=False)
            )

        kept, away = pick(tensor_index), pick(1 - tensor_index).astype(BF)
        return ordered(kept, away, after)

    def finish(kept, away):
        return lax.all_to_all((kept + away.astype(F32)).astype(BF), "fsdp", 0, 0, tiled=True)

    wide_acc = pltpu.VMEM((rows, width), F32)
    rank_acc = pltpu.VMEM((rows, rank), F32)
    rank_keep = pltpu.VMEM((rows, rank), BF)

    n1, query, self_kv, self_low = call(
        qkv_kernel,
        3,
        [
            whole(hidden),
            whole(ln_gains),
            weight_cols(lambda i: i),
            slot_of(sel_in, lambda i: i),
            slot_of(part_out, lambda i: i),
        ],
        [
            out((rows, width), BF),
            out((rows, cols), BF),
            (
                shape((2, rows, cols), BF),
                pl.BlockSpec((1, rows, cols), lambda i: (jnp.maximum(i - 1, 0), 0, 0)),
            ),
            (shape((3, rows, rank), BF), pl.BlockSpec((1, rows, rank), lambda i: (i, 0, 0))),
        ],
        name="qkv",
    )
    self_kv_other = swap(self_kv, "ctx")
    cross_kv, frames_low = call(
        frames_kernel,
        2,
        [
            whole(encoder),
            weight_cols(lambda i: 4 + i),
            slot_of(sel_in, lambda i: 5 + i),
            slot_of(part_out, lambda i: 5 + i),
        ],
        [
            (
                shape((2, padded, cols), BF),
                pl.BlockSpec((1, padded, cols), lambda i: (i, 0, 0)),
            ),
            (
                shape((2, frames, rank), BF),
                pl.BlockSpec((1, frames, rank), lambda i: (i, 0, 0)),
            ),
        ],
        name="frames",
        cost=7,
    )
    cross_kv_other = swap(cross_kv, "ctx")
    self_mixed, self_logsum, branch, self_o_low = call(
        self_kernel,
        pairs,
        [
            pair_in(query),
            kv_pair(self_kv),
            kv_pair(self_kv_other),
            weight_pair(6),
            slot_pair(part_in, 3),
            slot_of(sel_out, lambda i: 3),
        ],
        [by_pair(rows), logsum_out, out((rows, width), BF), out((rows, rank), BF)],
        [wide_acc, rank_acc],
        scalars,
        name="self_attention",
        cost=7,
    )
    branch, branch_other = with_other(branch, "tp")
    first_mid, n2, cross_q, cross_q_low, cross_mixed, cross_logsum, branch, cross_o_low = call(
        partial(cross_kernel, frames),
        pairs,
        [
            whole(hidden),
            whole(branch),
            whole(branch_other),
            whole(ln_gains),
            weight_pair(3),
            slot_of(sel_in, lambda i: 4),
            slot_pair(part_out, 4),
            kv_pair(cross_kv),
            kv_pair(cross_kv_other),
            weight_pair(7),
            slot_pair(part_in, 7),
            slot_of(sel_out, lambda i: 7),
        ],
        [
            out((rows, width), F32),
            out((rows, width), BF),
            by_pair(rows),
            out((rows, rank), BF),
            by_pair(rows),
            logsum_in(saved_shape),
            out((rows, width), BF),
            out((rows, rank), BF),
        ],
        [wide_acc, rank_acc],
        name="cross_attention",
        cost=13,
    )
    branch, branch_other = with_other(branch, "tp")
    chunk = min(units, 1024)

    def unit_weight(slot):
        return ff_full, pl.BlockSpec((shards, 1, half_rows, chunk), lambda i: (0, slot, 0, i))

    def unit_cols(array):
        return array, pl.BlockSpec((rank, chunk), lambda i: (0, i))

    second_mid, n3, up_low, down_back = call(
        third_norm_kernel,
        1,
        [
            whole(a)
            for a in (
                first_mid, branch, branch_other, ln_gains, cotangent, up_in, down_out
            )
        ],
        [
            out((rows, width), F32),
            out((rows, width), BF),
            out((rows, rank), BF),
            out((rows, rank), BF),
        ],
        name="third_norm",
    )
    branch, grad_n3, up_in_t, up_out_t, down_in_t, down_out_t = call(
        units_kernel,
        units // chunk,
        [
            whole(n3),
            whole(up_low),
            whole(down_back),
            whole(cotangent),
            unit_weight(0),
            unit_weight(1),
            whole(up_in),
            unit_cols(up_out),
            unit_cols(down_in),
            whole(down_out),
        ],
        [
            out((rows, width), BF),
            out((rows, width), BF),
            out((rank, width), F32),
            unit_cols(shape((rank, units), F32)),
            unit_cols(shape((rank, units), F32)),
            out((rank, width), F32),
        ],
        [wide_acc, wide_acc, rank_acc, rank_acc],
        name="units",
        cost=11,
    )
    grad_n3, grad_n3_other = with_other(grad_n3, "tp")
    branch, grad_n3_other = ordered(branch, grad_n3_other)
    branch, branch_other = with_other(branch, "tp")

    def back_call(
        kernel, scalar, carried, middle, grad, grad_other, slots, queries, mixed, kv, kv_other,
        logsum, normed, query_low, low, kind, name, cost,
    ):
        weight_slot, low_slot, query_slot, query_low_slot = slots
        count = kv.shape[1]
        kv_out = (
            shape((2, count, cols), BF),
            pl.BlockSpec((2, count, PAIR), lambda p, *_: (0, 0, p)),
        )
        return call(
            kernel,
            pairs,
            [
                whole(carried),
                whole(middle),
                whole(ln_gains),
                whole(grad),
                whole(grad_other),
                weight_pair(weight_slot),
                slot_pair(part_in, low_slot),
                slot_of(sel_out, lambda i: low_slot),
                weight_pair(query_slot),
                slot_of(sel_in, lambda i: query_low_slot),
                slot_pair(part_out, query_low_slot),
                pair_in(queries),
                pair_in(mixed),
                kv_pair(kv),
                kv_pair(kv_other),
                logsum_in(logsum),
                whole(normed),
                at_slot(query_low),
                whole(low),
            ],
            [
                out((rows, width), F32),
                out((rows, width), kind),
                kv_out,
                kv_out,
                by_pair(rank, F32),
                out((rank, width), F32),
                out((rank, width), F32),
                by_pair(rank, F32),
            ],
            [pltpu.VMEM((rows, width), BF), rank_keep, wide_acc, rank_acc],
            scalar,
            name=name,
            cost=cost,
        )

    grad_second, grad_n2, grad_ckv, grad_ckv_send, co_in_t, co_out_t, cq_in_t, cq_out_t = back_call(
        partial(attention_back, no_limit, 2, frames, True), None, cotangent, second_mid, grad_n3, grad_n3_other, (7, 7, 3, 4),
        cross_q, cross_mixed, cross_kv, cross_kv_other, cross_logsum, n2, cross_q_low[None],
        cross_o_low, BF, "cross_back", 18,
    )
    grad_n2, grad_ckv_send, branch_other = ordered(grad_n2, grad_ckv_send, branch_other)
    grad_n2, grad_n2_other = with_other(grad_n2, "tp")
    grad_ckv_other = swap(grad_ckv_send, "ctx")
    layer_out = (
        second_mid + (branch.astype(F32) + branch_other.astype(F32))
    ).astype(BF)
    block_rows = 128
    grad_frames, ckv_in_t, ckv_out_t = call(
        frames_back_kernel,
        2,
        [
            at(grad_ckv),
            at(grad_ckv_other),
            weight_cols(lambda i: 4 + i),
            slot_of(sel_in, lambda i: 5 + i),
            slot_of(part_out, lambda i: 5 + i),
            whole(encoder),
            at(frames_low),
        ],
        [
            out((frames, width), BF),
            at(shape((2, rank, width), F32)),
            at(shape((2, rank, cols), F32)),
        ],
        [pltpu.VMEM((frames, width), F32)],
        name="frames_back",
        cost=9,
    )
    grad_frames, grad_n2_other = ordered(grad_frames, grad_n2_other)
    grad_frames, grad_frames_other = with_other(grad_frames, "tp")
    grad_first, grad_n1_start, grad_skv, grad_skv_send, so_in_t, so_out_t, q_in_t, q_out_t = back_call(
        partial(self_back_kernel, rows), scalars, grad_second, first_mid, grad_n2, grad_n2_other, (6, 3, 0, 0),
        query, self_mixed, self_kv, self_kv_other, self_logsum, n1, self_low,
        self_o_low, F32, "self_back", 12,
    )
    grad_skv_other = swap(grad_skv_send, "ctx")
    grad_n1, kv_in_t, kv_out_t = call(
        pair_project_kernel,
        2,
        [
            at(grad_skv),
            at(grad_skv_other),
            weight_cols(lambda i: 1 + i),
            slot_of(sel_in, lambda i: 1 + i),
            slot_of(part_out, lambda i: 1 + i),
            whole(n1),
            at(self_low, 1),
            whole(grad_n1_start),
        ],
        [
            out((rows, width), BF),
            at(shape((2, rank, width), F32)),
            at(shape((2, rank, cols), F32)),
        ],
        [wide_acc],
        name="self_project_back",
    )
    grad_n1, grad_n1_other = with_other(grad_n1, "tp")
    def row_blocks(array):
        rest = (0,) * (array.ndim - 1)
        return array, pl.BlockSpec((block_rows,) + array.shape[1:], lambda i: (i, *rest))

    block_rows = 256
    encoder_args = (
        add_rows_kernel,
        -(-frames // block_rows),
        [row_blocks(grad_frames)],
        [row_blocks(shape((frames, 1, width), F32))],
    )

    def encoder_total(other):
        kernel, steps, ins, outs = encoder_args
        (total,) = call(kernel, steps, ins + [row_blocks(other)], outs, name="encoder_total")
        return total

    full = [q_in_t, kv_in_t, cq_in_t, ckv_in_t, so_out_t, co_out_t, up_in_t, down_out_t]
    part = [so_in_t, co_in_t, q_out_t, kv_out_t, cq_out_t, ckv_out_t]
    if regular:
        order = (0, 1, 2, 10, 3, 4, 5, 11, 12, 13, 14, 6, 15, 16, 17, 7, 8, 9)
        full[0], layer_out = ordered(q_in_t, layer_out)
        kept, away, grad_frames_other = pack(
            full, part, [up_out_t, down_in_t], order, 1, "pack", grad_frames_other
        )
        grad_encoder = encoder_total(grad_frames_other)
        away, grad_encoder = ordered(swap(away, "tp"), grad_encoder)
        parts = finish(kept, away)
        narrow_out = (attn_adapt_in.shape[0], adapters, rank, PIECE)
        tables = call(
            unpack_kernel,
            1,
            [whole(parts)],
            [
                out(narrow_out, F32),
                out(narrow_out, F32),
                out((adapters, rank, PIECE), F32),
                out((adapters, rank, LANE), F32),
                out((adapters, rank, LANE), F32),
                out((adapters, rank, PIECE), F32),
            ],
            name="unpack",
        )
    else:
        grad_encoder = encoder_total(grad_frames_other)
        chosen = (mine == jnp.arange(adapters, dtype=jnp.int32)).astype(F32)

        def summed(parts, start, full):
            parts = [t for p in parts for t in ([p] if p.ndim == 2 else [p[0], p[1]])]

            def spread_out(part):
                if part.shape[1] == full:
                    return part
                blank = jnp.zeros((part.shape[0], full), F32)
                return lax.dynamic_update_slice_in_dim(blank, part, start, axis=1)

            stacked = jnp.stack([spread_out(p) for p in parts])
            table = chosen[None, :, None, None] * stacked[:, None]
            return lax.psum_scatter(
                table, ("fsdp", "ctx", "tp"), scatter_dimension=3, tiled=True
            )

        attn_in_t = summed(
            [q_in_t, kv_in_t, so_in_t, cq_in_t, ckv_in_t, co_in_t], head_start, width
        )
        attn_out_t = summed(
            [q_out_t, kv_out_t, so_out_t, cq_out_t, ckv_out_t, co_out_t], head_start, width
        )
        small = summed([up_in_t, down_out_t], head_start, width)
        large = summed([up_out_t, down_in_t], unit_start, wide)
        tables = (attn_in_t, attn_out_t, small[0], large[0], large[1], small[1])
    grad_encoder = grad_encoder.reshape(frames, width)
    (grad_hidden,) = call(
        close_kernel,
        1,
        [whole(a) for a in (hidden, ln_gains, grad_first, grad_n1, grad_n1_other)],
        [out((rows, width), F32)],
        name="hidden_total",
    )
    return (
        layer_out[None],
        grad_hidden[None],
        grad_encoder[None],
        *tables,
    )
def solution(mesh):
    in_specs = (
        P("fsdp", "ctx", None),
        P("fsdp", "ctx", None),
        P("fsdp", "ctx", None),
        P("fsdp"),
        P(),
        P(None, "fsdp", "tp"),
        P(None, "fsdp", "tp"),
        P("fsdp", "tp"),
        P("fsdp", "tp"),
        P(),
        P(),
        P(),
        P(),
        P(),
        P(),
    )
    out_specs = (
        P("fsdp", "ctx", None),
        P("fsdp", "ctx", None),
        P("fsdp", "ctx", None),
        P(None, None, None, ("fsdp", "ctx", "tp")),
        P(None, None, None, ("fsdp", "ctx", "tp")),
        P(None, None, ("fsdp", "ctx", "tp")),
        P(None, None, ("fsdp", "ctx", "tp")),
        P(None, None, ("fsdp", "ctx", "tp")),
        P(None, None, ("fsdp", "ctx", "tp")),
    )
    return jax.shard_map(
        on_device, mesh=mesh, in_specs=in_specs, out_specs=out_specs, check_vma=False
    )
```

```python
from functools import partial

import jax
import jax.numpy as jnp
from jax import lax
from jax.experimental import pallas as pl
from jax.experimental.pallas import tpu as pltpu
from jax.sharding import PartitionSpec as P

HEAD_DIM = 64
PAIR = 2 * HEAD_DIM
EPSILON = 1e-05
MASKED_SCORE = -1000000000.0
SCALE = HEAD_DIM ** (-0.5)
BF = jnp.bfloat16
F32 = jnp.float32


def mm(a, b):
    return lax.dot_general(a, b, (((1,), (0,)), ((), ())), preferred_element_type=F32)


def mm_nt(a, b):
    return lax.dot_general(a, b, (((1,), (1,)), ((), ())), preferred_element_type=F32)


def mm_tn(a, b):
    return lax.dot_general(a, b, (((0,), (0,)), ((), ())), preferred_element_type=F32)


def norm_parts(rows):
    centred = rows - jnp.mean(rows, axis=-1, keepdims=True)
    spread = jnp.mean(centred * centred, axis=-1, keepdims=True)
    inverse = lax.rsqrt(spread + EPSILON)
    return centred * inverse, inverse


def normalize(rows, gain):
    return norm_parts(rows)[0] * gain


def normalize_back(rows, gain, gradient):
    unit, inverse = norm_parts(rows)
    scaled = gradient * gain
    first = jnp.mean(scaled, axis=-1, keepdims=True)
    second = jnp.mean(scaled * unit, axis=-1, keepdims=True)
    return (scaled - first - unit * second) * inverse


def swap(value, axis):
    return lax.ppermute(value, axis, [(0, 1), (1, 0)])


def with_other(partial_value, axis):
    if lax.axis_size(axis) == 2:
        return partial_value, swap(partial_value, axis)
    return lax.psum(partial_value, axis), jnp.zeros_like(partial_value)


def matrix(ref):
    block = ref[...]
    return block.reshape(block.shape[0] * block.shape[2], block.shape[3])


def half_masks(rows):
    lane = lax.broadcasted_iota(jnp.int32, (rows, PAIR), 1)
    return lane < HEAD_DIM, lane >= HEAD_DIM


def pick_half(rows, keep):
    return jnp.where(keep, rows, jnp.zeros_like(rows))


def join_halves(first, second):
    row = lax.broadcasted_iota(jnp.int32, first.shape, 0)
    return jnp.where(row < HEAD_DIM, first, second).T


def pair_forward(queries, keys, values, limit, saved=None):
    mixed, logsums = [], []
    turned = [v.T for v in values]
    for half, keep in enumerate(half_masks(queries.shape[0])):
        mine = pick_half(queries, keep) * BF(SCALE)
        scores = [limit(i, mm_nt(k, mine)) for i, k in enumerate(keys)]
        top = jnp.max(scores[0], axis=0, keepdims=True)
        for s in scores[1:]:
            top = jnp.maximum(top, jnp.max(s, axis=0, keepdims=True))
        powers = [jnp.exp(s - top) for s in scores]
        total = sum(jnp.sum(e, axis=0, keepdims=True) for e in powers)
        share = 1.0 / total
        weights = [(e * share).astype(BF) for e in powers]
        if saved is not None:
            for i, w in enumerate(weights):
                saved[0, half, i, : w.shape[0]] = w
        mixed.append(sum(mm(v, w) for v, w in zip(turned, weights)))
        logsums.append(top + jnp.log(total))
    return join_halves(*mixed), logsums


def pair_backward(grad, mixed, queries, keys, values, logsums, limit, saved=None):
    grad_query, grad_keys, grad_values = [], [0.0] * len(keys), [0.0] * len(keys)
    inners = (grad.astype(F32) * mixed.astype(F32)).T
    turned = [k.T for k in keys]
    for half, (keep, logsum) in enumerate(zip(half_masks(queries.shape[0]), logsums)):
        mine = pick_half(queries, keep) * BF(SCALE)
        grad_mine = pick_half(grad, keep)
        at = HEAD_DIM * half
        inner = jnp.sum(inners[at : at + HEAD_DIM], axis=0, keepdims=True)
        part = 0.0
        for i, (key, value) in enumerate(zip(keys, values)):
            if saved is None:
                weights = jnp.exp(limit(i, mm_nt(key, mine)) - logsum)
                rounded = weights.astype(BF)
            else:
                rounded = saved[0, half, i, : key.shape[0]]
                weights = rounded.astype(F32)
            grad_scores = (weights * (mm_nt(value, grad_mine) - inner)).astype(BF)
            part = part + mm(turned[i], grad_scores)
            grad_keys[i] = grad_keys[i] + mm(grad_scores, mine)
            grad_values[i] = grad_values[i] + mm(rounded, grad_mine)
        grad_query.append(part)
    return (
        (join_halves(*grad_query) * SCALE).astype(BF),
        [g.astype(BF) for g in grad_keys],
        [g.astype(BF) for g in grad_values],
    )


def no_limit(index, scores):
    return scores


def causal_limit(context):
    def limit(index, scores):
        if index == 0:
            key = lax.broadcasted_iota(jnp.int32, scores.shape, 0)
            query = lax.broadcasted_iota(jnp.int32, scores.shape, 1)
            return jnp.where(key <= query, scores, MASKED_SCORE)
        return jnp.where(context == 1, scores, MASKED_SCORE)

    return limit


def at_first(step=0):
    return pl.when(pl.program_id(0) == step)


def at_last():
    return pl.when(pl.program_id(0) == pl.num_programs(0) - 1)


def halves_kernel(where, inputs, outputs, joined):
    count = inputs.shape[0]
    joined[:count] = inputs[...]
    joined[count:] = outputs[...]


def qkv_kernel(hidden, gains, weight, low_in, low_out, normed, query, key_value, low):
    @at_first()
    def _():
        normed[...] = normalize(hidden[...].astype(F32), gains[0:1, :]).astype(BF)

    rows = normed[...]
    rank_rows = mm_nt(rows, low_in[0]).astype(BF)
    low[0] = rank_rows
    value = (mm(rows, matrix(weight)) + mm(rank_rows, low_out[0])).astype(BF)

    @at_first()
    def _():
        query[...] = value

    @pl.when(pl.program_id(0) > 0)
    def _():
        key_value[0] = value


def frames_kernel(frames, weight, low_in, low_out, key_value, low):
    rows = frames[...]
    rank_rows = mm_nt(rows, low_in[0]).astype(BF)
    low[0] = rank_rows
    count = rows.shape[0]
    key_value[0, :count] = (mm(rows, matrix(weight)) + mm(rank_rows, low_out[0])).astype(BF)
    spare = key_value.shape[1] - count
    if spare:
        key_value[0, count:] = jnp.zeros((spare, key_value.shape[2]), BF)


def self_kernel(
    where, query, mine, other, weight, low_in, low_out, mixed, logsum, branch, low, acc, low_acc
):
    @at_first()
    def _():
        acc[...] = jnp.zeros_like(acc)
        low_acc[...] = jnp.zeros_like(low_acc)

    out, logs = pair_forward(
        query[...], (mine[0], other[0]), (mine[1], other[1]), causal_limit(where[0])
    )
    out = out.astype(BF)
    mixed[...] = out
    logsum[0, 0:1, :] = logs[0]
    logsum[0, 1:2, :] = logs[1]
    acc[...] += mm_nt(out, matrix(weight))
    low_acc[...] += mm_nt(out, low_in[0])

    @at_last()
    def _():
        rank_rows = low_acc[...].astype(BF)
        low[...] = rank_rows
        branch[...] = (acc[...] + mm(rank_rows, low_out[0])).astype(BF)


def cross_kernel(
    count,
    hidden, branch_mine, branch_other, gains, query_weight, query_in, query_out, mine, other,
    weight, low_in, low_out,
    middle, normed, query, query_low, mixed, saved, branch, low, acc, low_acc,
):
    @at_first()
    def _():
        acc[...] = jnp.zeros_like(acc)
        low_acc[...] = jnp.zeros_like(low_acc)
        total = hidden[...].astype(F32) + (
            branch_mine[...].astype(F32) + branch_other[...].astype(F32)
        )
        middle[...] = total
        rows = normalize(total, gains[1:2, :]).astype(BF)
        normed[...] = rows
        query_low[...] = mm_nt(rows, query_in[0]).astype(BF)

    queries = (
        mm(normed[...], matrix(query_weight)) + mm(query_low[...], query_out[0])
    ).astype(BF)
    query[...] = queries
    out, _ = pair_forward(
        queries,
        (mine[0, :count], other[0, :count]),
        (mine[1, :count], other[1, :count]),
        no_limit,
        saved,
    )
    out = out.astype(BF)
    mixed[...] = out
    acc[...] += mm_nt(out, matrix(weight))
    low_acc[...] += mm_nt(out, low_in[0])

    @at_last()
    def _():
        rank_rows = low_acc[...].astype(BF)
        low[...] = rank_rows
        branch[...] = (acc[...] + mm(rank_rows, low_out[0])).astype(BF)


def third_norm_kernel(
    middle, branch_mine, branch_other, gains, cotangent, up_in, down_out,
    second, normed, up_low, down_back,
):
    total = middle[...] + (branch_mine[...].astype(F32) + branch_other[...].astype(F32))
    second[...] = total
    rows = normalize(total, gains[2:3, :]).astype(BF)
    normed[...] = rows
    up_low[...] = mm_nt(rows, up_in[...]).astype(BF)
    down_back[...] = mm_nt(cotangent[...], down_out[...]).astype(BF)


def units_kernel(
    normed, up_low, down_back, cotangent, up, down, up_in, up_out, down_in,
    grad_normed, table_up_in, active, grad_units,
    back, back_low,
):
    @at_first()
    def _():
        back[...] = jnp.zeros_like(back)
        back_low[...] = jnp.zeros_like(back_low)

    up_rows = matrix(up)
    value = mm(normed[...], up_rows) + mm(up_low[...], up_out[...])
    spread = 1.0 + lax.erf(value * 0.7071067811865476)
    active[...] = (0.5 * value * spread).astype(BF)
    slope = 0.5 * spread + value * (0.3989422804014327 * jnp.exp(-0.5 * value * value))
    grad_act = mm(cotangent[...], matrix(down)) + mm(down_back[...], down_in[...])
    grad = (grad_act * slope).astype(BF)
    grad_units[...] = grad
    back[...] += mm_nt(grad, up_rows)
    back_low[...] += mm_nt(grad, up_out[...])

    @at_last()
    def _():
        up_back = back_low[...].astype(BF)
        grad_normed[...] = (back[...] + mm(up_back, up_in[...])).astype(BF)
        table_up_in[...] = mm_tn(up_back, normed[...])


def units_out_kernel(
    active, grad_units, up_low, down_back, cotangent, down, down_in, down_out,
    branch, table_up_out, table_down_in, table_down_out,
    acc, low_acc,
):
    @at_first()
    def _():
        acc[...] = jnp.zeros_like(acc)
        low_acc[...] = jnp.zeros_like(low_acc)

    act = active[...]
    acc[...] += mm_nt(act, matrix(down))
    low_acc[...] += mm_nt(act, down_in[...])
    table_up_out[...] = mm_tn(up_low[...], grad_units[...])
    table_down_in[...] = mm_tn(down_back[...], act)

    @at_last()
    def _():
        down_low = low_acc[...].astype(BF)
        branch[...] = (acc[...] + mm(down_low, down_out[...])).astype(BF)
        table_down_out[...] = mm_tn(down_low, cotangent[...])


def attention_back(
    limit, slot, count, stored, carried, rows, gains, grad_mine, grad_other, weight, low_in, low_out,
    query_weight, query_in, query_out, query, mixed, mine, other, logsum, normed, query_low, low,
    carry, grad_normed, grad_kv, grad_kv_other,
    table_in, table_out, table_query_in, table_query_out,
    narrow, back_low, acc, query_back,
):
    @at_first()
    def _():
        total = carried[...].astype(F32) + normalize_back(
            rows[...],
            gains[slot : slot + 1, :],
            grad_mine[...].astype(F32) + grad_other[...].astype(F32),
        )
        carry[...] = total
        narrow[...] = total.astype(BF)
        back_low[...] = mm_nt(narrow[...], low_out[0]).astype(BF)
        acc[...] = jnp.zeros_like(acc)
        query_back[...] = jnp.zeros_like(query_back)
        table_out[...] = mm_tn(low[...], narrow[...])

    grad = (mm(narrow[...], matrix(weight)) + mm(back_low[...], low_in[0])).astype(BF)
    table_in[...] = mm_tn(back_low[...], mixed[...])
    grad_query, grad_keys, grad_values = pair_backward(
        grad,
        mixed[...],
        query[...],
        (mine[0, :count], other[0, :count]),
        (mine[1, :count], other[1, :count]),
        (None, None) if stored else (logsum[0, 0:1, :], logsum[0, 1:2, :]),
        limit,
        logsum if stored else None,
    )
    for which, (first, second) in enumerate((grad_keys, grad_values)):
        grad_kv[which, :count] = first
        grad_kv_other[which, :count] = second
        spare = grad_kv.shape[1] - count
        if spare:
            grad_kv[which, count:] = jnp.zeros((spare, PAIR), BF)
            grad_kv_other[which, count:] = jnp.zeros((spare, PAIR), BF)
    acc[...] += mm_nt(grad_query, matrix(query_weight))
    query_back[...] += mm_nt(grad_query, query_out[0])
    table_query_out[...] = mm_tn(query_low[0], grad_query)

    @at_last()
    def _():
        rank_rows = query_back[...].astype(BF)
        total = acc[...] + mm(rank_rows, query_in[0])
        grad_normed[...] = total.astype(grad_normed.dtype)
        table_query_in[...] = mm_tn(rank_rows, normed[...])


def self_back_kernel(count, where, *refs):
    attention_back(causal_limit(where[0]), 1, count, False, *refs)


def pair_project_kernel(
    grad_mine, grad_other, weight, low_in, low_out, rows, low, start, total, table_in, table_out,
    acc,
):
    @at_first()
    def _():
        acc[...] = start[...]

    pair_project_step(
        grad_mine, grad_other, weight, low_in, low_out, rows, low, table_in, table_out, acc
    )

    @at_last()
    def _():
        total[...] = acc[...].astype(BF)


def close_kernel(hidden, gains, carried, grad_mine, grad_other, total):
    total[...] = carried[...] + normalize_back(
        hidden[...].astype(F32),
        gains[0:1, :],
        grad_mine[...].astype(F32) + grad_other[...].astype(F32),
    )


def add_rows_kernel(mine, other, *refs):
    total = refs[-1]
    value = mine[...].astype(F32) + other[...].astype(F32)
    total[...] = value[:, None, :]


def frames_back_kernel(
    grad_mine, grad_other, weight, low_in, low_out, rows, low, total, table_in, table_out, acc
):
    @at_first()
    def _():
        acc[...] = jnp.zeros_like(acc)

    pair_project_step(
        grad_mine, grad_other, weight, low_in, low_out, rows, low, table_in, table_out, acc
    )

    @at_last()
    def _():
        total[...] = acc[...].astype(BF)


def pair_project_step(
    grad_mine, grad_other, weight, low_in, low_out, rows, low, table_in, table_out, acc
):
    count = rows.shape[0]
    grad = (grad_mine[0, :count].astype(F32) + grad_other[0, :count].astype(F32)).astype(BF)
    rank_rows = mm_nt(grad, low_out[0]).astype(BF)
    acc[...] += mm_nt(grad, matrix(weight)) + mm(rank_rows, low_in[0])
    table_in[0] = mm_tn(rank_rows, rows[...])
    table_out[0] = mm_tn(low[0], grad)


LANE = 128
PIECE = 32


def pack_kernel(fulls, shares, order, tagged, *refs):
    where = refs[0]
    keep, send = refs[-2:]
    flat = []
    for ref in refs[1:-2]:
        flat += [ref] if len(ref.shape) == 2 else [ref.at[i] for i in range(ref.shape[0])]
    tables, broad = flat[: fulls + shares], flat[fulls + shares :]
    context, tensor = where[0], where[1]
    blocks = keep.shape[1]
    per_group = (len(order) + 3) // 4
    rows = per_group * 16
    lane = lax.broadcasted_iota(jnp.int32, (rows, LANE), 1) // PIECE
    padded = list(order) + [None] * (4 * per_group - len(order))

    def one_block(f, carry):
        shard = f // (blocks // 2)
        local = f - shard * (blocks // 2)
        owned = tensor == shard

        def table_of(k):
            if k is None:
                return jnp.zeros((16, LANE), F32)
            if k < fulls:
                return tables[k][:, pl.ds(pl.multiple_of(f * LANE, LANE), LANE)]
            part = tables[k][:, pl.ds(pl.multiple_of(local * LANE, LANE), LANE)]
            return jnp.where(owned, part, 0.0)

        groups = [
            jnp.concatenate(
                [table_of(k) for k in padded[g * per_group : (g + 1) * per_group]], axis=0
            )
            for g in range(4)
        ]
        for target, side in ((keep, context), (send, 1 - context)):
            for t in range(2):
                p = 2 * side + t
                value = jnp.zeros((rows, LANE), F32)
                for g in range(4):
                    turned = pltpu.roll(groups[g], (PIECE * (g + 4 - p)) % LANE, 1)
                    value = jnp.where(lane == g, turned, value)
                if tagged:
                    spare = 4 * per_group - len(order)
                    tag = where[2].astype(F32) * 0.25
                    low = rows - 16 * spare
                    at_row = lax.broadcasted_iota(jnp.int32, (rows, LANE), 0)
                    value = jnp.where((lane == 3) & (at_row >= low), tag, value)
                target[t, f, :rows] = value
                row = rows
                for w in broad:
                    at = pl.multiple_of(local * 4 * LANE + p * LANE, LANE)
                    target[t, f, row : row + 16] = jnp.where(owned, w[:, pl.ds(at, LANE)], 0.0)
                    row += 16
        return carry

    lax.fori_loop(0, blocks, one_block, 0)


def unpack_kernel(parts, attn_in, attn_out, up_in, up_out, down_in, down_out):
    projections, adapters = attn_in.shape[:2]
    clips, rows = parts.shape[:2]
    per_group = (2 * projections + 2 + 3) // 4
    narrow = 16 * per_group

    tags = []
    for c in range(clips):
        tag = parts[c, narrow - 16 : narrow, 3 * PIECE :].astype(F32)[0:1, 0:1]
        tags.append(jnp.broadcast_to(tag, (1, LANE)))

    def one(a, carry):
        adapter = a.astype(F32)
        block = jnp.zeros((rows, LANE), F32)
        for c in range(clips):
            same = (tags[c] > adapter - 0.5) & (tags[c] < adapter + 0.5)
            weight = jnp.where(same, 1.0, 0.0)
            block = block + parts[c].astype(F32) * weight

        def piece(k):
            g, at = k // per_group, 16 * (k % per_group)
            return block[at : at + 16, PIECE * g : PIECE * (g + 1)]

        for j in range(projections):
            attn_in[j, a] = piece(j)
            attn_out[j, a] = piece(projections + j)
        up_in[a] = piece(2 * projections)
        down_out[a] = piece(2 * projections + 1)
        up_out[a] = block[narrow : narrow + 16]
        down_in[a] = block[narrow + 16 : narrow + 32]
        return carry

    lax.fori_loop(0, adapters, one, 0)


def shape(dims, dtype):
    return jax.ShapeDtypeStruct(tuple(dims), dtype)


def fixed(array):
    zeros = (0,) * array.ndim
    return pl.BlockSpec(array.shape, lambda *_: zeros)


def fixed_out(*dims):
    zeros = (0,) * len(dims)
    return pl.BlockSpec(dims, lambda *_: zeros)


def call(kernel, steps, ins, outs, scratch=(), scalars=None, name=None, cost=5, aliases=None):
    arrays = [a for a, _ in ins]
    spec = pltpu.PrefetchScalarGridSpec(
        num_scalar_prefetch=0 if scalars is None else 1,
        grid=(steps,),
        in_specs=[s for _, s in ins],
        out_specs=[s for _, s in outs],
        scratch_shapes=list(scratch),
    )
    run = pl.pallas_call(
        kernel,
        grid_spec=spec,
        out_shape=[o for o, _ in outs],
        compiler_params=pltpu.CompilerParams(dimension_semantics=("arbitrary",)),
        cost_estimate=pl.CostEstimate(
            flops=cost * 10_000_000, transcendentals=0, bytes_accessed=cost * 36_900
        ),
        input_output_aliases=aliases or {},
        name=name,
    )
    return run(*arrays) if scalars is None else run(scalars, *arrays)


def on_device(
    hidden,
    encoder,
    cotangent,
    adapter_index,
    ln_gains,
    attn_in_weight,
    attn_out_weight,
    up_weight,
    down_weight,
    attn_adapt_in,
    attn_adapt_out,
    up_adapt_in,
    up_adapt_out,
    down_adapt_in,
    down_adapt_out,
):
    fsdp_size = lax.axis_size("fsdp")
    ctx_size = lax.axis_size("ctx")
    tp_size = lax.axis_size("tp")
    tensor_index = lax.axis_index("tp")
    context_index = lax.axis_index("ctx")
    hidden, encoder, cotangent = hidden[0], encoder[0], cotangent[0]
    rows, width = hidden.shape
    frames = encoder.shape[0]
    padded = -(-frames // 16) * 16
    wide = up_adapt_out.shape[2]
    cols = attn_in_weight.shape[2]
    units = up_weight.shape[1]
    rank = attn_adapt_in.shape[2]
    adapters = attn_adapt_in.shape[1]
    pairs = cols // PAIR
    head_start = tensor_index * cols
    unit_start = tensor_index * units
    mine = adapter_index[0]
    scalars = jnp.stack(
        [context_index.astype(jnp.int32), tensor_index.astype(jnp.int32), mine]
    )

    def out(dims, dtype):
        return shape(dims, dtype), fixed_out(*dims)

    half_rows = attn_in_weight.shape[1] // ctx_size
    shards = fsdp_size * ctx_size

    def my_half(table):
        return lax.dynamic_slice_in_dim(
            table, context_index * half_rows, half_rows, axis=table.ndim - 2
        )

    heads_tables = (attn_in_weight, attn_out_weight)
    (attn_half,) = call(
        halves_kernel,
        1,
        [
            (t, pl.BlockSpec((t.shape[0], half_rows, cols), lambda i, where: (0, where[0], 0)))
            for t in heads_tables
        ],
        [out((sum(t.shape[0] for t in heads_tables), half_rows, cols), BF)],
        scalars=context_index.astype(jnp.int32).reshape(1),
        name="halves",
    )
    ff_half = jnp.stack([my_half(up_weight), my_half(down_weight)])
    attn_full = lax.all_gather(attn_half, ("fsdp", "ctx"), axis=0)
    ff_full = lax.all_gather(ff_half, ("fsdp", "ctx"), axis=0)

    sel_in = lax.dynamic_index_in_dim(attn_adapt_in, mine, 1, keepdims=False)
    sel_out = lax.dynamic_index_in_dim(attn_adapt_out, mine, 1, keepdims=False)
    part_in = lax.dynamic_slice_in_dim(sel_in, head_start, cols, 2)
    part_out = lax.dynamic_slice_in_dim(sel_out, head_start, cols, 2)
    up_in = lax.dynamic_index_in_dim(up_adapt_in, mine, 0, keepdims=False)
    up_out = lax.dynamic_slice(up_adapt_out, (mine, 0, unit_start), (1, rank, units))[0]
    down_in = lax.dynamic_slice(down_adapt_in, (mine, 0, unit_start), (1, rank, units))[0]
    down_out = lax.dynamic_index_in_dim(down_adapt_out, mine, 0, keepdims=False)

    def weight_cols(slot):
        return attn_full, pl.BlockSpec((shards, 1, half_rows, cols), lambda i, *_: (0, slot(i), 0, 0))

    def weight_pair(slot):
        return attn_full, pl.BlockSpec((shards, 1, half_rows, PAIR), lambda p, *_: (0, slot, 0, p))

    def slot_of(table, slot):
        return table, pl.BlockSpec((1,) + table.shape[1:], lambda i, *_: (slot(i), 0, 0))

    def slot_pair(table, slot):
        return table, pl.BlockSpec((1, rank, PAIR), lambda p, *_: (slot, 0, p))

    def whole(array):
        return array, fixed(array)

    def by_pair(count, dtype=BF):
        return shape((count, cols), dtype), pl.BlockSpec((count, PAIR), lambda p, *_: (0, p))

    def kv_pair(array):
        return array, pl.BlockSpec((2, array.shape[1], PAIR), lambda p, *_: (0, 0, p))

    def at(array, first=0):
        return array, pl.BlockSpec((1,) + array.shape[1:], lambda i, *_: (first + i, 0, 0))

    def at_slot(array):
        return array, pl.BlockSpec((1,) + array.shape[1:], lambda i, *_: (0, 0, 0))

    logsum_out = (
        shape((pairs, 2, rows), F32),
        pl.BlockSpec((1, 2, rows), lambda p, *_: (p, 0, 0)),
    )

    def logsum_in(array):
        rest = (0,) * (array.ndim - 1)
        return array, pl.BlockSpec((1,) + array.shape[1:], lambda p, *_: (p, *rest))

    saved_shape = shape((pairs, 2, 2, padded, rows), BF)

    def pair_in(array):
        return array, pl.BlockSpec((array.shape[0], PAIR), lambda p, *_: (0, p))

    regular = (
        ctx_size == 2 and tp_size == 2 and rank == 16
        and width == LANE * fsdp_size and wide == 4 * LANE * fsdp_size
    )

    def ordered(first, *others):
        return lax.optimization_barrier((first, *others))

    def pack(full, part, wides, order, tagged, name, after):
        count = 16 * ((len(order) + 3) // 4 + len(wides))
        dims = (2, fsdp_size, count, LANE)

        def number(arrays):
            return sum(1 if a.ndim == 2 else a.shape[0] for a in arrays)

        keep, send = call(
            partial(pack_kernel, number(full), number(part), order, tagged),
            1,
            [whole(a) for a in full + part + wides],
            [out(dims, F32), out(dims, F32)],
            scalars=scalars,
            name=name,
        )
        recv = swap(send, "ctx")

        def pick(i):
            return lax.dynamic_index_in_dim(keep, i, 0, keepdims=False) + (
                lax.dynamic_index_in_dim(recv, i, 0, keepdims=False)
            )

        kept, away = pick(tensor_index), pick(1 - tensor_index).astype(BF)
        return ordered(kept, away, after)

    def finish(kept, away):
        return lax.all_to_all((kept + away.astype(F32)).astype(BF), "fsdp", 0, 0, tiled=True)

    wide_acc = pltpu.VMEM((rows, width), F32)
    rank_acc = pltpu.VMEM((rows, rank), F32)
    rank_keep = pltpu.VMEM((rows, rank), BF)

    n1, query, self_kv, self_low = call(
        qkv_kernel,
        3,
        [
            whole(hidden),
            whole(ln_gains),
            weight_cols(lambda i: i),
            slot_of(sel_in, lambda i: i),
            slot_of(part_out, lambda i: i),
        ],
        [
            out((rows, width), BF),
            out((rows, cols), BF),
            (
                shape((2, rows, cols), BF),
                pl.BlockSpec((1, rows, cols), lambda i: (jnp.maximum(i - 1, 0), 0, 0)),
            ),
            (shape((3, rows, rank), BF), pl.BlockSpec((1, rows, rank), lambda i: (i, 0, 0))),
        ],
        name="qkv",
    )
    self_kv_other = swap(self_kv, "ctx")
    cross_kv, frames_low = call(
        frames_kernel,
        2,
        [
            whole(encoder),
            weight_cols(lambda i: 4 + i),
            slot_of(sel_in, lambda i: 5 + i),
            slot_of(part_out, lambda i: 5 + i),
        ],
        [
            (
                shape((2, padded, cols), BF),
                pl.BlockSpec((1, padded, cols), lambda i: (i, 0, 0)),
            ),
            (
                shape((2, frames, rank), BF),
                pl.BlockSpec((1, frames, rank), lambda i: (i, 0, 0)),
            ),
        ],
        name="frames",
        cost=7,
    )
    cross_kv_other = swap(cross_kv, "ctx")
    self_mixed, self_logsum, branch, self_o_low = call(
        self_kernel,
        pairs,
        [
            pair_in(query),
            kv_pair(self_kv),
            kv_pair(self_kv_other),
            weight_pair(6),
            slot_pair(part_in, 3),
            slot_of(sel_out, lambda i: 3),
        ],
        [by_pair(rows), logsum_out, out((rows, width), BF), out((rows, rank), BF)],
        [wide_acc, rank_acc],
        scalars,
        name="self_attention",
        cost=7,
    )
    branch, branch_other = with_other(branch, "tp")
    first_mid, n2, cross_q, cross_q_low, cross_mixed, cross_logsum, branch, cross_o_low = call(
        partial(cross_kernel, frames),
        pairs,
        [
            whole(hidden),
            whole(branch),
            whole(branch_other),
            whole(ln_gains),
            weight_pair(3),
            slot_of(sel_in, lambda i: 4),
            slot_pair(part_out, 4),
            kv_pair(cross_kv),
            kv_pair(cross_kv_other),
            weight_pair(7),
            slot_pair(part_in, 7),
            slot_of(sel_out, lambda i: 7),
        ],
        [
            out((rows, width), F32),
            out((rows, width), BF),
            by_pair(rows),
            out((rows, rank), BF),
            by_pair(rows),
            logsum_in(saved_shape),
            out((rows, width), BF),
            out((rows, rank), BF),
        ],
        [wide_acc, rank_acc],
        name="cross_attention",
        cost=13,
    )
    branch, branch_other = with_other(branch, "tp")
    chunk = min(units, 1024)

    def unit_weight(slot):
        return ff_full, pl.BlockSpec((shards, 1, half_rows, chunk), lambda i: (0, slot, 0, i))

    def unit_cols(array):
        return array, pl.BlockSpec((rank, chunk), lambda i: (0, i))

    second_mid, n3, up_low, down_back = call(
        third_norm_kernel,
        1,
        [
            whole(a)
            for a in (
                first_mid, branch, branch_other, ln_gains, cotangent, up_in, down_out
            )
        ],
        [
            out((rows, width), F32),
            out((rows, width), BF),
            out((rows, rank), BF),
            out((rows, rank), BF),
        ],
        name="third_norm",
    )
    def unit_rows(array):
        return array, pl.BlockSpec((rows, chunk), lambda i: (0, i))

    grad_n3, up_in_t, active, grad_units = call(
        units_kernel,
        units // chunk,
        [
            whole(n3),
            whole(up_low),
            whole(down_back),
            whole(cotangent),
            unit_weight(0),
            unit_weight(1),
            whole(up_in),
            unit_cols(up_out),
            unit_cols(down_in),
        ],
        [
            out((rows, width), BF),
            out((rank, width), F32),
            unit_rows(shape((rows, units), BF)),
            unit_rows(shape((rows, units), BF)),
        ],
        [wide_acc, rank_acc],
        name="units",
        cost=11,
    )
    branch, up_out_t, down_in_t, down_out_t = call(
        units_out_kernel,
        units // chunk,
        [
            unit_rows(active),
            unit_rows(grad_units),
            whole(up_low),
            whole(down_back),
            whole(cotangent),
            unit_weight(1),
            unit_cols(down_in),
            whole(down_out),
        ],
        [
            out((rows, width), BF),
            unit_cols(shape((rank, units), F32)),
            unit_cols(shape((rank, units), F32)),
            out((rank, width), F32),
        ],
        [wide_acc, rank_acc],
        name="units_out",
    )
    grad_n3, grad_n3_other = with_other(grad_n3, "tp")
    branch, grad_n3_other = ordered(branch, grad_n3_other)
    branch, branch_other = with_other(branch, "tp")

    def back_call(
        kernel, scalar, carried, middle, grad, grad_other, slots, queries, mixed, kv, kv_other,
        logsum, normed, query_low, low, kind, name, cost,
    ):
        weight_slot, low_slot, query_slot, query_low_slot = slots
        count = kv.shape[1]
        kv_out = (
            shape((2, count, cols), BF),
            pl.BlockSpec((2, count, PAIR), lambda p, *_: (0, 0, p)),
        )
        return call(
            kernel,
            pairs,
            [
                whole(carried),
                whole(middle),
                whole(ln_gains),
                whole(grad),
                whole(grad_other),
                weight_pair(weight_slot),
                slot_pair(part_in, low_slot),
                slot_of(sel_out, lambda i: low_slot),
                weight_pair(query_slot),
                slot_of(sel_in, lambda i: query_low_slot),
                slot_pair(part_out, query_low_slot),
                pair_in(queries),
                pair_in(mixed),
                kv_pair(kv),
                kv_pair(kv_other),
                logsum_in(logsum),
                whole(normed),
                at_slot(query_low),
                whole(low),
            ],
            [
                out((rows, width), F32),
                out((rows, width), kind),
                kv_out,
                kv_out,
                by_pair(rank, F32),
                out((rank, width), F32),
                out((rank, width), F32),
                by_pair(rank, F32),
            ],
            [pltpu.VMEM((rows, width), BF), rank_keep, wide_acc, rank_acc],
            scalar,
            name=name,
            cost=cost,
        )

    grad_second, grad_n2, grad_ckv, grad_ckv_send, co_in_t, co_out_t, cq_in_t, cq_out_t = back_call(
        partial(attention_back, no_limit, 2, frames, True), None, cotangent, second_mid, grad_n3, grad_n3_other, (7, 7, 3, 4),
        cross_q, cross_mixed, cross_kv, cross_kv_other, cross_logsum, n2, cross_q_low[None],
        cross_o_low, BF, "cross_back", 18,
    )
    grad_n2, grad_ckv_send, branch_other = ordered(grad_n2, grad_ckv_send, branch_other)
    grad_n2, grad_n2_other = with_other(grad_n2, "tp")
    grad_ckv_other = swap(grad_ckv_send, "ctx")
    layer_out = (
        second_mid + (branch.astype(F32) + branch_other.astype(F32))
    ).astype(BF)
    block_rows = 128
    grad_frames, ckv_in_t, ckv_out_t = call(
        frames_back_kernel,
        2,
        [
            at(grad_ckv),
            at(grad_ckv_other),
            weight_cols(lambda i: 4 + i),
            slot_of(sel_in, lambda i: 5 + i),
            slot_of(part_out, lambda i: 5 + i),
            whole(encoder),
            at(frames_low),
        ],
        [
            out((frames, width), BF),
            at(shape((2, rank, width), F32)),
            at(shape((2, rank, cols), F32)),
        ],
        [pltpu.VMEM((frames, width), F32)],
        name="frames_back",
        cost=9,
    )
    grad_frames, grad_n2_other = ordered(grad_frames, grad_n2_other)
    grad_frames, grad_frames_other = with_other(grad_frames, "tp")
    grad_first, grad_n1_start, grad_skv, grad_skv_send, so_in_t, so_out_t, q_in_t, q_out_t = back_call(
        partial(self_back_kernel, rows), scalars, grad_second, first_mid, grad_n2, grad_n2_other, (6, 3, 0, 0),
        query, self_mixed, self_kv, self_kv_other, self_logsum, n1, self_low,
        self_o_low, F32, "self_back", 12,
    )
    grad_skv_other = swap(grad_skv_send, "ctx")
    grad_n1, kv_in_t, kv_out_t = call(
        pair_project_kernel,
        2,
        [
            at(grad_skv),
            at(grad_skv_other),
            weight_cols(lambda i: 1 + i),
            slot_of(sel_in, lambda i: 1 + i),
            slot_of(part_out, lambda i: 1 + i),
            whole(n1),
            at(self_low, 1),
            whole(grad_n1_start),
        ],
        [
            out((rows, width), BF),
            at(shape((2, rank, width), F32)),
            at(shape((2, rank, cols), F32)),
        ],
        [wide_acc],
        name="self_project_back",
    )
    grad_n1, grad_n1_other = with_other(grad_n1, "tp")
    def row_blocks(array):
        rest = (0,) * (array.ndim - 1)
        return array, pl.BlockSpec((block_rows,) + array.shape[1:], lambda i: (i, *rest))

    block_rows = 256
    encoder_args = (
        add_rows_kernel,
        -(-frames // block_rows),
        [row_blocks(grad_frames)],
        [row_blocks(shape((frames, 1, width), F32))],
    )

    def encoder_total(other):
        kernel, steps, ins, outs = encoder_args
        (total,) = call(kernel, steps, ins + [row_blocks(other)], outs, name="encoder_total")
        return total

    full = [q_in_t, kv_in_t, cq_in_t, ckv_in_t, so_out_t, co_out_t, up_in_t, down_out_t]
    part = [so_in_t, co_in_t, q_out_t, kv_out_t, cq_out_t, ckv_out_t]
    if regular:
        order = (0, 1, 2, 10, 3, 4, 5, 11, 12, 13, 14, 6, 15, 16, 17, 7, 8, 9)
        full[0], layer_out = ordered(q_in_t, layer_out)
        kept, away, grad_frames_other = pack(
            full, part, [up_out_t, down_in_t], order, 1, "pack", grad_frames_other
        )
        grad_encoder = encoder_total(grad_frames_other)
        away, grad_encoder = ordered(swap(away, "tp"), grad_encoder)
        parts = finish(kept, away)
        narrow_out = (attn_adapt_in.shape[0], adapters, rank, PIECE)
        tables = call(
            unpack_kernel,
            1,
            [whole(parts)],
            [
                out(narrow_out, F32),
                out(narrow_out, F32),
                out((adapters, rank, PIECE), F32),
                out((adapters, rank, LANE), F32),
                out((adapters, rank, LANE), F32),
                out((adapters, rank, PIECE), F32),
            ],
            name="unpack",
        )
    else:
        grad_encoder = encoder_total(grad_frames_other)
        chosen = (mine == jnp.arange(adapters, dtype=jnp.int32)).astype(F32)

        def summed(parts, start, full):
            parts = [t for p in parts for t in ([p] if p.ndim == 2 else [p[0], p[1]])]

            def spread_out(part):
                if part.shape[1] == full:
                    return part
                blank = jnp.zeros((part.shape[0], full), F32)
                return lax.dynamic_update_slice_in_dim(blank, part, start, axis=1)

            stacked = jnp.stack([spread_out(p) for p in parts])
            table = chosen[None, :, None, None] * stacked[:, None]
            return lax.psum_scatter(
                table, ("fsdp", "ctx", "tp"), scatter_dimension=3, tiled=True
            )

        attn_in_t = summed(
            [q_in_t, kv_in_t, so_in_t, cq_in_t, ckv_in_t, co_in_t], head_start, width
        )
        attn_out_t = summed(
            [q_out_t, kv_out_t, so_out_t, cq_out_t, ckv_out_t, co_out_t], head_start, width
        )
        small = summed([up_in_t, down_out_t], head_start, width)
        large = summed([up_out_t, down_in_t], unit_start, wide)
        tables = (attn_in_t, attn_out_t, small[0], large[0], large[1], small[1])
    grad_encoder = grad_encoder.reshape(frames, width)
    (grad_hidden,) = call(
        close_kernel,
        1,
        [whole(a) for a in (hidden, ln_gains, grad_first, grad_n1, grad_n1_other)],
        [out((rows, width), F32)],
        name="hidden_total",
    )
    return (
        layer_out[None],
        grad_hidden[None],
        grad_encoder[None],
        *tables,
    )
def solution(mesh):
    in_specs = (
        P("fsdp", "ctx", None),
        P("fsdp", "ctx", None),
        P("fsdp", "ctx", None),
        P("fsdp"),
        P(),
        P(None, "fsdp", "tp"),
        P(None, "fsdp", "tp"),
        P("fsdp", "tp"),
        P("fsdp", "tp"),
        P(),
        P(),
        P(),
        P(),
        P(),
        P(),
    )
    out_specs = (
        P("fsdp", "ctx", None),
        P("fsdp", "ctx", None),
        P("fsdp", "ctx", None),
        P(None, None, None, ("fsdp", "ctx", "tp")),
        P(None, None, None, ("fsdp", "ctx", "tp")),
        P(None, None, ("fsdp", "ctx", "tp")),
        P(None, None, ("fsdp", "ctx", "tp")),
        P(None, None, ("fsdp", "ctx", "tp")),
        P(None, None, ("fsdp", "ctx", "tp")),
    )
    return jax.shard_map(
        on_device, mesh=mesh, in_specs=in_specs, out_specs=out_specs, check_vma=False
    )
```

```python
from functools import partial

import jax
import jax.numpy as jnp
from jax import lax
from jax.experimental import pallas as pl
from jax.experimental.pallas import tpu as pltpu
from jax.sharding import PartitionSpec as P

HEAD_DIM = 64
PAIR = 2 * HEAD_DIM
EPSILON = 1e-05
MASKED_SCORE = -1000000000.0
SCALE = HEAD_DIM ** (-0.5)
BF = jnp.bfloat16
F32 = jnp.float32


def mm(a, b):
    return lax.dot_general(a, b, (((1,), (0,)), ((), ())), preferred_element_type=F32)


def mm_nt(a, b):
    return lax.dot_general(a, b, (((1,), (1,)), ((), ())), preferred_element_type=F32)


def mm_tn(a, b):
    return lax.dot_general(a, b, (((0,), (0,)), ((), ())), preferred_element_type=F32)


def norm_parts(rows):
    centred = rows - jnp.mean(rows, axis=-1, keepdims=True)
    spread = jnp.mean(centred * centred, axis=-1, keepdims=True)
    inverse = lax.rsqrt(spread + EPSILON)
    return centred * inverse, inverse


def normalize(rows, gain):
    return norm_parts(rows)[0] * gain


def normalize_back(rows, gain, gradient):
    unit, inverse = norm_parts(rows)
    scaled = gradient * gain
    first = jnp.mean(scaled, axis=-1, keepdims=True)
    second = jnp.mean(scaled * unit, axis=-1, keepdims=True)
    return (scaled - first - unit * second) * inverse


def swap(value, axis):
    return lax.ppermute(value, axis, [(0, 1), (1, 0)])


def with_other(partial_value, axis):
    if lax.axis_size(axis) == 2:
        return partial_value, swap(partial_value, axis)
    return lax.psum(partial_value, axis), jnp.zeros_like(partial_value)


def matrix(ref):
    block = ref[...]
    return block.reshape(block.shape[0] * block.shape[2], block.shape[3])


def half_masks(rows):
    lane = lax.broadcasted_iota(jnp.int32, (rows, PAIR), 1)
    return lane < HEAD_DIM, lane >= HEAD_DIM


def pick_half(rows, keep):
    return jnp.where(keep, rows, jnp.zeros_like(rows))


def join_halves(first, second):
    row = lax.broadcasted_iota(jnp.int32, first.shape, 0)
    return jnp.where(row < HEAD_DIM, first, second).T


def pair_forward(queries, keys, values, limit, saved=None):
    mixed, logsums = [], []
    turned = [v.T for v in values]
    for half, keep in enumerate(half_masks(queries.shape[0])):
        mine = pick_half(queries, keep) * BF(SCALE)
        scores = [limit(i, mm_nt(k, mine)) for i, k in enumerate(keys)]
        top = jnp.max(scores[0], axis=0, keepdims=True)
        for s in scores[1:]:
            top = jnp.maximum(top, jnp.max(s, axis=0, keepdims=True))
        powers = [jnp.exp(s - top) for s in scores]
        total = sum(jnp.sum(e, axis=0, keepdims=True) for e in powers)
        share = 1.0 / total
        weights = [(e * share).astype(BF) for e in powers]
        if saved is not None:
            for i, w in enumerate(weights):
                saved[0, half, i, : w.shape[0]] = w
        mixed.append(sum(mm(v, w) for v, w in zip(turned, weights)))
        logsums.append(top + jnp.log(total))
    return join_halves(*mixed), logsums


def pair_backward(grad, mixed, queries, keys, values, logsums, limit, saved=None):
    grad_query, grad_keys, grad_values = [], [0.0] * len(keys), [0.0] * len(keys)
    inners = (grad.astype(F32) * mixed.astype(F32)).T
    turned = [k.T for k in keys]
    for half, (keep, logsum) in enumerate(zip(half_masks(queries.shape[0]), logsums)):
        mine = pick_half(queries, keep) * BF(SCALE)
        grad_mine = pick_half(grad, keep)
        at = HEAD_DIM * half
        inner = jnp.sum(inners[at : at + HEAD_DIM], axis=0, keepdims=True)
        part = 0.0
        for i, (key, value) in enumerate(zip(keys, values)):
            if saved is None:
                weights = jnp.exp(limit(i, mm_nt(key, mine)) - logsum)
                rounded = weights.astype(BF)
            else:
                rounded = saved[0, half, i, : key.shape[0]]
                weights = rounded.astype(F32)
            grad_scores = (weights * (mm_nt(value, grad_mine) - inner)).astype(BF)
            part = part + mm(turned[i], grad_scores)
            grad_keys[i] = grad_keys[i] + mm(grad_scores, mine)
            grad_values[i] = grad_values[i] + mm(rounded, grad_mine)
        grad_query.append(part)
    return (
        (join_halves(*grad_query) * SCALE).astype(BF),
        [g.astype(BF) for g in grad_keys],
        [g.astype(BF) for g in grad_values],
    )


def no_limit(index, scores):
    return scores


def causal_limit(context):
    def limit(index, scores):
        if index == 0:
            key = lax.broadcasted_iota(jnp.int32, scores.shape, 0)
            query = lax.broadcasted_iota(jnp.int32, scores.shape, 1)
            return jnp.where(key <= query, scores, MASKED_SCORE)
        return jnp.where(context == 1, scores, MASKED_SCORE)

    return limit


def at_first(step=0):
    return pl.when(pl.program_id(0) == step)


def at_last():
    return pl.when(pl.program_id(0) == pl.num_programs(0) - 1)


def halves_kernel(where, inputs, outputs, joined):
    count = inputs.shape[0]
    joined[:count] = inputs[...]
    joined[count:] = outputs[...]


def qkv_kernel(hidden, gains, weight, low_in, low_out, normed, query, key_value, low):
    @at_first()
    def _():
        normed[...] = normalize(hidden[...].astype(F32), gains[0:1, :]).astype(BF)

    rows = normed[...]
    rank_rows = mm_nt(rows, low_in[0]).astype(BF)
    low[0] = rank_rows
    value = (mm(rows, matrix(weight)) + mm(rank_rows, low_out[0])).astype(BF)

    @at_first()
    def _():
        query[...] = value

    @pl.when(pl.program_id(0) > 0)
    def _():
        key_value[0] = value


def frames_kernel(frames, weight, low_in, low_out, key_value, low):
    rows = frames[...]
    rank_rows = mm_nt(rows, low_in[0]).astype(BF)
    low[0] = rank_rows
    count = rows.shape[0]
    key_value[0, :count] = (mm(rows, matrix(weight)) + mm(rank_rows, low_out[0])).astype(BF)
    spare = key_value.shape[1] - count
    if spare:
        key_value[0, count:] = jnp.zeros((spare, key_value.shape[2]), BF)


def self_kernel(
    where, query, mine, other, weight, low_in, low_out, mixed, logsum, branch, low, acc, low_acc
):
    @at_first()
    def _():
        acc[...] = jnp.zeros_like(acc)
        low_acc[...] = jnp.zeros_like(low_acc)

    out, logs = pair_forward(
        query[...], (mine[0], other[0]), (mine[1], other[1]), causal_limit(where[0])
    )
    out = out.astype(BF)
    mixed[...] = out
    logsum[0, 0:1, :] = logs[0]
    logsum[0, 1:2, :] = logs[1]
    acc[...] += mm_nt(out, matrix(weight))
    low_acc[...] += mm_nt(out, low_in[0])

    @at_last()
    def _():
        rank_rows = low_acc[...].astype(BF)
        low[...] = rank_rows
        branch[...] = (acc[...] + mm(rank_rows, low_out[0])).astype(BF)


def cross_kernel(
    count,
    hidden, branch_mine, branch_other, gains, query_weight, query_in, query_out, mine, other,
    weight, low_in, low_out,
    middle, normed, query, query_low, mixed, saved, branch, low, acc, low_acc,
):
    @at_first()
    def _():
        acc[...] = jnp.zeros_like(acc)
        low_acc[...] = jnp.zeros_like(low_acc)
        total = hidden[...].astype(F32) + (
            branch_mine[...].astype(F32) + branch_other[...].astype(F32)
        )
        middle[...] = total
        rows = normalize(total, gains[1:2, :]).astype(BF)
        normed[...] = rows
        query_low[...] = mm_nt(rows, query_in[0]).astype(BF)

    queries = (
        mm(normed[...], matrix(query_weight)) + mm(query_low[...], query_out[0])
    ).astype(BF)
    query[...] = queries
    out, _ = pair_forward(
        queries,
        (mine[0, :count], other[0, :count]),
        (mine[1, :count], other[1, :count]),
        no_limit,
        saved,
    )
    out = out.astype(BF)
    mixed[...] = out
    acc[...] += mm_nt(out, matrix(weight))
    low_acc[...] += mm_nt(out, low_in[0])

    @at_last()
    def _():
        rank_rows = low_acc[...].astype(BF)
        low[...] = rank_rows
        branch[...] = (acc[...] + mm(rank_rows, low_out[0])).astype(BF)


def third_norm_kernel(
    middle, branch_mine, branch_other, gains, cotangent, up_in, down_out,
    second, normed, up_low, down_back,
):
    total = middle[...] + (branch_mine[...].astype(F32) + branch_other[...].astype(F32))
    second[...] = total
    rows = normalize(total, gains[2:3, :]).astype(BF)
    normed[...] = rows
    up_low[...] = mm_nt(rows, up_in[...]).astype(BF)
    down_back[...] = mm_nt(cotangent[...], down_out[...]).astype(BF)


def units_kernel(
    normed, up_low, down_back, cotangent, up, down, up_in, up_out, down_in,
    grad_normed, up_back, active, grad_units,
    back, back_low,
):
    @at_first()
    def _():
        back[...] = jnp.zeros_like(back)
        back_low[...] = jnp.zeros_like(back_low)

    up_rows = matrix(up)
    value = mm(normed[...], up_rows) + mm(up_low[...], up_out[...])
    spread = 1.0 + lax.erf(value * 0.7071067811865476)
    active[...] = (0.5 * value * spread).astype(BF)
    slope = 0.5 * spread + value * (0.3989422804014327 * jnp.exp(-0.5 * value * value))
    grad_act = mm(cotangent[...], matrix(down)) + mm(down_back[...], down_in[...])
    grad = (grad_act * slope).astype(BF)
    grad_units[...] = grad
    back[...] += mm_nt(grad, up_rows)
    back_low[...] += mm_nt(grad, up_out[...])

    @at_last()
    def _():
        rank_rows = back_low[...].astype(BF)
        up_back[...] = rank_rows
        grad_normed[...] = (back[...] + mm(rank_rows, up_in[...])).astype(BF)


def units_out_kernel(
    active, grad_units, normed, up_low, up_back, down_back, cotangent, down, down_in, down_out,
    branch, table_up_in, table_up_out, table_down_in, table_down_out,
    acc, low_acc,
):
    @at_first()
    def _():
        acc[...] = jnp.zeros_like(acc)
        low_acc[...] = jnp.zeros_like(low_acc)

    act = active[...]
    acc[...] += mm_nt(act, matrix(down))
    low_acc[...] += mm_nt(act, down_in[...])
    table_up_out[...] = mm_tn(up_low[...], grad_units[...])
    table_down_in[...] = mm_tn(down_back[...], act)

    @at_last()
    def _():
        down_low = low_acc[...].astype(BF)
        branch[...] = (acc[...] + mm(down_low, down_out[...])).astype(BF)
        table_down_out[...] = mm_tn(down_low, cotangent[...])
        table_up_in[...] = mm_tn(up_back[...], normed[...])


def attention_back(
    limit, slot, count, stored, carried, rows, gains, grad_mine, grad_other, weight, low_in, low_out,
    query_weight, query_in, query_out, query, mixed, mine, other, logsum, normed, query_low, low,
    carry, grad_normed, grad_kv, grad_kv_other,
    table_in, table_out, table_query_in, table_query_out,
    narrow, back_low, acc, query_back,
):
    @at_first()
    def _():
        total = carried[...].astype(F32) + normalize_back(
            rows[...],
            gains[slot : slot + 1, :],
            grad_mine[...].astype(F32) + grad_other[...].astype(F32),
        )
        carry[...] = total
        narrow[...] = total.astype(BF)
        back_low[...] = mm_nt(narrow[...], low_out[0]).astype(BF)
        acc[...] = jnp.zeros_like(acc)
        query_back[...] = jnp.zeros_like(query_back)
        table_out[...] = mm_tn(low[...], narrow[...])

    grad = (mm(narrow[...], matrix(weight)) + mm(back_low[...], low_in[0])).astype(BF)
    table_in[...] = mm_tn(back_low[...], mixed[...])
    grad_query, grad_keys, grad_values = pair_backward(
        grad,
        mixed[...],
        query[...],
        (mine[0, :count], other[0, :count]),
        (mine[1, :count], other[1, :count]),
        (None, None) if stored else (logsum[0, 0:1, :], logsum[0, 1:2, :]),
        limit,
        logsum if stored else None,
    )
    for which, (first, second) in enumerate((grad_keys, grad_values)):
        grad_kv[which, :count] = first
        grad_kv_other[which, :count] = second
        spare = grad_kv.shape[1] - count
        if spare:
            grad_kv[which, count:] = jnp.zeros((spare, PAIR), BF)
            grad_kv_other[which, count:] = jnp.zeros((spare, PAIR), BF)
    acc[...] += mm_nt(grad_query, matrix(query_weight))
    query_back[...] += mm_nt(grad_query, query_out[0])
    table_query_out[...] = mm_tn(query_low[0], grad_query)

    @at_last()
    def _():
        rank_rows = query_back[...].astype(BF)
        total = acc[...] + mm(rank_rows, query_in[0])
        grad_normed[...] = total.astype(grad_normed.dtype)
        table_query_in[...] = mm_tn(rank_rows, normed[...])


def self_back_kernel(count, where, *refs):
    attention_back(causal_limit(where[0]), 1, count, False, *refs)


def pair_project_kernel(
    grad_mine, grad_other, weight, low_in, low_out, rows, low, start, total, table_in, table_out,
    acc,
):
    @at_first()
    def _():
        acc[...] = start[...]

    pair_project_step(
        grad_mine, grad_other, weight, low_in, low_out, rows, low, table_in, table_out, acc
    )

    @at_last()
    def _():
        total[...] = acc[...].astype(BF)


def close_kernel(hidden, gains, carried, grad_mine, grad_other, total):
    total[...] = carried[...] + normalize_back(
        hidden[...].astype(F32),
        gains[0:1, :],
        grad_mine[...].astype(F32) + grad_other[...].astype(F32),
    )


def add_rows_kernel(mine, other, *refs):
    total = refs[-1]
    value = mine[...].astype(F32) + other[...].astype(F32)
    total[...] = value[:, None, :]


def frames_back_kernel(
    grad_mine, grad_other, weight, low_in, low_out, rows, low, total, table_in, table_out, acc
):
    @at_first()
    def _():
        acc[...] = jnp.zeros_like(acc)

    pair_project_step(
        grad_mine, grad_other, weight, low_in, low_out, rows, low, table_in, table_out, acc
    )

    @at_last()
    def _():
        total[...] = acc[...].astype(BF)


def pair_project_step(
    grad_mine, grad_other, weight, low_in, low_out, rows, low, table_in, table_out, acc
):
    count = rows.shape[0]
    grad = (grad_mine[0, :count].astype(F32) + grad_other[0, :count].astype(F32)).astype(BF)
    rank_rows = mm_nt(grad, low_out[0]).astype(BF)
    acc[...] += mm_nt(grad, matrix(weight)) + mm(rank_rows, low_in[0])
    table_in[0] = mm_tn(rank_rows, rows[...])
    table_out[0] = mm_tn(low[0], grad)


LANE = 128
PIECE = 32


def pack_kernel(fulls, shares, order, tagged, *refs):
    where = refs[0]
    keep, send = refs[-2:]
    flat = []
    for ref in refs[1:-2]:
        flat += [ref] if len(ref.shape) == 2 else [ref.at[i] for i in range(ref.shape[0])]
    tables, broad = flat[: fulls + shares], flat[fulls + shares :]
    context, tensor = where[0], where[1]
    blocks = keep.shape[1]
    per_group = (len(order) + 3) // 4
    rows = per_group * 16
    lane = lax.broadcasted_iota(jnp.int32, (rows, LANE), 1) // PIECE
    padded = list(order) + [None] * (4 * per_group - len(order))

    def one_block(f, carry):
        shard = f // (blocks // 2)
        local = f - shard * (blocks // 2)
        owned = tensor == shard

        def table_of(k):
            if k is None:
                return jnp.zeros((16, LANE), F32)
            if k < fulls:
                return tables[k][:, pl.ds(pl.multiple_of(f * LANE, LANE), LANE)]
            part = tables[k][:, pl.ds(pl.multiple_of(local * LANE, LANE), LANE)]
            return jnp.where(owned, part, 0.0)

        groups = [
            jnp.concatenate(
                [table_of(k) for k in padded[g * per_group : (g + 1) * per_group]], axis=0
            )
            for g in range(4)
        ]
        for target, side in ((keep, context), (send, 1 - context)):
            for t in range(2):
                p = 2 * side + t
                value = jnp.zeros((rows, LANE), F32)
                for g in range(4):
                    turned = pltpu.roll(groups[g], (PIECE * (g + 4 - p)) % LANE, 1)
                    value = jnp.where(lane == g, turned, value)
                if tagged:
                    spare = 4 * per_group - len(order)
                    tag = where[2].astype(F32) * 0.25
                    low = rows - 16 * spare
                    at_row = lax.broadcasted_iota(jnp.int32, (rows, LANE), 0)
                    value = jnp.where((lane == 3) & (at_row >= low), tag, value)
                target[t, f, :rows] = value
                row = rows
                for w in broad:
                    at = pl.multiple_of(local * 4 * LANE + p * LANE, LANE)
                    target[t, f, row : row + 16] = jnp.where(owned, w[:, pl.ds(at, LANE)], 0.0)
                    row += 16
        return carry

    lax.fori_loop(0, blocks, one_block, 0)


def unpack_kernel(parts, attn_in, attn_out, up_in, up_out, down_in, down_out):
    projections, adapters = attn_in.shape[:2]
    clips, rows = parts.shape[:2]
    per_group = (2 * projections + 2 + 3) // 4
    narrow = 16 * per_group

    tags = []
    for c in range(clips):
        tag = parts[c, narrow - 16 : narrow, 3 * PIECE :].astype(F32)[0:1, 0:1]
        tags.append(jnp.broadcast_to(tag, (1, LANE)))

    def one(a, carry):
        adapter = a.astype(F32)
        block = jnp.zeros((rows, LANE), F32)
        for c in range(clips):
            same = (tags[c] > adapter - 0.5) & (tags[c] < adapter + 0.5)
            weight = jnp.where(same, 1.0, 0.0)
            block = block + parts[c].astype(F32) * weight

        def piece(k):
            g, at = k // per_group, 16 * (k % per_group)
            return block[at : at + 16, PIECE * g : PIECE * (g + 1)]

        for j in range(projections):
            attn_in[j, a] = piece(j)
            attn_out[j, a] = piece(projections + j)
        up_in[a] = piece(2 * projections)
        down_out[a] = piece(2 * projections + 1)
        up_out[a] = block[narrow : narrow + 16]
        down_in[a] = block[narrow + 16 : narrow + 32]
        return carry

    lax.fori_loop(0, adapters, one, 0)


def shape(dims, dtype):
    return jax.ShapeDtypeStruct(tuple(dims), dtype)


def fixed(array):
    zeros = (0,) * array.ndim
    return pl.BlockSpec(array.shape, lambda *_: zeros)


def fixed_out(*dims):
    zeros = (0,) * len(dims)
    return pl.BlockSpec(dims, lambda *_: zeros)


def call(kernel, steps, ins, outs, scratch=(), scalars=None, name=None, cost=5, aliases=None):
    arrays = [a for a, _ in ins]
    spec = pltpu.PrefetchScalarGridSpec(
        num_scalar_prefetch=0 if scalars is None else 1,
        grid=(steps,),
        in_specs=[s for _, s in ins],
        out_specs=[s for _, s in outs],
        scratch_shapes=list(scratch),
    )
    run = pl.pallas_call(
        kernel,
        grid_spec=spec,
        out_shape=[o for o, _ in outs],
        compiler_params=pltpu.CompilerParams(dimension_semantics=("arbitrary",)),
        cost_estimate=pl.CostEstimate(
            flops=cost * 10_000_000, transcendentals=0, bytes_accessed=cost * 36_900
        ),
        input_output_aliases=aliases or {},
        name=name,
    )
    return run(*arrays) if scalars is None else run(scalars, *arrays)


def on_device(
    hidden,
    encoder,
    cotangent,
    adapter_index,
    ln_gains,
    attn_in_weight,
    attn_out_weight,
    up_weight,
    down_weight,
    attn_adapt_in,
    attn_adapt_out,
    up_adapt_in,
    up_adapt_out,
    down_adapt_in,
    down_adapt_out,
):
    fsdp_size = lax.axis_size("fsdp")
    ctx_size = lax.axis_size("ctx")
    tp_size = lax.axis_size("tp")
    tensor_index = lax.axis_index("tp")
    context_index = lax.axis_index("ctx")
    hidden, encoder, cotangent = hidden[0], encoder[0], cotangent[0]
    rows, width = hidden.shape
    frames = encoder.shape[0]
    padded = -(-frames // 16) * 16
    wide = up_adapt_out.shape[2]
    cols = attn_in_weight.shape[2]
    units = up_weight.shape[1]
    rank = attn_adapt_in.shape[2]
    adapters = attn_adapt_in.shape[1]
    pairs = cols // PAIR
    head_start = tensor_index * cols
    unit_start = tensor_index * units
    mine = adapter_index[0]
    scalars = jnp.stack(
        [context_index.astype(jnp.int32), tensor_index.astype(jnp.int32), mine]
    )

    def out(dims, dtype):
        return shape(dims, dtype), fixed_out(*dims)

    half_rows = attn_in_weight.shape[1] // ctx_size
    shards = fsdp_size * ctx_size

    def my_half(table):
        return lax.dynamic_slice_in_dim(
            table, context_index * half_rows, half_rows, axis=table.ndim - 2
        )

    heads_tables = (attn_in_weight, attn_out_weight)
    (attn_half,) = call(
        halves_kernel,
        1,
        [
            (t, pl.BlockSpec((t.shape[0], half_rows, cols), lambda i, where: (0, where[0], 0)))
            for t in heads_tables
        ],
        [out((sum(t.shape[0] for t in heads_tables), half_rows, cols), BF)],
        scalars=context_index.astype(jnp.int32).reshape(1),
        name="halves",
    )
    ff_half = jnp.stack([my_half(up_weight), my_half(down_weight)])
    attn_full = lax.all_gather(attn_half, ("fsdp", "ctx"), axis=0)
    ff_full = lax.all_gather(ff_half, ("fsdp", "ctx"), axis=0)

    sel_in = lax.dynamic_index_in_dim(attn_adapt_in, mine, 1, keepdims=False)
    sel_out = lax.dynamic_index_in_dim(attn_adapt_out, mine, 1, keepdims=False)
    part_in = lax.dynamic_slice_in_dim(sel_in, head_start, cols, 2)
    part_out = lax.dynamic_slice_in_dim(sel_out, head_start, cols, 2)
    up_in = lax.dynamic_index_in_dim(up_adapt_in, mine, 0, keepdims=False)
    up_out = lax.dynamic_slice(up_adapt_out, (mine, 0, unit_start), (1, rank, units))[0]
    down_in = lax.dynamic_slice(down_adapt_in, (mine, 0, unit_start), (1, rank, units))[0]
    down_out = lax.dynamic_index_in_dim(down_adapt_out, mine, 0, keepdims=False)

    def weight_cols(slot):
        return attn_full, pl.BlockSpec((shards, 1, half_rows, cols), lambda i, *_: (0, slot(i), 0, 0))

    def weight_pair(slot):
        return attn_full, pl.BlockSpec((shards, 1, half_rows, PAIR), lambda p, *_: (0, slot, 0, p))

    def slot_of(table, slot):
        return table, pl.BlockSpec((1,) + table.shape[1:], lambda i, *_: (slot(i), 0, 0))

    def slot_pair(table, slot):
        return table, pl.BlockSpec((1, rank, PAIR), lambda p, *_: (slot, 0, p))

    def whole(array):
        return array, fixed(array)

    def by_pair(count, dtype=BF):
        return shape((count, cols), dtype), pl.BlockSpec((count, PAIR), lambda p, *_: (0, p))

    def kv_pair(array):
        return array, pl.BlockSpec((2, array.shape[1], PAIR), lambda p, *_: (0, 0, p))

    def at(array, first=0):
        return array, pl.BlockSpec((1,) + array.shape[1:], lambda i, *_: (first + i, 0, 0))

    def at_slot(array):
        return array, pl.BlockSpec((1,) + array.shape[1:], lambda i, *_: (0, 0, 0))

    logsum_out = (
        shape((pairs, 2, rows), F32),
        pl.BlockSpec((1, 2, rows), lambda p, *_: (p, 0, 0)),
    )

    def logsum_in(array):
        rest = (0,) * (array.ndim - 1)
        return array, pl.BlockSpec((1,) + array.shape[1:], lambda p, *_: (p, *rest))

    saved_shape = shape((pairs, 2, 2, padded, rows), BF)

    def pair_in(array):
        return array, pl.BlockSpec((array.shape[0], PAIR), lambda p, *_: (0, p))

    regular = (
        ctx_size == 2 and tp_size == 2 and rank == 16
        and width == LANE * fsdp_size and wide == 4 * LANE * fsdp_size
    )

    def ordered(first, *others):
        return lax.optimization_barrier((first, *others))

    def pack(full, part, wides, order, tagged, name, after):
        count = 16 * ((len(order) + 3) // 4 + len(wides))
        dims = (2, fsdp_size, count, LANE)

        def number(arrays):
            return sum(1 if a.ndim == 2 else a.shape[0] for a in arrays)

        keep, send = call(
            partial(pack_kernel, number(full), number(part), order, tagged),
            1,
            [whole(a) for a in full + part + wides],
            [out(dims, F32), out(dims, F32)],
            scalars=scalars,
            name=name,
        )
        recv = swap(send, "ctx")

        def pick(i):
            return lax.dynamic_index_in_dim(keep, i, 0, keepdims=False) + (
                lax.dynamic_index_in_dim(recv, i, 0, keepdims=False)
            )

        kept, away = pick(tensor_index), pick(1 - tensor_index).astype(BF)
        return ordered(kept, away, after)

    def finish(kept, away):
        return lax.all_to_all((kept + away.astype(F32)).astype(BF), "fsdp", 0, 0, tiled=True)

    wide_acc = pltpu.VMEM((rows, width), F32)
    rank_acc = pltpu.VMEM((rows, rank), F32)
    rank_keep = pltpu.VMEM((rows, rank), BF)

    n1, query, self_kv, self_low = call(
        qkv_kernel,
        3,
        [
            whole(hidden),
            whole(ln_gains),
            weight_cols(lambda i: i),
            slot_of(sel_in, lambda i: i),
            slot_of(part_out, lambda i: i),
        ],
        [
            out((rows, width), BF),
            out((rows, cols), BF),
            (
                shape((2, rows, cols), BF),
                pl.BlockSpec((1, rows, cols), lambda i: (jnp.maximum(i - 1, 0), 0, 0)),
            ),
            (shape((3, rows, rank), BF), pl.BlockSpec((1, rows, rank), lambda i: (i, 0, 0))),
        ],
        name="qkv",
    )
    self_kv_other = swap(self_kv, "ctx")
    cross_kv, frames_low = call(
        frames_kernel,
        2,
        [
            whole(encoder),
            weight_cols(lambda i: 4 + i),
            slot_of(sel_in, lambda i: 5 + i),
            slot_of(part_out, lambda i: 5 + i),
        ],
        [
            (
                shape((2, padded, cols), BF),
                pl.BlockSpec((1, padded, cols), lambda i: (i, 0, 0)),
            ),
            (
                shape((2, frames, rank), BF),
                pl.BlockSpec((1, frames, rank), lambda i: (i, 0, 0)),
            ),
        ],
        name="frames",
        cost=7,
    )
    cross_kv_other = swap(cross_kv, "ctx")
    self_mixed, self_logsum, branch, self_o_low = call(
        self_kernel,
        pairs,
        [
            pair_in(query),
            kv_pair(self_kv),
            kv_pair(self_kv_other),
            weight_pair(6),
            slot_pair(part_in, 3),
            slot_of(sel_out, lambda i: 3),
        ],
        [by_pair(rows), logsum_out, out((rows, width), BF), out((rows, rank), BF)],
        [wide_acc, rank_acc],
        scalars,
        name="self_attention",
        cost=7,
    )
    branch, branch_other = with_other(branch, "tp")
    first_mid, n2, cross_q, cross_q_low, cross_mixed, cross_logsum, branch, cross_o_low = call(
        partial(cross_kernel, frames),
        pairs,
        [
            whole(hidden),
            whole(branch),
            whole(branch_other),
            whole(ln_gains),
            weight_pair(3),
            slot_of(sel_in, lambda i: 4),
            slot_pair(part_out, 4),
            kv_pair(cross_kv),
            kv_pair(cross_kv_other),
            weight_pair(7),
            slot_pair(part_in, 7),
            slot_of(sel_out, lambda i: 7),
        ],
        [
            out((rows, width), F32),
            out((rows, width), BF),
            by_pair(rows),
            out((rows, rank), BF),
            by_pair(rows),
            logsum_in(saved_shape),
            out((rows, width), BF),
            out((rows, rank), BF),
        ],
        [wide_acc, rank_acc],
        name="cross_attention",
        cost=13,
    )
    branch, branch_other = with_other(branch, "tp")
    chunk = min(units, 1024)

    def unit_weight(slot):
        return ff_full, pl.BlockSpec((shards, 1, half_rows, chunk), lambda i: (0, slot, 0, i))

    def unit_cols(array):
        return array, pl.BlockSpec((rank, chunk), lambda i: (0, i))

    second_mid, n3, up_low, down_back = call(
        third_norm_kernel,
        1,
        [
            whole(a)
            for a in (
                first_mid, branch, branch_other, ln_gains, cotangent, up_in, down_out
            )
        ],
        [
            out((rows, width), F32),
            out((rows, width), BF),
            out((rows, rank), BF),
            out((rows, rank), BF),
        ],
        name="third_norm",
    )
    def unit_rows(array):
        return array, pl.BlockSpec((rows, chunk), lambda i: (0, i))

    grad_n3, up_back, active, grad_units = call(
        units_kernel,
        units // chunk,
        [
            whole(n3),
            whole(up_low),
            whole(down_back),
            whole(cotangent),
            unit_weight(0),
            unit_weight(1),
            whole(up_in),
            unit_cols(up_out),
            unit_cols(down_in),
        ],
        [
            out((rows, width), BF),
            out((rows, rank), BF),
            unit_rows(shape((rows, units), BF)),
            unit_rows(shape((rows, units), BF)),
        ],
        [wide_acc, rank_acc],
        name="units",
        cost=11,
    )
    branch, up_in_t, up_out_t, down_in_t, down_out_t = call(
        units_out_kernel,
        units // chunk,
        [
            unit_rows(active),
            unit_rows(grad_units),
            whole(n3),
            whole(up_low),
            whole(up_back),
            whole(down_back),
            whole(cotangent),
            unit_weight(1),
            unit_cols(down_in),
            whole(down_out),
        ],
        [
            out((rows, width), BF),
            out((rank, width), F32),
            unit_cols(shape((rank, units), F32)),
            unit_cols(shape((rank, units), F32)),
            out((rank, width), F32),
        ],
        [wide_acc, rank_acc],
        name="units_out",
    )
    grad_n3, grad_n3_other = with_other(grad_n3, "tp")
    branch, grad_n3_other = ordered(branch, grad_n3_other)
    branch, branch_other = with_other(branch, "tp")

    def back_call(
        kernel, scalar, carried, middle, grad, grad_other, slots, queries, mixed, kv, kv_other,
        logsum, normed, query_low, low, kind, name, cost,
    ):
        weight_slot, low_slot, query_slot, query_low_slot = slots
        count = kv.shape[1]
        kv_out = (
            shape((2, count, cols), BF),
            pl.BlockSpec((2, count, PAIR), lambda p, *_: (0, 0, p)),
        )
        return call(
            kernel,
            pairs,
            [
                whole(carried),
                whole(middle),
                whole(ln_gains),
                whole(grad),
                whole(grad_other),
                weight_pair(weight_slot),
                slot_pair(part_in, low_slot),
                slot_of(sel_out, lambda i: low_slot),
                weight_pair(query_slot),
                slot_of(sel_in, lambda i: query_low_slot),
                slot_pair(part_out, query_low_slot),
                pair_in(queries),
                pair_in(mixed),
                kv_pair(kv),
                kv_pair(kv_other),
                logsum_in(logsum),
                whole(normed),
                at_slot(query_low),
                whole(low),
            ],
            [
                out((rows, width), F32),
                out((rows, width), kind),
                kv_out,
                kv_out,
                by_pair(rank, F32),
                out((rank, width), F32),
                out((rank, width), F32),
                by_pair(rank, F32),
            ],
            [pltpu.VMEM((rows, width), BF), rank_keep, wide_acc, rank_acc],
            scalar,
            name=name,
            cost=cost,
        )

    grad_second, grad_n2, grad_ckv, grad_ckv_send, co_in_t, co_out_t, cq_in_t, cq_out_t = back_call(
        partial(attention_back, no_limit, 2, frames, True), None, cotangent, second_mid, grad_n3, grad_n3_other, (7, 7, 3, 4),
        cross_q, cross_mixed, cross_kv, cross_kv_other, cross_logsum, n2, cross_q_low[None],
        cross_o_low, BF, "cross_back", 18,
    )
    grad_n2, grad_ckv_send, branch_other = ordered(grad_n2, grad_ckv_send, branch_other)
    grad_n2, grad_n2_other = with_other(grad_n2, "tp")
    grad_ckv_other = swap(grad_ckv_send, "ctx")
    layer_out = (
        second_mid + (branch.astype(F32) + branch_other.astype(F32))
    ).astype(BF)
    block_rows = 128
    grad_frames, ckv_in_t, ckv_out_t = call(
        frames_back_kernel,
        2,
        [
            at(grad_ckv),
            at(grad_ckv_other),
            weight_cols(lambda i: 4 + i),
            slot_of(sel_in, lambda i: 5 + i),
            slot_of(part_out, lambda i: 5 + i),
            whole(encoder),
            at(frames_low),
        ],
        [
            out((frames, width), BF),
            at(shape((2, rank, width), F32)),
            at(shape((2, rank, cols), F32)),
        ],
        [pltpu.VMEM((frames, width), F32)],
        name="frames_back",
        cost=9,
    )
    grad_frames, grad_n2_other = ordered(grad_frames, grad_n2_other)
    grad_frames, grad_frames_other = with_other(grad_frames, "tp")
    grad_first, grad_n1_start, grad_skv, grad_skv_send, so_in_t, so_out_t, q_in_t, q_out_t = back_call(
        partial(self_back_kernel, rows), scalars, grad_second, first_mid, grad_n2, grad_n2_other, (6, 3, 0, 0),
        query, self_mixed, self_kv, self_kv_other, self_logsum, n1, self_low,
        self_o_low, F32, "self_back", 12,
    )
    grad_skv_other = swap(grad_skv_send, "ctx")
    grad_n1, kv_in_t, kv_out_t = call(
        pair_project_kernel,
        2,
        [
            at(grad_skv),
            at(grad_skv_other),
            weight_cols(lambda i: 1 + i),
            slot_of(sel_in, lambda i: 1 + i),
            slot_of(part_out, lambda i: 1 + i),
            whole(n1),
            at(self_low, 1),
            whole(grad_n1_start),
        ],
        [
            out((rows, width), BF),
            at(shape((2, rank, width), F32)),
            at(shape((2, rank, cols), F32)),
        ],
        [wide_acc],
        name="self_project_back",
    )
    grad_n1, grad_n1_other = with_other(grad_n1, "tp")
    def row_blocks(array):
        rest = (0,) * (array.ndim - 1)
        return array, pl.BlockSpec((block_rows,) + array.shape[1:], lambda i: (i, *rest))

    block_rows = 256
    encoder_args = (
        add_rows_kernel,
        -(-frames // block_rows),
        [row_blocks(grad_frames)],
        [row_blocks(shape((frames, 1, width), F32))],
    )

    def encoder_total(other):
        kernel, steps, ins, outs = encoder_args
        (total,) = call(kernel, steps, ins + [row_blocks(other)], outs, name="encoder_total")
        return total

    full = [q_in_t, kv_in_t, cq_in_t, ckv_in_t, so_out_t, co_out_t, up_in_t, down_out_t]
    part = [so_in_t, co_in_t, q_out_t, kv_out_t, cq_out_t, ckv_out_t]
    if regular:
        order = (0, 1, 2, 10, 3, 4, 5, 11, 12, 13, 14, 6, 15, 16, 17, 7, 8, 9)
        full[0], layer_out = ordered(q_in_t, layer_out)
        kept, away, grad_frames_other = pack(
            full, part, [up_out_t, down_in_t], order, 1, "pack", grad_frames_other
        )
        grad_encoder = encoder_total(grad_frames_other)
        away, grad_encoder = ordered(swap(away, "tp"), grad_encoder)
        parts = finish(kept, away)
        narrow_out = (attn_adapt_in.shape[0], adapters, rank, PIECE)
        tables = call(
            unpack_kernel,
            1,
            [whole(parts)],
            [
                out(narrow_out, F32),
                out(narrow_out, F32),
                out((adapters, rank, PIECE), F32),
                out((adapters, rank, LANE), F32),
                out((adapters, rank, LANE), F32),
                out((adapters, rank, PIECE), F32),
            ],
            name="unpack",
        )
    else:
        grad_encoder = encoder_total(grad_frames_other)
        chosen = (mine == jnp.arange(adapters, dtype=jnp.int32)).astype(F32)

        def summed(parts, start, full):
            parts = [t for p in parts for t in ([p] if p.ndim == 2 else [p[0], p[1]])]

            def spread_out(part):
                if part.shape[1] == full:
                    return part
                blank = jnp.zeros((part.shape[0], full), F32)
                return lax.dynamic_update_slice_in_dim(blank, part, start, axis=1)

            stacked = jnp.stack([spread_out(p) for p in parts])
            table = chosen[None, :, None, None] * stacked[:, None]
            return lax.psum_scatter(
                table, ("fsdp", "ctx", "tp"), scatter_dimension=3, tiled=True
            )

        attn_in_t = summed(
            [q_in_t, kv_in_t, so_in_t, cq_in_t, ckv_in_t, co_in_t], head_start, width
        )
        attn_out_t = summed(
            [q_out_t, kv_out_t, so_out_t, cq_out_t, ckv_out_t, co_out_t], head_start, width
        )
        small = summed([up_in_t, down_out_t], head_start, width)
        large = summed([up_out_t, down_in_t], unit_start, wide)
        tables = (attn_in_t, attn_out_t, small[0], large[0], large[1], small[1])
    grad_encoder = grad_encoder.reshape(frames, width)
    (grad_hidden,) = call(
        close_kernel,
        1,
        [whole(a) for a in (hidden, ln_gains, grad_first, grad_n1, grad_n1_other)],
        [out((rows, width), F32)],
        name="hidden_total",
    )
    return (
        layer_out[None],
        grad_hidden[None],
        grad_encoder[None],
        *tables,
    )
def solution(mesh):
    in_specs = (
        P("fsdp", "ctx", None),
        P("fsdp", "ctx", None),
        P("fsdp", "ctx", None),
        P("fsdp"),
        P(),
        P(None, "fsdp", "tp"),
        P(None, "fsdp", "tp"),
        P("fsdp", "tp"),
        P("fsdp", "tp"),
        P(),
        P(),
        P(),
        P(),
        P(),
        P(),
    )
    out_specs = (
        P("fsdp", "ctx", None),
        P("fsdp", "ctx", None),
        P("fsdp", "ctx", None),
        P(None, None, None, ("fsdp", "ctx", "tp")),
        P(None, None, None, ("fsdp", "ctx", "tp")),
        P(None, None, ("fsdp", "ctx", "tp")),
        P(None, None, ("fsdp", "ctx", "tp")),
        P(None, None, ("fsdp", "ctx", "tp")),
        P(None, None, ("fsdp", "ctx", "tp")),
    )
    return jax.shard_map(
        on_device, mesh=mesh, in_specs=in_specs, out_specs=out_specs, check_vma=False
    )
```
